32 devices in a mesh: dp: 4 (over y, x), fsdp: 2 (over core), expert: 4 (over z).
Axes of the slice: x: 2, y: 2, z: 4, core: 2. Of those that a mesh axis runs over, the one named last changes fastest.
Arguments:
- tokens: bfloat16 [16, 1024, 768], P(('dp', 'expert'), 'fsdp'), may hold values from -6 to 6
- attention_norm_gain: bfloat16 [768], replicated, may hold values from 0.25 to 1.75
- expert_norm_gain: bfloat16 [768], replicated, may hold values from 0.25 to 1.75
- query_key_value_weight: bfloat16 [3, 768, 768], P(None, 'fsdp'), may hold values from -0.21875 to 0.21875
- attention_output_weight: bfloat16 [768, 768], P('fsdp'), may hold values from -1.75 to 1.75
- router_weight: bfloat16 [768, 8], replicated, may hold values from -0.21875 to 0.21875
- expert_input_weight: bfloat16 [8, 768, 3072], P('expert'), may hold values from -0.21875 to 0.21875
- expert_output_weight: bfloat16 [8, 3072, 768], P('expert'), may hold values from -0.109375 to 0.109375
- adapter_down_factors: bfloat16 [6, 8, 768, 16], replicated, may hold values from -0.21875 to 0.21875
- adapter_up_attention: bfloat16 [4, 8, 16, 768], replicated, may hold values from -1.5 to 1.5
- adapter_up_routing: bfloat16 [8, 16, 8], replicated, may hold values from -1.5 to 1.5
- adapter_up_expert: bfloat16 [8, 16, 3072], replicated, may hold values from -1.5 to 1.5
- sequence_adapter: int32 [16], P(('dp', 'expert')), may hold values from 0 to 7
- position_document: int32 [16, 1024], P(('dp', 'expert')), may hold values from 0 to 3, never falling along the last dimension, each value on 1 to 512 neighbouring positions
- routes: int32 [16, 1024, 2], P(('dp', 'expert'), 'fsdp'), may hold values from 0 to 7, all different within a row; in each aligned block of 512 rows (0 to 511, 512 to 1023, ..., all dimensions but the last counted through in order) at most 256 rows name the same one
- output_gradient: bfloat16 [16, 1024, 768], P(('dp', 'expert'), 'fsdp'), may hold values from -6 to 6
Outputs:
- output: bfloat16 [16, 1024, 768], P(('dp', 'expert'), 'fsdp')
- grad_tokens: bfloat16 [16, 1024, 768], P(('dp', 'expert'), 'fsdp')
- grad_lora_down: float32 [6, 8, 768, 16], P(None, None, ('fsdp', 'expert'))
- grad_lora_up_attn: float32 [4, 8, 16, 768], P(None, None, None, ('fsdp', 'expert'))
- grad_lora_up_router: float32 [8, 16, 8], P(None, None, ('fsdp', 'expert'))
- grad_lora_up_ffn: float32 [8, 16, 3072], P(None, None, ('fsdp', 'expert'))
The draws below stay inside these ranges and needn't reach their ends.
Inputs may be any that keep to these rules, and one draw needn't show every extreme that they name: `routes`: in each aligned block of 512 rows (the tokens of one device) no expert is named more than 256 times, a bound that some block reaches; a token's two experts differ. `position_document`: along each sequence the document number never falls; a document holds 1 to 512 positions.
All inputs are finite; a program needn't handle non-finite values.
Results may differ from the reference program's by a relative error of at most 0.015.
The reference program's roundings to bfloat16 on the way count: a program that leaves them out, or rounds other values in their place, can miss the bound.
Values may be sent and summed in bfloat16 or wider, within the bound.
No kernel may reach another device: no remote copies, remote signals or barrier semaphores. Data moves between devices by JAX's collectives and lax.ppermute only.
A program may use at most 192 MiB of HBM per device.

```python
import math
import jax
import jax.numpy as jnp
import numpy as np
from jax import lax

MODEL_WIDTH = 768
HEADS = 12
HEAD_DIM = 64
EXPERT_HIDDEN = 3072
ADAPTER_CHOICES = 8
ADAPTER_RANK = 16
SEQ_LEN = 1024
EXPERT_TOTAL = 8
TOK_DEV = 512
SEQS = 16
CAP = 256


def place_ends(values, key, low, high):
    longest = values.shape.index(max(values.shape))
    spots = []
    for shift in (0, 1):
        where = [jax.random.randint(jax.random.fold_in(key, axis), (), 0, length) for axis, length in enumerate(values.shape)]
        where[longest] = (where[longest] + shift) % values.shape[longest]
        spots.append(tuple(where))
    return values.at[spots[0]].set(low).at[spots[1]].set(high)


def block_levels(key, dims, pieces, smallest, largest):
    gain, own = 1.0, jax.random.fold_in(key, 6)
    for axis_at, blocks in pieces:
        heights = jnp.exp(jax.random.uniform(jax.random.fold_in(own, axis_at), (blocks,), jnp.float32, smallest / len(pieces), largest / len(pieces)))
        gain = gain * jnp.repeat(heights, dims[axis_at] // blocks).reshape([-1 if axis == axis_at else 1 for axis in range(len(dims))])
    return gain


def profile(count, total, most, lean):
    portions = [(1 << 20) // math.isqrt(standing ** lean) + 1 for standing in range(2, count + 1)]
    spare, given = total - most - (count - 1), [1] * (count - 1)
    while spare > 0:
        movable = [i for i in range(count - 1) if given[i] < most]
        mass, remaining = sum([portions[i] for i in movable]), spare
        for i in movable:
            more = min(most - given[i], max(1, remaining * portions[i] // mass), spare)
            given[i] = given[i] + more
            spare = spare - more
    return np.array([most] + given)


def uneven(stream_key, amount, total, bound, lean):
    if amount == 2:
        one = jax.random.randint(stream_key, (), max(1, total - bound), min(bound, total - 1) + 1)
        return jnp.stack([one, total - one])
    lengths = jnp.asarray(profile(amount, total, bound, lean), jnp.int32)
    couples = (amount - 1) // 2
    giver, sink = lengths[1:1 + 2 * couples:2], lengths[2:2 + 2 * couples:2]
    slack = jnp.minimum(giver - 1, bound - sink)
    shifted = jax.random.randint(jax.random.fold_in(stream_key, 1), (couples,), 0, 1 << 20) % (slack + 1)
    lengths = lengths.at[1:1 + 2 * couples:2].set(giver - shifted).at[2:2 + 2 * couples:2].set(sink + shifted)
    return lengths[jax.random.permutation(jax.random.fold_in(stream_key, 2), amount)]


def shared_out(key, own, number, rows, number_of, top, most, slope):
    sequence = jax.random.permutation(key, number_of)
    heavy_load, common = portions_of(number_of, rows * top, most, slope, True), portions_of(number_of, rows * top, most, slope, False)
    places = jnp.arange(number_of)

    def named(tallies, offset_by):
        used = int((tallies > 0).sum())
        fixed = max(1, used // 4)
        shifted = fixed + (places - fixed + offset_by * (used - fixed)) % max(1, number_of - fixed)
        return jnp.zeros((number_of,), jnp.int32).at[sequence[jnp.where(places < fixed, places, shifted)]].set(jnp.asarray(tallies, jnp.int32))

    tallies = jnp.where(number % 4 == 0, named(heavy_load, number // 4), named(common, number - number // 4 - 1))
    mixed = jax.random.permutation(jax.random.fold_in(own, 3), number_of)
    source_of, receiver = mixed[0:number_of // 2 * 2:2], mixed[1:number_of // 2 * 2:2]
    margin = jnp.minimum(tallies[source_of] - 1, most - tallies[receiver]) // 2
    margin = jnp.where((source_of == sequence[0]) | (receiver == sequence[0]) | (tallies[receiver] == 0), 0, jnp.maximum(margin, 0))
    shifted = jax.random.randint(jax.random.fold_in(own, 4), (number_of // 2,), 0, 1 << 20) % (margin + 1)
    tallies = tallies.at[source_of].add(-shifted).at[receiver].add(shifted)
    items = jnp.searchsorted(jnp.cumsum(tallies), jnp.arange(rows * top), side="right").astype(jnp.int32)
    listing = items.reshape(top, rows).T
    listing = listing[jax.random.permutation(jax.random.fold_in(own, 1), rows)]
    offset_by = jax.random.randint(jax.random.fold_in(own, 2), (rows, 1), 0, top)
    return jnp.take_along_axis(listing, (jnp.arange(top)[None, :] + offset_by) % top, axis=1)


def portions_of(number_of, total, most, slope, full):
    loads = [(1 << 20) // math.isqrt(standing ** slope) + 1 for standing in range(1, number_of + 1)]
    largest = most if full else min(most, max(-(-total // number_of), total * loads[0] // sum(loads)))
    least = 1 if total - largest >= number_of - 1 else 0
    holding, surplus = [largest] + [least] * (number_of - 1), total - largest - least * (number_of - 1)
    while surplus > 0:
        movable = [i for i in range(1, number_of) if holding[i] < largest] or [i for i in range(1, number_of) if holding[i] < most]
        pool, budget = sum([loads[i] for i in movable]), surplus
        for i in movable:
            extra = min(most - holding[i], max(1, budget * loads[i] // pool), surplus)
            holding[i] = holding[i] + extra
            surplus = surplus - extra
    return np.array(holding)


def noise(key, dims, spread, reach, split=(), held_as=jnp.bfloat16):
    values = jax.random.normal(key, dims, jnp.float32) * spread
    if len(split) > 0:
        values = block_levels(key, dims, split, -0.22, 0.18) * values
    return jnp.clip(values, min=-reach, max=reach).astype(held_as)


def setup_inputs(seed: int = 0) -> dict:
    seeds = jax.random.split(jax.random.key(seed), 17)
    tokens = noise(seeds[0], (SEQS, SEQ_LEN, MODEL_WIDTH), 1.0, 6.0, ((0, 16), (1, 2)))
    attention_norm_gain = jnp.clip(1.0 + 0.15 * jax.random.normal(seeds[1], (MODEL_WIDTH,), jnp.float32), 0.25, 1.75).astype(jnp.bfloat16)
    expert_norm_gain = jnp.clip(1.0 + 0.15 * jax.random.normal(seeds[2], (MODEL_WIDTH,), jnp.float32), 0.25, 1.75).astype(jnp.bfloat16)
    query_key_value_weight = noise(seeds[3], (3, MODEL_WIDTH, MODEL_WIDTH), MODEL_WIDTH ** -0.5, 0.21875, ((1, 2),))
    attention_output_weight = noise(seeds[4], (MODEL_WIDTH, MODEL_WIDTH), (MODEL_WIDTH // 64) ** -0.5, 1.75, ((0, 2),))
    router_weight = noise(seeds[5], (MODEL_WIDTH, EXPERT_TOTAL), MODEL_WIDTH ** -0.5, 0.21875)
    expert_input_weight = noise(seeds[6], (EXPERT_TOTAL, MODEL_WIDTH, EXPERT_HIDDEN), MODEL_WIDTH ** -0.5, 0.21875, ((0, 4),))
    expert_output_weight = noise(seeds[7], (EXPERT_TOTAL, EXPERT_HIDDEN, MODEL_WIDTH), EXPERT_HIDDEN ** -0.5, 0.109375, ((0, 4),))
    adapter_down_factors = noise(seeds[8], (6, ADAPTER_CHOICES, MODEL_WIDTH, ADAPTER_RANK), MODEL_WIDTH ** -0.5, 0.21875)
    adapter_up_attention = noise(seeds[9], (4, ADAPTER_CHOICES, ADAPTER_RANK, MODEL_WIDTH), ADAPTER_RANK ** -0.5, 1.5)
    adapter_up_routing = noise(seeds[10], (ADAPTER_CHOICES, ADAPTER_RANK, EXPERT_TOTAL), ADAPTER_RANK ** -0.5, 1.5)
    adapter_up_expert = noise(seeds[11], (ADAPTER_CHOICES, ADAPTER_RANK, EXPERT_HIDDEN), ADAPTER_RANK ** -0.5, 1.5)
    sequence_adapter = place_ends(jax.random.randint(seeds[12], (SEQS,), 0, ADAPTER_CHOICES), jax.random.fold_in(seeds[12], 1), 0, ADAPTER_CHOICES - 1).astype(jnp.int32)
    position_document = jax.vmap(lambda own: jnp.searchsorted(jnp.cumsum(uneven(own, 4, SEQ_LEN, SEQ_LEN // 2, 0)), jnp.arange(SEQ_LEN), side="right"))(jax.random.split(seeds[13], SEQS)).reshape((SEQS, SEQ_LEN)).astype(jnp.int32)
    routes_keys = jax.random.split(jax.random.fold_in(seeds[14], 1), SEQS * SEQ_LEN // TOK_DEV)
    routes_turns = jax.random.permutation(jax.random.fold_in(seeds[14], 3), SEQS * SEQ_LEN // TOK_DEV)
    routes = jax.vmap(lambda own, number: shared_out(jax.random.fold_in(seeds[14], 2), own, number, TOK_DEV, EXPERT_TOTAL, 2, CAP, 2))(routes_keys, routes_turns).reshape((SEQS, SEQ_LEN, 2))
    output_gradient = noise(seeds[15], (SEQS, SEQ_LEN, MODEL_WIDTH), 1.0, 6.0, ((0, 16), (1, 2)))
    return dict(tokens=tokens, attention_norm_gain=attention_norm_gain, expert_norm_gain=expert_norm_gain, query_key_value_weight=query_key_value_weight, attention_output_weight=attention_output_weight, router_weight=router_weight, expert_input_weight=expert_input_weight, expert_output_weight=expert_output_weight, adapter_down_factors=adapter_down_factors, adapter_up_attention=adapter_up_attention, adapter_up_routing=adapter_up_routing, adapter_up_expert=adapter_up_expert, sequence_adapter=sequence_adapter, position_document=position_document, routes=routes, output_gradient=output_gradient)


@jax.custom_vjp
def low(v):
    return lax.optimization_barrier(v.astype(jnp.bfloat16)).astype(jnp.float32)

@jax.custom_vjp
def low_back(v):
    return v

def low_keep(v):
    return (low(v), None)

def low_pass(kept, grad):
    return (grad,)

def back_keep(v):
    return (v, None)

def back_low(kept, grad):
    return (low(grad),)
low.defvjp(low_keep, low_pass)
low_back.defvjp(back_keep, back_low)
EPSILON = 1e-06
MASKED = -1e+30
HIGH = lax.Precision.HIGHEST

def rms_norm(values, gain_vec):
    return values * lax.rsqrt(lax.optimization_barrier(jnp.mean(values * values, axis=-1, keepdims=True)) + EPSILON) * gain_vec

def reference(tokens, attention_norm_gain, expert_norm_gain, query_key_value_weight, attention_output_weight, router_weight, expert_input_weight, expert_output_weight, adapter_down_factors, adapter_up_attention, adapter_up_routing, adapter_up_expert, sequence_adapter, position_document, routes, output_gradient):
    gain_one = attention_norm_gain.astype(jnp.float32)
    gain_two = expert_norm_gain.astype(jnp.float32)
    weight_qkv = query_key_value_weight.astype(jnp.float32)
    weight_out = attention_output_weight.astype(jnp.float32)
    weight_router = router_weight.astype(jnp.float32)
    weight_in = expert_input_weight.astype(jnp.float32)
    weight_back = expert_output_weight.astype(jnp.float32)
    score_scale = 1.0 / math.sqrt(HEAD_DIM)
    positions = jnp.arange(SEQ_LEN, dtype=jnp.int32)
    token_count = SEQS * SEQ_LEN
    block_count = token_count // TOK_DEV
    flat_routes = routes.reshape(block_count, 2 * TOK_DEV)
    route_hot = (flat_routes[:, :, None] == jnp.arange(EXPERT_TOTAL, dtype=jnp.int32)[None, None, :]).astype(jnp.int32)
    route_rank = lax.optimization_barrier(jnp.sum((jnp.cumsum(route_hot, axis=1) - route_hot) * route_hot, axis=2))
    slot_index = (flat_routes * (block_count * CAP) + jnp.arange(block_count, dtype=jnp.int32)[:, None] * CAP + route_rank).reshape(-1)
    assign_count = 2 * token_count
    slot_owner = jnp.full((EXPERT_TOTAL * block_count * CAP,), assign_count, jnp.int32).at[slot_index].set(jnp.arange(assign_count, dtype=jnp.int32))
    owner_token = slot_owner // 2
    choose_hot = (routes.reshape(token_count, 2)[:, :, None] == jnp.arange(EXPERT_TOTAL, dtype=jnp.int32)[None, None, :]).astype(jnp.float32)
    adapter_tok = jnp.repeat(sequence_adapter, SEQ_LEN, total_repeat_length=token_count)
    adapter_hot = (adapter_tok[:, None] == jnp.arange(ADAPTER_CHOICES, dtype=jnp.int32)[None, :]).astype(jnp.float32)

    def forward(inputs, downs_all, ups_attn, ups_router, ups_ffn):

        def one_sequence(seq_item):
            x_seq, adapter_choice, doc_row = seq_item
            down_factor_list = downs_all[:, adapter_choice]
            up_factor_list = ups_attn[:, adapter_choice]
            normed = low(rms_norm(x_seq, gain_one))
            low_qkv = low(jnp.einsum('td,pdr->ptr', normed, down_factor_list[:3], precision=HIGH))
            qkv = jnp.einsum('td,pde->pte', normed, weight_qkv, precision=HIGH) + jnp.einsum('ptr,pre->pte', low_qkv, up_factor_list[:3], precision=HIGH)
            qkv = low_back(low(qkv)).reshape(3, SEQ_LEN, HEADS, HEAD_DIM)
            scores = jnp.einsum('qhd,khd->hqk', qkv[0], qkv[1], precision=HIGH) * score_scale
            allowed = (positions[None, :] <= positions[:, None]) & (doc_row[None, :] == doc_row[:, None])
            scores = low_back(jnp.where(allowed[None], scores, MASKED))
            probability = jax.nn.softmax(scores, axis=-1)
            mixture = jnp.einsum('hqk,khd->qhd', low(probability), qkv[2], precision=HIGH).reshape(SEQ_LEN, MODEL_WIDTH)
            mixture = low_back(low(mixture))
            low_out = low(jnp.dot(mixture, down_factor_list[3], precision=HIGH))
            branch = low_back(jnp.dot(mixture, weight_out, precision=HIGH) + jnp.dot(low_out, up_factor_list[3], precision=HIGH))
            hidden_res = x_seq + branch
            normed_two = low(rms_norm(hidden_res, gain_two))
            low_router = low(jnp.dot(normed_two, down_factor_list[4], precision=HIGH))
            logits = jnp.dot(normed_two, weight_router, precision=HIGH) + jnp.dot(low_router, ups_router[adapter_choice], precision=HIGH)
            low_ffn = low(jnp.dot(normed_two, down_factor_list[5], precision=HIGH))
            return (hidden_res, normed_two, logits, low_ffn)
        hidden_res, normed_two, logits, low_ffn = lax.map(jax.checkpoint(one_sequence), (inputs, sequence_adapter, position_document))
        hidden_res = hidden_res.reshape(token_count, MODEL_WIDTH)
        normed_two = normed_two.reshape(token_count, MODEL_WIDTH)
        logits = logits.reshape(token_count, EXPERT_TOTAL)
        low_ffn = low_ffn.reshape(token_count, ADAPTER_RANK)
        picked = lax.optimization_barrier(jnp.sum(logits[:, None, :] * choose_hot, axis=-1))
        gate_probs = jax.nn.softmax(picked, axis=-1)
        adapter_rows = (adapter_hot[:, :, None] * low_ffn[:, None, :]).reshape(token_count, ADAPTER_CHOICES * ADAPTER_RANK)
        pad_tokens = jnp.concatenate([normed_two, jnp.zeros((1, MODEL_WIDTH), jnp.float32)], axis=0)
        pad_adapt = jnp.concatenate([adapter_rows, jnp.zeros((1, ADAPTER_CHOICES * ADAPTER_RANK), jnp.float32)], axis=0)
        token_buf = low_back(pad_tokens[owner_token]).reshape(EXPERT_TOTAL, block_count * CAP, MODEL_WIDTH)
        adapt_buf = low_back(pad_adapt[owner_token]).reshape(EXPERT_TOTAL, block_count * CAP, ADAPTER_CHOICES * ADAPTER_RANK)
        flattened_up_factors = ups_ffn.reshape(ADAPTER_CHOICES * ADAPTER_RANK, EXPERT_HIDDEN)

        def one_expert(exp_item):
            token_part, adapt_part, first_w, second_w = exp_item
            preact = low_back(jnp.dot(token_part, first_w, precision=HIGH) + jnp.dot(adapt_part, flattened_up_factors, precision=HIGH))
            activation = low(jax.nn.gelu(preact))
            return low(jnp.dot(activation, second_w, precision=HIGH))
        result_buf = lax.map(jax.checkpoint(one_expert), (token_buf, adapt_buf, weight_in, weight_back))
        expert_rows = low_back(result_buf.reshape(-1, MODEL_WIDTH)[slot_index]).reshape(token_count, 2, MODEL_WIDTH)
        expert_sum = lax.optimization_barrier(jnp.sum(gate_probs[:, :, None] * expert_rows, axis=1))
        return (hidden_res + expert_sum).reshape(SEQS, SEQ_LEN, MODEL_WIDTH)
    forward_value = (tokens.astype(jnp.float32), adapter_down_factors.astype(jnp.float32), adapter_up_attention.astype(jnp.float32), adapter_up_routing.astype(jnp.float32), adapter_up_expert.astype(jnp.float32))
    result, pullback = jax.vjp(forward, *forward_value)
    grads = pullback(output_gradient.astype(jnp.float32))
    return (result.astype(jnp.bfloat16), grads[0].astype(jnp.bfloat16), grads[1], grads[2], grads[3], grads[4])
```

```python
import functools
import math

import jax
import jax.numpy as jnp
from jax import lax
from jax.experimental import pallas as pl
from jax.experimental.pallas import tpu as pltpu
from jax.sharding import PartitionSpec as P

HEADS = 12
HEAD_DIM = 64


EPSILON = 1e-06
MASKED = -1e30


def shifted(block, axis, distance):
    devices = range(lax.axis_size(axis))
    route = [(i - distance, i) for i in devices if i - distance in devices]
    return lax.ppermute(block, axis, route)


def rms_norm(values, gain_vec):
    return (
        values * lax.rsqrt(jnp.mean(values * values, axis=-1, keepdims=True) + EPSILON) * gain_vec
    )


def mxu(left, right, left_dim=1, right_dim=0):
    return lax.dot_general(
        left, right, (((left_dim,), (right_dim,)), ((), ())), preferred_element_type=jnp.float32
    )


def window_bias(bias, kdoc_ref, qdoc_ref, block):
    keys, cols = bias.shape[1:]
    kpos = lax.broadcasted_iota(jnp.int32, (keys, cols), 0) - (keys - cols)
    qpos = lax.broadcasted_iota(jnp.int32, (keys, cols), 1)
    key_doc = kdoc_ref[pl.ds(pl.multiple_of(block * cols, cols), keys), :]
    bias[block] = jnp.where((kpos <= qpos) & (key_doc == qdoc_ref[...]), 0.0, MASKED)


def head_probability(queries, key_parts, bias, block, first):
    tall = queries.shape[0]
    scores = [
        mxu(part, queries, 1, 1) + bias[block, (first + i) * tall : (first + i + 1) * tall, :]
        for i, part in enumerate(key_parts)
    ]
    top = functools.reduce(jnp.maximum, [jnp.max(s, axis=0, keepdims=True) for s in scores])
    parts = [jnp.exp(s - top) for s in scores]
    total = sum(jnp.sum(p, axis=0, keepdims=True) for p in parts)
    share = 1.0 / total
    return [p * share for p in parts]


def windows(refs, block):
    far_ref, left_ref, own_ref, near_ref = refs
    return [far_ref[0], jnp.where(block == 0, left_ref[0], own_ref[0]), near_ref[0]]


def attend_kernel(reach, kdoc_ref, qdoc_ref, q_ref, *refs):
    key_refs, value_refs = refs[:4], refs[4:8]
    out_ref, bias = refs[8:]
    block = pl.program_id(1)

    @pl.when(pl.program_id(0) == 0)
    def _():
        window_bias(bias, kdoc_ref, qdoc_ref, block)

    def run(first):
        keys, values = (windows(part, block)[first:] for part in (key_refs, value_refs))
        mixed = []
        for head in range(q_ref.shape[2] // HEAD_DIM):
            cols = slice(head * HEAD_DIM, (head + 1) * HEAD_DIM)
            queries = q_ref[0, :, cols] * (1.0 / math.sqrt(HEAD_DIM))
            probability = head_probability(
                queries, [key[:, cols] for key in keys], bias, block, first
            )
            mixed.append(
                sum(
                    mxu(value[:, cols], p.astype(jnp.bfloat16), 0, 0)
                    for value, p in zip(values, probability)
                )
            )
        out_ref[...] = jnp.concatenate(mixed, axis=0).T.astype(out_ref.dtype)

    for first in range(3):
        pl.when(reach[block] == first)(functools.partial(run, first))


def attend_back_kernel(reach, kdoc_ref, qdoc_ref, q_ref, *refs):
    key_refs, value_refs = refs[:4], refs[4:8]
    grad_ref, dq_ref, dk_ref, dv_ref, dkl_ref, dvl_ref, bias, acc = refs[8:]
    block = pl.program_id(1)
    scale = 1.0 / math.sqrt(HEAD_DIM)

    @pl.when(pl.program_id(0) == 0)
    def _():
        window_bias(bias, kdoc_ref, qdoc_ref, block)

    @pl.when(block == 0)
    def _():
        acc[...] = jnp.zeros_like(acc)

    def run(first):
        keys, values = (windows(part, block)[first:] for part in (key_refs, value_refs))
        grad_queries = []
        for head in range(q_ref.shape[2] // HEAD_DIM):
            cols = slice(head * HEAD_DIM, (head + 1) * HEAD_DIM)
            queries = q_ref[0, :, cols] * scale
            grad = grad_ref[:, cols]
            probability = head_probability(
                queries, [key[:, cols] for key in keys], bias, block, first
            )
            grad_prob = [mxu(value[:, cols], grad, 1, 1) for value in values]
            inner = sum(
                jnp.sum(p * g, axis=0, keepdims=True) for p, g in zip(probability, grad_prob)
            )
            grad_score = [
                (p * (g - inner)).astype(jnp.bfloat16) for p, g in zip(probability, grad_prob)
            ]
            grad_queries.append(
                sum(mxu(key[:, cols], g, 0, 0) for key, g in zip(keys, grad_score)) * scale
            )
            for i, (p, g) in enumerate(zip(probability, grad_score)):
                acc[0, block + first + i, :, cols] += mxu(g, queries)
                acc[1, block + first + i, :, cols] += mxu(p.astype(jnp.bfloat16), grad)
        dq_ref[...] = jnp.concatenate(grad_queries, axis=0).T.astype(dq_ref.dtype)

    for first in range(3):
        pl.when(reach[block] == first)(functools.partial(run, first))

    @pl.when(block == pl.num_programs(1) - 1)
    def _():
        tall = q_ref.shape[1]
        for i in range(2):
            rows = slice(i * tall, (i + 1) * tall)
            dkl_ref[rows, :] = acc[0, i].astype(dkl_ref.dtype)
            dvl_ref[rows, :] = acc[1, i].astype(dvl_ref.dtype)
            dk_ref[rows, :] = acc[0, 2 + i].astype(dk_ref.dtype)
            dv_ref[rows, :] = acc[1, 2 + i].astype(dv_ref.dtype)


def attention_call(kernel, qkv, left_kv, grads, key_doc, query_doc, outs, scratch, flops):
    rows, width = qkv.shape[1:]
    lanes = 2 * HEAD_DIM
    tall = rows // 2
    starts = jnp.arange(2, dtype=jnp.int32) * tall
    reach = sum(
        (key_doc[starts + (i + 1) * tall - 1] != query_doc[starts]).astype(jnp.int32)
        for i in range(2)
    )

    def part(p, at):
        return pl.BlockSpec((1, tall, lanes), lambda g, b, s: (p, at(b), g))

    spots = [lambda b: b, lambda b: 1, lambda b: 0, lambda b: b]
    sides = [left_kv, left_kv, qkv, qkv]
    sources = [
        part(p + (0 if side is left_kv else 1), at)
        for p in range(2)
        for side, at in zip(sides, spots)
    ]

    def stack(kind):
        return {
            "block": pl.BlockSpec((tall, lanes), lambda g, b, s: (b, g)),
            "cols": pl.BlockSpec((rows, lanes), lambda g, b, s: (0, g)),
        }[kind]

    return pl.pallas_call(
        kernel,
        grid_spec=pltpu.PrefetchScalarGridSpec(
            num_scalar_prefetch=1,
            grid=(width // lanes, 2),
            in_specs=[
                pl.BlockSpec((2 * rows, 1), lambda g, b, s: (0, 0)),
                pl.BlockSpec((1, tall), lambda g, b, s: (0, b)),
                pl.BlockSpec((1, tall, lanes), lambda g, b, s: (0, b, g)),
                *sources,
            ]
            + [stack("block")] * len(grads),
            out_specs=[stack(kind) for kind, _ in outs],
            scratch_shapes=[pltpu.VMEM((2, 3 * tall, tall), jnp.float32)]
            + [pltpu.VMEM((2, 4, tall, lanes), jnp.float32)] * scratch,
        ),
        out_shape=[jax.ShapeDtypeStruct((rows, width), dtype) for _, dtype in outs],
        compiler_params=pltpu.CompilerParams(vmem_limit_bytes=56000 * 1024),
        cost_estimate=pl.CostEstimate(
            flops=flops * rows * rows * width,
            bytes_accessed=12 * rows * width,
            transcendentals=HEADS * rows * rows,
        ),
        name="attend_back" if scratch else "attend",
    )(reach, key_doc.reshape(-1, 1), query_doc.reshape(1, -1), qkv, *sides, *sides, *grads)


def expert_preact(token_part, adapt_part, expert_input_weight, flattened_up_factors):
    return jnp.einsum(
        "sxnd,xdf->sxnf", token_part, expert_input_weight, preferred_element_type=jnp.float32
    ) + jnp.einsum(
        "sxnr,rf->sxnf", adapt_part, flattened_up_factors, preferred_element_type=jnp.float32
    )


def gelu_both(u):
    c = math.sqrt(2.0 / math.pi)
    sq = u * u
    t = jnp.tanh(u * (c + (c * 0.044715) * sq))
    half = 0.5 + 0.5 * t
    slope = half + (0.5 * u) * (1.0 - t * t) * (c + (3.0 * c * 0.044715) * sq)
    return u * half, slope


def expert_kernel(shard_count, capacity, expert_count, rank, *refs):
    scalars, first_ref = refs[:2]
    refs = refs[2:]
    x_refs, g_refs, route_refs, down_refs, upr_refs, uf_refs = (
        refs[i * shard_count : (i + 1) * shard_count] for i in range(6)
    )
    router_ref, w1_ref, w2_ref = refs[6 * shard_count : 6 * shard_count + 3]
    refs = refs[6 * shard_count + 3 :]
    y_refs, dx_refs, gff_refs = (refs[i * shard_count : (i + 1) * shard_count] for i in range(3))
    (
        xe,
        dye,
        lfe,
        yacc,
        dxacc,
        dleacc,
        onehot_s,
        lft_s,
        gate_s,
        rank_s,
        ysum,
        dxsum,
        ext_s,
    ) = refs[3 * shard_count :]
    e = pl.program_id(0)
    t = pl.program_id(1)
    last_t = pl.num_programs(1) - 1
    last_e = pl.num_programs(0) - 1
    rows = x_refs[0].shape[0]
    tile = w1_ref.shape[2]
    ident = first_ref[0] + e
    for s in range(shard_count):
        count = scalars[2 * shard_count + s * pl.num_programs(0) + e]

        @pl.when((e == 0) & (t == 0))
        def _():
            ysum[s] = jnp.zeros_like(ysum[s])
            dxsum[s] = jnp.zeros_like(dxsum[s])
            ext_s[s] = jnp.zeros_like(ext_s[s])
            gff_refs[s][...] = jnp.zeros_like(gff_refs[s])
            x = x_refs[s][...]
            low = mxu(down_refs[s][0], x, 1, 1)
            lr = low[:rank].astype(jnp.bfloat16)
            lft_s[s] = low[rank:].astype(jnp.bfloat16)
            logits = mxu(router_ref[...], x, 1, 1) + mxu(upr_refs[s][0], lr)
            ids = lax.broadcasted_iota(jnp.int32, (expert_count, rows), 0)
            r = route_refs[s][0]
            hot = (ids == r[0:1]) | (ids == r[1:2])
            top = jnp.max(jnp.where(hot, logits, -jnp.inf), axis=0, keepdims=True)
            ex = jnp.where(hot, jnp.exp(logits - top), 0.0)
            gate_s[s] = ex / jnp.sum(ex, axis=0, keepdims=True)
            before = lax.broadcasted_iota(jnp.int32, (rows, rows), 0) < lax.broadcasted_iota(
                jnp.int32, (rows, rows), 1
            )
            ranks = mxu(
                hot.astype(jnp.float32).astype(jnp.bfloat16),
                before.astype(jnp.float32).astype(jnp.bfloat16),
            )
            rank_s[s] = jnp.where(hot, ranks, -1.0)

        def slots():
            row = rank_s[s, pl.ds(ident, 1), :]
            picks = lax.broadcasted_iota(jnp.int32, (capacity, rows), 0).astype(jnp.float32) == row
            gate = gate_s[s, pl.ds(ident, 1), :]
            return picks, jnp.sum(jnp.where(picks, gate, 0.0), axis=1, keepdims=True)

        @pl.when((count > 0) & (t == 0))
        def _():
            picks, gate_slot = slots()
            onehot = picks.astype(jnp.float32).astype(jnp.bfloat16)
            onehot_s[s] = onehot
            xe[s] = mxu(onehot, x_refs[s][...]).astype(jnp.bfloat16)
            dye[s] = (mxu(onehot, g_refs[s][...]) * gate_slot).astype(jnp.bfloat16)
            lfe[s] = mxu(onehot, lft_s[s], 1, 1).astype(jnp.bfloat16)
            yacc[s] = jnp.zeros_like(yacc[s])
            dxacc[s] = jnp.zeros_like(dxacc[s])
            dleacc[s] = jnp.zeros_like(dleacc[s])

        @pl.when(count > 0)
        def _():
            off = pl.multiple_of(t * tile, tile)
            pre = mxu(xe[s], w1_ref[0]) + mxu(lfe[s], uf_refs[s][0])
            act, slope = gelu_both(pre)
            yacc[s] += mxu(act.astype(jnp.bfloat16), w2_ref[0])
            dpre = (mxu(dye[s], w2_ref[0], 1, 1) * slope).astype(jnp.bfloat16)
            dxacc[s] += mxu(dpre, w1_ref[0], 1, 1)
            dleacc[s] += mxu(uf_refs[s][0], dpre, 1, 1)
            gff_refs[s][:, pl.ds(off, tile)] += mxu(lfe[s], dpre, 0, 0)

        @pl.when((count > 0) & (t == last_t))
        def _():
            picks, gate_slot = slots()
            onehot = onehot_s[s]
            y = yacc[s].astype(jnp.bfloat16).astype(jnp.float32)
            dgate = jnp.sum(mxu(onehot, g_refs[s][...]) * y, axis=1, keepdims=True)
            dgate_row = jnp.sum(jnp.where(picks, dgate, 0.0), axis=0, keepdims=True)
            for k in range(2):
                mine = route_refs[s][0, k : k + 1] == ident
                ext_s[s, rank + k : rank + k + 1, :] += jnp.where(mine, dgate_row, 0.0)
            ext_s[s, 0:rank, :] += mxu(dleacc[s].astype(jnp.bfloat16), onehot)
            ysum[s] += mxu(onehot, (y * gate_slot).astype(jnp.bfloat16), 0, 0)
            dxsum[s] += mxu(onehot, dxacc[s].astype(jnp.bfloat16), 0, 0)

        @pl.when((e == last_e) & (t == last_t))
        def _():
            y_refs[s][...] = ysum[s].astype(jnp.bfloat16)
            dx_refs[s][:rows, :] = dxsum[s].astype(jnp.bfloat16)
            extra = ext_s[s]
            gates = extra[rank:]
            low = gates - gates.astype(jnp.bfloat16).astype(jnp.float32)
            packed = jnp.concatenate([extra, low], axis=0).astype(jnp.bfloat16)
            width = dxsum.shape[2]
            if width > rows:
                blank = jnp.zeros((packed.shape[0], width - rows), jnp.bfloat16)
                packed = jnp.concatenate([packed, blank], axis=1)
            dx_refs[s][rows:, :] = packed


def run_experts(
    scalars, first, xs, gs, route_rows, down_t, router_t, upr_t, up_ffn, w1, w2, capacity
):
    count = len(xs)
    rows, width = xs[0].shape
    local, _, hidden = w1.shape
    expert_count = router_t.shape[0]
    rank = up_ffn.shape[1]
    tile = 1024 if hidden % 1024 == 0 else hidden
    fixed = lambda *shape, **kw: pl.BlockSpec(shape, lambda e, t, sc, fi: (0,) * len(shape), **kw)

    def adapter(s, *shape):
        return pl.BlockSpec((1, *shape), lambda e, t, sc, fi, s=s: (sc[s], 0, 0))

    shards_of = range(count)
    in_specs = (
        [fixed(rows, width, pipeline_mode=pl.Buffered(1)) for _ in shards_of] * 2
        + [
            pl.BlockSpec((1, 2, rows), lambda e, t, sc, fi, s=s: (sc[count + s], 0, 0))
            for s in shards_of
        ]
        + [adapter(s, 2 * rank, width) for s in shards_of]
        + [adapter(s, expert_count, rank) for s in shards_of]
        + [
            pl.BlockSpec((1, rank, tile), lambda e, t, sc, fi, s=s: (sc[s], 0, t))
            for s in shards_of
        ]
        + [
            fixed(expert_count, width),
            pl.BlockSpec((1, width, tile), lambda e, t, sc, fi: (e, 0, t)),
            pl.BlockSpec((1, tile, width), lambda e, t, sc, fi: (e, t, 0)),
        ]
    )
    bf16, f32 = jnp.bfloat16, jnp.float32
    outs = (
        [((rows, width), bf16)] * count
        + [((rows + rank + 16, width), bf16)] * count
        + [((rank, hidden), f32)] * count
    )
    scratch = [
        ((capacity, width), bf16),
        ((capacity, width), bf16),
        ((capacity, rank), bf16),
        ((capacity, width), f32),
        ((capacity, width), f32),
        ((rank, capacity), f32),
        ((capacity, rows), bf16),
        ((rank, rows), bf16),
        ((expert_count, rows), f32),
        ((expert_count, rows), f32),
        ((rows, width), f32),
        ((rows, width), f32),
        ((rank + 8, rows), f32),
    ]
    result = pl.pallas_call(
        functools.partial(expert_kernel, count, capacity, expert_count, rank),
        grid_spec=pltpu.PrefetchScalarGridSpec(
            num_scalar_prefetch=2,
            grid=(local, hidden // tile),
            in_specs=in_specs,
            out_specs=[fixed(*shape) for shape, _ in outs],
            scratch_shapes=[pltpu.VMEM((count, *shape), kind) for shape, kind in scratch],
        ),
        out_shape=[jax.ShapeDtypeStruct(shape, kind) for shape, kind in outs],
        compiler_params=pltpu.CompilerParams(vmem_limit_bytes=58 * 1024 * 1024),
        cost_estimate=pl.CostEstimate(
            flops=8 * count * local * capacity * width * hidden,
            bytes_accessed=4 * local * width * hidden + 8 * count * rows * width,
            transcendentals=0,
        ),
        name="experts",
    )(
        scalars,
        first,
        *xs,
        *gs,
        *([route_rows] * count),
        *([down_t] * count),
        *([upr_t] * count),
        *([up_ffn] * count),
        router_t,
        w1,
        w2,
    )
    return tuple(result[i * count : (i + 1) * count] for i in range(3))


CROSS = [(0, 1), (1, 0), (2, 3), (3, 2)]
INNER = [(1, 2), (2, 1)]
OUTWARD = [(1, 0), (2, 3)]
TWICE = [(0, 2), (2, 0), (1, 3), (3, 1)]
ENDS = [(0, 3), (3, 0)]
MIRROR = [(0, 3), (3, 0), (1, 2), (2, 1)]


def on_line(block, route):
    return lax.ppermute(block, "expert", route)


def send_line(block):
    return tuple(on_line(block, route) for route in (CROSS, INNER, TWICE, ENDS))


def return_line(parts, routes):
    return [on_line(part, route) for part, route in zip(parts, routes)]


def moe_by_tokens(
    normed_two,
    grad_sides,
    meta,
    adapter_down_factors,
    router_weight,
    adapter_up_routing,
    adapter_up_expert,
    expert_input_weight,
    expert_output_weight,
    capacity,
):
    groups = lax.axis_size("expert")
    place = lax.axis_index("expert")
    local = expert_input_weight.shape[0]
    adapter_total, rank, _ = adapter_up_expert.shape
    down_t = jnp.transpose(adapter_down_factors[4:6], (1, 0, 3, 2)).reshape(
        adapter_total, 2 * rank, -1
    )
    upr_t = jnp.transpose(adapter_up_routing, (0, 2, 1))
    route_rows, adapters = meta
    first = (place * local).astype(jnp.int32)
    ids = first + jnp.arange(local, dtype=jnp.int32)
    counts = jnp.sum(
        (route_rows[:, None] == ids[None, :, None, None]).astype(jnp.int32), axis=(2, 3)
    )
    at_end = (place == 0) | (place == groups - 1)

    def call(spots, present, xs, gs):
        spot = jnp.array(spots, jnp.int32)
        scalars = jnp.concatenate(
            [adapters[spot], spot, (counts[spot] * jnp.stack(present)[:, None]).reshape(-1)]
        ).astype(jnp.int32)
        return run_experts(
            scalars,
            first.reshape(1),
            xs,
            gs,
            route_rows,
            down_t,
            router_weight.T,
            upr_t,
            adapter_up_expert,
            expert_input_weight,
            expert_output_weight,
            capacity,
        )

    always = jnp.int32(1)
    ends = at_end.astype(jnp.int32)
    across, inner, last = (on_line(normed_two, route) for route in (CROSS, INNER, ENDS))
    g_across, g_inner, g_far, g_last, g_own = grad_sides
    own = call([0], [always], [normed_two], [g_own])
    far_inner, far_ends = on_line(across, INNER), on_line(inner, OUTWARD)
    near = call([1, 3], [always, 1 - ends], [across, inner], [g_across, g_inner])
    far = jnp.where(at_end, far_ends, far_inner)
    near_dx = return_line(near[1], (CROSS, INNER))
    away = call([2, 3], [always, ends], [far, last], [g_far, g_last])
    away_dx = return_line(away[1], (TWICE, ENDS))
    dx = sum(part.astype(jnp.float32) for part in [own[1][0], *near_dx, *away_dx])
    outs, _ = lax.optimization_barrier(([*near[0], *away[0]], dx))
    outs = return_line(outs, (CROSS, INNER, TWICE, ENDS))
    y = [own[0][0], *outs]
    grad_up = jnp.stack([own[2][0], near[2][0], away[2][0], near[2][1] + away[2][1]])
    rows = normed_two.shape[0]
    extra = dx[rows:, :rows]
    grad_gate = extra[rank : rank + 2] + extra[rank + 8 : rank + 10]
    return y, dx[:rows], grad_gate.T, extra[:rank].T, grad_up


def moe_by_slots(
    normed_two,
    gate_probs,
    route_rows,
    low_ffn,
    grad_out,
    adapter_one,
    adapter_up_expert,
    expert_input_weight,
    expert_output_weight,
    capacity,
):
    row_count, width = normed_two.shape
    local_experts = expert_input_weight.shape[0]
    expert_groups = lax.axis_size("expert")
    expert_count = local_experts * expert_groups
    adapter_total, adapter_rank_width, expert_hidden_width = adapter_up_expert.shape
    expert_ids = jnp.arange(expert_count, dtype=jnp.int32)
    adapter_place = adapter_one.astype(jnp.bfloat16)
    adapter_rows = (adapter_place[None, :, None] * low_ffn[:, None, :]).reshape(
        row_count, adapter_total * adapter_rank_width
    )
    flat_routes = route_rows.reshape(-1)
    route_hot = (flat_routes[:, None] == expert_ids[None, :]).astype(jnp.int32)
    route_rank = jnp.sum((jnp.cumsum(route_hot, axis=0) - route_hot) * route_hot, axis=1)
    slot_index = flat_routes * capacity + route_rank
    assign_count = 2 * row_count
    slot_owner = (
        jnp.full((expert_count * capacity,), assign_count, jnp.int32)
        .at[slot_index]
        .set(jnp.arange(assign_count, dtype=jnp.int32))
    )
    owner_token = slot_owner // 2
    pad_rows = jnp.zeros((1, width), jnp.bfloat16)
    send_tokens = jnp.concatenate([normed_two, pad_rows], axis=0)[owner_token].reshape(
        expert_groups, local_experts, capacity, width
    )
    send_adapt = jnp.concatenate(
        [adapter_rows, jnp.zeros((1, adapter_total * adapter_rank_width), jnp.bfloat16)], axis=0
    )[owner_token].reshape(
        expert_groups, local_experts, capacity, adapter_total * adapter_rank_width
    )
    flattened_up_factors = adapter_up_expert.reshape(
        adapter_total * adapter_rank_width, expert_hidden_width
    )
    token_part = lax.all_to_all(send_tokens, "expert", split_axis=0, concat_axis=0, tiled=True)
    adapt_part = lax.all_to_all(send_adapt, "expert", split_axis=0, concat_axis=0, tiled=True)
    preact = expert_preact(token_part, adapt_part, expert_input_weight, flattened_up_factors)
    activation = jax.nn.gelu(preact).astype(jnp.bfloat16)
    result = jnp.einsum(
        "sxnf,xfd->sxnd", activation, expert_output_weight, preferred_element_type=jnp.float32
    ).astype(jnp.bfloat16)
    returned = lax.all_to_all(result, "expert", split_axis=0, concat_axis=0, tiled=True)
    expert_rows = (
        returned.reshape(expert_count * capacity, width)[slot_index]
        .reshape(row_count, 2, width)
        .astype(jnp.float32)
    )
    expert_sum = jnp.sum(gate_probs[:, :, None] * expert_rows, axis=1)
    grad_gate = jnp.sum(grad_out[:, None, :] * expert_rows, axis=-1)
    grad_assign = (
        (gate_probs[:, :, None] * grad_out[:, None, :])
        .astype(jnp.bfloat16)
        .reshape(assign_count, width)
    )
    send_grad = jnp.concatenate([grad_assign, pad_rows], axis=0)[slot_owner].reshape(
        expert_groups, local_experts, capacity, width
    )
    grad_recv = lax.all_to_all(send_grad, "expert", split_axis=0, concat_axis=0, tiled=True)
    grad_act = jnp.einsum(
        "sxnd,xfd->sxnf", grad_recv, expert_output_weight, preferred_element_type=jnp.float32
    )
    grad_pre = jax.vjp(jax.nn.gelu, preact)[1](grad_act)[0].astype(jnp.bfloat16)
    grad_tok_expert = jnp.einsum(
        "sxnf,xdf->sxnd", grad_pre, expert_input_weight, preferred_element_type=jnp.float32
    ).astype(jnp.bfloat16)
    grad_adapt_expert = jnp.einsum(
        "sxnf,rf->sxnr", grad_pre, flattened_up_factors, preferred_element_type=jnp.float32
    ).astype(jnp.bfloat16)
    grad_up_ffn = jnp.einsum(
        "sxnr,sxnf->rf", adapt_part, grad_pre, preferred_element_type=jnp.float32
    ).reshape(adapter_total, adapter_rank_width, expert_hidden_width)
    grad_back_tok, grad_back_adapt = (
        lax.all_to_all(grad_tok_expert, "expert", split_axis=0, concat_axis=0, tiled=True),
        lax.all_to_all(grad_adapt_expert, "expert", split_axis=0, concat_axis=0, tiled=True),
    )
    grad_normed_two = jnp.sum(
        grad_back_tok.reshape(expert_count * capacity, width)[slot_index]
        .astype(jnp.float32)
        .reshape(row_count, 2, width),
        axis=1,
    )
    adapt_back = grad_back_adapt.reshape(
        expert_count * capacity, adapter_total, adapter_rank_width
    )[slot_index].astype(jnp.float32)
    grad_low_ffn = jnp.sum(
        jnp.sum(adapt_back * adapter_one[None, :, None], axis=1).reshape(
            row_count, 2, adapter_rank_width
        ),
        axis=1,
    )
    return expert_sum, grad_normed_two, grad_gate, grad_low_ffn, grad_up_ffn


def exchange_all(block, axis):
    count = lax.axis_size(axis)
    return [block] + [
        lax.ppermute(block, axis, [(i, (i + step) % count) for i in range(count)])
        for step in range(1, count)
    ]


def spread_sums(
    grad_rows, grad_up_router, grad_up_ffn, adapter_choice, adapter_total, by_tokens
):
    half_index = lax.axis_index("fsdp")
    groups = lax.axis_size("expert")
    rank, choices = grad_up_router.shape
    width = grad_rows.shape[1]
    share = width // (2 * groups)
    wide = choices // (2 * groups)
    router = jnp.pad(
        grad_up_router.reshape(rank, 2 * groups, wide), ((0, 0), (0, 0), (0, share - wide))
    ).reshape(rank, width)
    label = jnp.full((8, width), 0.5 * adapter_choice.astype(jnp.float32))
    grad_rows = jnp.concatenate([grad_rows, router, label])
    row_total = grad_rows.shape[0]

    def over_halves(rows):
        halves = rows.reshape(rows.shape[0], 2, -1)
        kept = lax.dynamic_index_in_dim(halves, half_index, 1, keepdims=False)
        given = lax.dynamic_index_in_dim(halves, 1 - half_index, 1, keepdims=False)
        return kept + lax.ppermute(given, "fsdp", [(0, 1), (1, 0)])

    def over_experts(rows):
        parts = jnp.swapaxes(rows.reshape(rows.shape[0], groups, -1), 0, 1)
        return lax.all_to_all(parts, "expert", split_axis=0, concat_axis=0, tiled=True)

    slots = jnp.arange(adapter_total, dtype=jnp.int32)
    ffn_parts = over_experts(over_halves(grad_up_ffn.reshape(-1, grad_up_ffn.shape[-1])))
    if by_tokens:
        ffn_parts = ffn_parts.reshape(groups, groups, rank, -1)
        ffn_parts = jnp.stack(
            [sum(ffn_parts[e, e ^ spot] for e in range(groups)) for spot in range(groups)]
        )
    else:
        ffn_parts = jnp.sum(ffn_parts, axis=0)
    ffn_parts = exchange_all(ffn_parts, "dp")
    parts = exchange_all(over_experts(over_halves(grad_rows)), "dp")
    summed, ffn = 0.0, 0.0
    for part, ffn_part in zip(parts, ffn_parts):
        label = part[:, row_total - 1, 0].astype(jnp.int32)
        hot = (slots[:, None] == label[None, :]).astype(jnp.float32)
        summed = summed + jnp.sum(hot[:, :, None, None] * part[None, :, : row_total - 8], axis=1)
        if by_tokens:
            ffn = ffn + jnp.sum(hot[:, :, None, None] * ffn_part[None], axis=1)
        else:
            ffn = ffn + ffn_part
    summed = summed.reshape(adapter_total, (row_total - 8) // rank, rank, share)
    downs = jnp.transpose(summed[:, :6], (1, 0, 3, 2))
    ups = jnp.transpose(summed[:, 6:10], (1, 0, 2, 3))
    router = summed[:, 10, :, :wide]
    return downs, ups, router, ffn.reshape(adapter_total, rank, -1)


def shards(
    tokens,
    attention_norm_gain,
    expert_norm_gain,
    query_key_value_weight,
    attention_output_weight,
    router_weight,
    expert_input_weight,
    expert_output_weight,
    adapter_down_factors,
    adapter_up_attention,
    adapter_up_routing,
    adapter_up_expert,
    sequence_adapter,
    position_document,
    routes,
    output_gradient,
):
    row_count = tokens.shape[1]
    width = tokens.shape[2]
    local_experts = expert_input_weight.shape[0]
    expert_groups = lax.axis_size("expert")
    expert_count = local_experts * expert_groups
    capacity = 4 * row_count // expert_count
    adapter_total = adapter_down_factors.shape[1]
    adapter_rank_width = adapter_down_factors.shape[3]
    adapter_choice = sequence_adapter[0]
    half_index = lax.axis_index("fsdp")
    doc_row = position_document[0]
    by_tokens = expert_groups == 4 and local_experts * capacity >= row_count
    if by_tokens:
        about = jnp.concatenate([routes[0].T, jnp.full((1, row_count), adapter_choice, jnp.int32)])
        about = jnp.stack(
            [about, on_line(about, CROSS), on_line(about, TWICE), on_line(about, MIRROR)]
        )
        meta = (about[:, :2], about[:, 2, 0])
        grad_sides = (*send_line(output_gradient[0]), output_gradient[0])
    x_in = tokens[0].astype(jnp.float32)
    gain_one = attention_norm_gain.astype(jnp.float32)
    gain_two = expert_norm_gain.astype(jnp.float32)
    normed_f, norm_one_back = jax.vjp(lambda values_in: rms_norm(values_in, gain_one), x_in)
    normed = normed_f.astype(jnp.bfloat16)
    weight_qkv, weight_out = (
        lax.all_gather(query_key_value_weight, "fsdp", axis=1, tiled=True),
        lax.all_gather(attention_output_weight, "fsdp", axis=0, tiled=True),
    )
    down_factor_list = lax.dynamic_index_in_dim(
        adapter_down_factors, adapter_choice, 1, keepdims=False
    )
    up_factor_list = lax.dynamic_index_in_dim(
        adapter_up_attention, adapter_choice, 1, keepdims=False
    )
    routing_up_factor = lax.dynamic_index_in_dim(
        adapter_up_routing, adapter_choice, 0, keepdims=False
    )
    low_qkv = jnp.einsum(
        "td,pdr->ptr", normed, down_factor_list[:3], preferred_element_type=jnp.float32
    ).astype(jnp.bfloat16)
    qkv = (
        jnp.einsum("td,pde->pte", normed, weight_qkv, preferred_element_type=jnp.float32)
        + jnp.einsum(
            "ptr,pre->pte", low_qkv, up_factor_list[:3], preferred_element_type=jnp.float32
        )
    ).astype(jnp.bfloat16)
    left_kv = shifted(qkv[1:], "fsdp", 1)
    own_doc = lax.dynamic_slice_in_dim(doc_row, half_index * row_count, row_count)
    left_doc = jnp.where(half_index > 0, doc_row[:row_count], -1)
    key_doc = jnp.concatenate([left_doc, own_doc])
    (mixture,) = attention_call(
        attend_kernel, qkv, left_kv, [], key_doc, own_doc, [("block", jnp.bfloat16)], 0, 4
    )
    low_out = jnp.dot(mixture, down_factor_list[3], preferred_element_type=jnp.float32).astype(
        jnp.bfloat16
    )
    branch = jnp.dot(mixture, weight_out, preferred_element_type=jnp.float32) + jnp.dot(
        low_out, up_factor_list[3], preferred_element_type=jnp.float32
    )
    hidden_res = x_in + branch
    normed_two_f, norm_two_back = jax.vjp(
        lambda values_in: rms_norm(values_in, gain_two), hidden_res
    )
    normed_two = normed_two_f.astype(jnp.bfloat16)
    low_router = jnp.dot(
        normed_two, down_factor_list[4], preferred_element_type=jnp.float32
    ).astype(jnp.bfloat16)
    logits = jnp.dot(normed_two, router_weight, preferred_element_type=jnp.float32) + jnp.dot(
        low_router, routing_up_factor, preferred_element_type=jnp.float32
    )
    route_rows = routes[0]
    expert_ids = jnp.arange(expert_count, dtype=jnp.int32)
    choose_hot = (route_rows[:, :, None] == expert_ids[None, None, :]).astype(jnp.float32)
    picked = jnp.sum(logits[:, None, :] * choose_hot, axis=-1)
    gate_probs = jax.nn.softmax(picked, axis=-1)
    low_ffn = jnp.dot(normed_two, down_factor_list[5], preferred_element_type=jnp.float32).astype(
        jnp.bfloat16
    )
    adapter_one = (jnp.arange(adapter_total, dtype=jnp.int32) == adapter_choice).astype(jnp.float32)
    grad_out = output_gradient[0].astype(jnp.float32)
    if by_tokens:
        expert_sum, grad_normed_two, grad_gate, grad_low_ffn, grad_up_ffn = moe_by_tokens(
            normed_two,
            grad_sides,
            meta,
            adapter_down_factors,
            router_weight,
            adapter_up_routing,
            adapter_up_expert,
            expert_input_weight,
            expert_output_weight,
            capacity,
        )
    else:
        expert_sum, grad_normed_two, grad_gate, grad_low_ffn, grad_up_ffn = moe_by_slots(
            normed_two,
            gate_probs,
            route_rows,
            low_ffn,
            grad_out,
            adapter_one,
            adapter_up_expert,
            expert_input_weight,
            expert_output_weight,
            capacity,
        )
    grad_pick = gate_probs * (grad_gate - jnp.sum(gate_probs * grad_gate, axis=-1, keepdims=True))
    grad_logits = jnp.sum(grad_pick[:, :, None] * choose_hot, axis=1)
    grad_low_router = jnp.einsum(
        "te,re->tr", grad_logits, routing_up_factor, preferred_element_type=jnp.float32
    )
    grad_up_router = jnp.einsum(
        "tr,te->re", low_router, grad_logits, preferred_element_type=jnp.float32
    )
    grad_down_router = jnp.einsum(
        "td,tr->rd", normed_two, grad_low_router, preferred_element_type=jnp.float32
    )
    grad_down_ffn = jnp.einsum(
        "td,tr->rd", normed_two, grad_low_ffn, preferred_element_type=jnp.float32
    )
    grad_normed_two = grad_normed_two + jnp.einsum(
        "tr,dr->td", grad_low_ffn, down_factor_list[5], preferred_element_type=jnp.float32
    )
    grad_normed_two = grad_normed_two + jnp.einsum(
        "te,de->td", grad_logits, router_weight, preferred_element_type=jnp.float32
    )
    grad_normed_two = grad_normed_two + jnp.einsum(
        "tr,dr->td", grad_low_router, down_factor_list[4], preferred_element_type=jnp.float32
    )
    grad_hidden = grad_out + norm_two_back(grad_normed_two)[0]
    grad_branch = grad_hidden.astype(jnp.bfloat16)
    weight_qkv_back, weight_out_back = (
        lax.all_gather(query_key_value_weight, "fsdp", axis=1, tiled=True),
        lax.all_gather(attention_output_weight, "fsdp", axis=0, tiled=True),
    )
    grad_up_out = jnp.einsum("tr,te->re", low_out, grad_branch, preferred_element_type=jnp.float32)
    grad_low_out = jnp.einsum(
        "te,re->tr", grad_branch, up_factor_list[3], preferred_element_type=jnp.float32
    )
    grad_down_out = jnp.einsum(
        "td,tr->rd", mixture, grad_low_out, preferred_element_type=jnp.float32
    )
    grad_mixture = (
        jnp.einsum("te,de->td", grad_branch, weight_out_back, preferred_element_type=jnp.float32)
        + jnp.einsum(
            "tr,dr->td", grad_low_out, down_factor_list[3], preferred_element_type=jnp.float32
        )
    ).astype(jnp.bfloat16)
    grad_query, grad_key, grad_value, *grad_left = attention_call(
        attend_back_kernel,
        qkv,
        left_kv,
        [grad_mixture],
        key_doc,
        own_doc,
        [
            ("block", jnp.bfloat16),
            ("cols", jnp.float32),
            ("cols", jnp.float32),
            ("cols", jnp.bfloat16),
            ("cols", jnp.bfloat16),
        ],
        1,
        10,
    )
    sent_back = shifted(jnp.stack(grad_left), "fsdp", -1).astype(jnp.float32)
    grad_qkv = jnp.stack(
        [
            grad_query,
            (grad_key + sent_back[0]).astype(jnp.bfloat16),
            (grad_value + sent_back[1]).astype(jnp.bfloat16),
        ]
    )
    grad_up_qkv = jnp.einsum("ptr,pte->pre", low_qkv, grad_qkv, preferred_element_type=jnp.float32)
    grad_low_qkv = jnp.einsum(
        "pte,pre->ptr", grad_qkv, up_factor_list[:3], preferred_element_type=jnp.float32
    )
    grad_down_qkv = jnp.einsum(
        "td,ptr->prd", normed, grad_low_qkv, preferred_element_type=jnp.float32
    )
    grad_normed = jnp.einsum(
        "pte,pde->td", grad_qkv, weight_qkv_back, preferred_element_type=jnp.float32
    ) + jnp.einsum(
        "ptr,pdr->td", grad_low_qkv, down_factor_list[:3], preferred_element_type=jnp.float32
    )
    grad_tokens = (grad_hidden + norm_one_back(grad_normed)[0]).astype(jnp.bfloat16)
    grad_rows = jnp.concatenate(
        [
            grad_down_qkv.reshape(3 * adapter_rank_width, width),
            grad_down_out,
            grad_down_router,
            grad_down_ffn,
            grad_up_qkv.reshape(3 * adapter_rank_width, width),
            grad_up_out,
        ]
    )
    totals = spread_sums(
        grad_rows, grad_up_router, grad_up_ffn, adapter_choice, adapter_total, by_tokens
    )
    if by_tokens:
        expert_sum, _ = lax.optimization_barrier((expert_sum, grad_qkv))
        expert_sum = sum(part.astype(jnp.float32) for part in expert_sum)
    output = (hidden_res + expert_sum).astype(jnp.bfloat16)
    return (output[None], grad_tokens[None], totals[0], totals[1], totals[2], totals[3])


def solution(mesh):
    in_specs = (
        P(("dp", "expert"), "fsdp", None),
        P(),
        P(),
        P(None, "fsdp", None),
        P("fsdp", None),
        P(),
        P("expert", None, None),
        P("expert", None, None),
        P(),
        P(),
        P(),
        P(),
        P(("dp", "expert")),
        P(("dp", "expert"), None),
        P(("dp", "expert"), "fsdp", None),
        P(("dp", "expert"), "fsdp", None),
    )
    out_specs = (
        P(("dp", "expert"), "fsdp", None),
        P(("dp", "expert"), "fsdp", None),
        P(None, None, ("fsdp", "expert"), None),
        P(None, None, None, ("fsdp", "expert")),
        P(None, None, ("fsdp", "expert")),
        P(None, None, ("fsdp", "expert")),
    )
    return jax.shard_map(shards, mesh=mesh, in_specs=in_specs, out_specs=out_specs, check_vma=False)
```

```python
import functools
import math

import jax
import jax.numpy as jnp
from jax import lax
from jax.experimental import pallas as pl
from jax.experimental.pallas import tpu as pltpu
from jax.sharding import PartitionSpec as P

DP, FSDP, EXPERT = "dp", "fsdp", "expert"
HEADS = 12
HEAD_DIM = 64


EPSILON = 1e-06
MASKED = -1e30


def shifted(block, axis, distance):
    devices = range(lax.axis_size(axis))
    route = [(i - distance, i) for i in devices if i - distance in devices]
    return lax.ppermute(block, axis, route)


def rms_norm(values, gain_vec):
    return (
        values * lax.rsqrt(jnp.mean(values * values, axis=-1, keepdims=True) + EPSILON) * gain_vec
    )


def block_scores(query_part, key_group, query_place, query_label, key_pos, key_doc, score_scale):
    raw_scores = (
        jnp.einsum("qhd,khd->hqk", query_part, key_group, preferred_element_type=jnp.float32)
        * score_scale
    )
    allowed = (
        (key_pos[None, :] <= query_place[:, None])
        & (key_pos[None, :] >= 0)
        & (key_doc[None, :] == query_label[:, None])
    )
    return jnp.where(allowed[None], raw_scores, MASKED)


def attend_forward(queries, key_rows, value_rows, query_pos, query_doc, key_pos, key_doc):
    row_count = queries.shape[0]
    key_count = key_rows.shape[0]
    group_heads = min(4, HEADS)
    group_count = HEADS // group_heads
    block_rows = min(512, row_count)
    block_count = row_count // block_rows
    group_width = group_heads * HEAD_DIM
    score_scale = 1.0 / math.sqrt(HEAD_DIM)

    def per_group(group_id):
        key_group = lax.dynamic_slice_in_dim(
            key_rows, group_id * group_width, group_width, 1
        ).reshape(key_count, group_heads, HEAD_DIM)
        value_group = lax.dynamic_slice_in_dim(
            value_rows, group_id * group_width, group_width, 1
        ).reshape(key_count, group_heads, HEAD_DIM)

        def per_block(block_id):
            query_part = lax.dynamic_slice(
                queries, (block_id * block_rows, group_id * group_width), (block_rows, group_width)
            ).reshape(block_rows, group_heads, HEAD_DIM)
            scores = block_scores(
                query_part, key_group, query_pos, query_doc, key_pos, key_doc, score_scale
            )
            largest = jnp.max(scores, axis=-1, keepdims=True)
            exp_scores = jnp.exp(scores - largest)
            row_total = jnp.sum(exp_scores, axis=-1, keepdims=True)
            probability = exp_scores / row_total
            log_total = largest[..., 0] + jnp.log(row_total[..., 0])
            mixture = jnp.einsum(
                "hqk,khd->qhd",
                probability.astype(jnp.bfloat16),
                value_group,
                preferred_element_type=jnp.float32,
            )
            return (mixture.reshape(block_rows, group_width), log_total)

        return lax.map(per_block, jnp.arange(block_count, dtype=jnp.int32))

    mixture, log_total = lax.map(per_group, jnp.arange(group_count, dtype=jnp.int32))
    mixture = mixture.transpose(1, 2, 0, 3).reshape(row_count, group_count * group_width)
    return (mixture, log_total)


def attend_backward(
    queries, key_rows, value_rows, grad_mix, log_total, query_pos, query_doc, key_pos, key_doc
):
    row_count = queries.shape[0]
    key_count = key_rows.shape[0]
    group_heads = min(4, HEADS)
    group_count = HEADS // group_heads
    block_rows = min(512, row_count)
    block_count = row_count // block_rows
    group_width = group_heads * HEAD_DIM
    score_scale = 1.0 / math.sqrt(HEAD_DIM)

    def per_group(group_id):
        key_group = lax.dynamic_slice_in_dim(
            key_rows, group_id * group_width, group_width, 1
        ).reshape(key_count, group_heads, HEAD_DIM)
        value_group = lax.dynamic_slice_in_dim(
            value_rows, group_id * group_width, group_width, 1
        ).reshape(key_count, group_heads, HEAD_DIM)
        log_group = lax.dynamic_index_in_dim(log_total, group_id, 0, keepdims=False)

        def per_block(carry, block_id):
            key_acc, value_acc = carry
            query_part = lax.dynamic_slice(
                queries, (block_id * block_rows, group_id * group_width), (block_rows, group_width)
            ).reshape(block_rows, group_heads, HEAD_DIM)
            grad_part = lax.dynamic_slice(
                grad_mix, (block_id * block_rows, group_id * group_width), (block_rows, group_width)
            ).reshape(block_rows, group_heads, HEAD_DIM)
            log_part = lax.dynamic_index_in_dim(log_group, block_id, 0, keepdims=False)
            scores = block_scores(
                query_part, key_group, query_pos, query_doc, key_pos, key_doc, score_scale
            )
            probability = jnp.exp(scores - log_part[:, :, None])
            grad_prob = jnp.einsum(
                "qhd,khd->hqk", grad_part, value_group, preferred_element_type=jnp.float32
            )
            inner = jnp.sum(probability * grad_prob, axis=-1, keepdims=True)
            grad_score = (probability * (grad_prob - inner)).astype(jnp.bfloat16)
            grad_query = (
                jnp.einsum(
                    "hqk,khd->qhd", grad_score, key_group, preferred_element_type=jnp.float32
                )
                * score_scale
            )
            key_acc = (
                key_acc
                + jnp.einsum(
                    "hqk,qhd->khd", grad_score, query_part, preferred_element_type=jnp.float32
                )
                * score_scale
            )
            value_acc = value_acc + jnp.einsum(
                "hqk,qhd->khd",
                probability.astype(jnp.bfloat16),
                grad_part,
                preferred_element_type=jnp.float32,
            )
            return ((key_acc, value_acc), grad_query.reshape(block_rows, group_width))

        empty = jnp.zeros((key_count, group_heads, HEAD_DIM), jnp.float32)
        (key_acc, value_acc), grad_query = lax.scan(
            per_block, (empty, empty), jnp.arange(block_count, dtype=jnp.int32)
        )
        return (
            grad_query,
            key_acc.reshape(key_count, group_width),
            value_acc.reshape(key_count, group_width),
        )

    grad_query, grad_key, grad_value = lax.map(per_group, jnp.arange(group_count, dtype=jnp.int32))
    grad_query = grad_query.transpose(1, 2, 0, 3).reshape(row_count, group_count * group_width)
    grad_key = grad_key.transpose(1, 0, 2).reshape(key_count, group_count * group_width)
    grad_value = grad_value.transpose(1, 0, 2).reshape(key_count, group_count * group_width)
    return (grad_query, grad_key, grad_value)


def expert_preact(token_part, adapt_part, expert_input_weight, flattened_up_factors):
    return jnp.einsum(
        "sxnd,xdf->sxnf", token_part, expert_input_weight, preferred_element_type=jnp.float32
    ) + jnp.einsum(
        "sxnr,rf->sxnf", adapt_part, flattened_up_factors, preferred_element_type=jnp.float32
    )


def shards_by_slots(
    tokens,
    attention_norm_gain,
    expert_norm_gain,
    query_key_value_weight,
    attention_output_weight,
    router_weight,
    expert_input_weight,
    expert_output_weight,
    adapter_down_factors,
    adapter_up_attention,
    adapter_up_routing,
    adapter_up_expert,
    sequence_adapter,
    position_document,
    routes,
    output_gradient,
):
    row_count = tokens.shape[1]
    width = tokens.shape[2]
    local_experts = expert_input_weight.shape[0]
    expert_groups = lax.axis_size(EXPERT)
    expert_count = local_experts * expert_groups
    capacity = 4 * row_count // expert_count
    adapter_total = adapter_down_factors.shape[1]
    adapter_rank_width = adapter_down_factors.shape[3]
    expert_hidden_width = expert_input_weight.shape[2]
    adapter_choice = sequence_adapter[0]
    half_index = lax.axis_index(FSDP)
    doc_row = position_document[0]
    x_in = tokens[0].astype(jnp.float32)
    gain_one = attention_norm_gain.astype(jnp.float32)
    gain_two = expert_norm_gain.astype(jnp.float32)
    normed_f, norm_one_back = jax.vjp(lambda values_in: rms_norm(values_in, gain_one), x_in)
    normed = normed_f.astype(jnp.bfloat16)
    weight_qkv, weight_out = (
        lax.all_gather(query_key_value_weight, FSDP, axis=1, tiled=True),
        lax.all_gather(attention_output_weight, FSDP, axis=0, tiled=True),
    )
    down_factor_list = lax.dynamic_index_in_dim(
        adapter_down_factors, adapter_choice, 1, keepdims=False
    )
    up_factor_list = lax.dynamic_index_in_dim(
        adapter_up_attention, adapter_choice, 1, keepdims=False
    )
    routing_up_factor = lax.dynamic_index_in_dim(
        adapter_up_routing, adapter_choice, 0, keepdims=False
    )
    low_qkv = jnp.einsum(
        "td,pdr->ptr", normed, down_factor_list[:3], preferred_element_type=jnp.float32
    ).astype(jnp.bfloat16)
    qkv = (
        jnp.einsum("td,pde->pte", normed, weight_qkv, preferred_element_type=jnp.float32)
        + jnp.einsum(
            "ptr,pre->pte", low_qkv, up_factor_list[:3], preferred_element_type=jnp.float32
        )
    ).astype(jnp.bfloat16)
    left_kv = shifted(qkv[1:], FSDP, 1)
    key_rows = jnp.concatenate([left_kv[0], qkv[1]], axis=0)
    value_rows = jnp.concatenate([left_kv[1], qkv[2]], axis=0)
    local_pos = jnp.arange(row_count, dtype=jnp.int32)
    query_pos = half_index * row_count + local_pos
    key_pos = jnp.concatenate([query_pos - row_count, query_pos])
    query_doc = lax.dynamic_slice_in_dim(doc_row, half_index * row_count, row_count)
    left_doc = lax.dynamic_slice_in_dim(
        doc_row, jnp.maximum(half_index - 1, 0) * row_count, row_count
    )
    key_doc = jnp.concatenate([left_doc, query_doc])
    mixture_f, log_total = attend_forward(
        qkv[0], key_rows, value_rows, query_pos, query_doc, key_pos, key_doc
    )
    mixture = mixture_f.astype(jnp.bfloat16)
    low_out = jnp.dot(mixture, down_factor_list[3], preferred_element_type=jnp.float32).astype(
        jnp.bfloat16
    )
    branch = jnp.dot(mixture, weight_out, preferred_element_type=jnp.float32) + jnp.dot(
        low_out, up_factor_list[3], preferred_element_type=jnp.float32
    )
    hidden_res = x_in + branch
    normed_two_f, norm_two_back = jax.vjp(
        lambda values_in: rms_norm(values_in, gain_two), hidden_res
    )
    normed_two = normed_two_f.astype(jnp.bfloat16)
    low_router = jnp.dot(
        normed_two, down_factor_list[4], preferred_element_type=jnp.float32
    ).astype(jnp.bfloat16)
    logits = jnp.dot(normed_two, router_weight, preferred_element_type=jnp.float32) + jnp.dot(
        low_router, routing_up_factor, preferred_element_type=jnp.float32
    )
    route_rows = routes[0]
    expert_ids = jnp.arange(expert_count, dtype=jnp.int32)
    choose_hot = (route_rows[:, :, None] == expert_ids[None, None, :]).astype(jnp.float32)
    picked = jnp.sum(logits[:, None, :] * choose_hot, axis=-1)
    gate_probs = jax.nn.softmax(picked, axis=-1)
    low_ffn = jnp.dot(normed_two, down_factor_list[5], preferred_element_type=jnp.float32).astype(
        jnp.bfloat16
    )
    adapter_one = (jnp.arange(adapter_total, dtype=jnp.int32) == adapter_choice).astype(jnp.float32)
    adapter_place = adapter_one.astype(jnp.bfloat16)
    adapter_rows = (adapter_place[None, :, None] * low_ffn[:, None, :]).reshape(
        row_count, adapter_total * adapter_rank_width
    )
    flat_routes = route_rows.reshape(-1)
    route_hot = (flat_routes[:, None] == expert_ids[None, :]).astype(jnp.int32)
    route_rank = jnp.sum((jnp.cumsum(route_hot, axis=0) - route_hot) * route_hot, axis=1)
    slot_index = flat_routes * capacity + route_rank
    assign_count = 2 * row_count
    slot_owner = (
        jnp.full((expert_count * capacity,), assign_count, jnp.int32)
        .at[slot_index]
        .set(jnp.arange(assign_count, dtype=jnp.int32))
    )
    owner_token = slot_owner // 2
    pad_rows = jnp.zeros((1, width), jnp.bfloat16)
    send_tokens = jnp.concatenate([normed_two, pad_rows], axis=0)[owner_token].reshape(
        expert_groups, local_experts, capacity, width
    )
    send_adapt = jnp.concatenate(
        [adapter_rows, jnp.zeros((1, adapter_total * adapter_rank_width), jnp.bfloat16)], axis=0
    )[owner_token].reshape(
        expert_groups, local_experts, capacity, adapter_total * adapter_rank_width
    )
    flattened_up_factors = adapter_up_expert.reshape(
        adapter_total * adapter_rank_width, expert_hidden_width
    )
    token_part = lax.all_to_all(send_tokens, EXPERT, split_axis=0, concat_axis=0, tiled=True)
    adapt_part = lax.all_to_all(send_adapt, EXPERT, split_axis=0, concat_axis=0, tiled=True)
    preact = expert_preact(token_part, adapt_part, expert_input_weight, flattened_up_factors)
    activation = jax.nn.gelu(preact).astype(jnp.bfloat16)
    result = jnp.einsum(
        "sxnf,xfd->sxnd", activation, expert_output_weight, preferred_element_type=jnp.float32
    ).astype(jnp.bfloat16)
    returned = lax.all_to_all(result, EXPERT, split_axis=0, concat_axis=0, tiled=True)
    expert_rows = (
        returned.reshape(expert_count * capacity, width)[slot_index]
        .reshape(row_count, 2, width)
        .astype(jnp.float32)
    )
    expert_sum = jnp.sum(gate_probs[:, :, None] * expert_rows, axis=1)
    output = (hidden_res + expert_sum).astype(jnp.bfloat16)
    grad_out = output_gradient[0].astype(jnp.float32)
    grad_gate = jnp.sum(grad_out[:, None, :] * expert_rows, axis=-1)
    grad_pick = gate_probs * (grad_gate - jnp.sum(gate_probs * grad_gate, axis=-1, keepdims=True))
    grad_logits = jnp.sum(grad_pick[:, :, None] * choose_hot, axis=1)
    grad_assign = (
        (gate_probs[:, :, None] * grad_out[:, None, :])
        .astype(jnp.bfloat16)
        .reshape(assign_count, width)
    )
    send_grad = jnp.concatenate([grad_assign, pad_rows], axis=0)[slot_owner].reshape(
        expert_groups, local_experts, capacity, width
    )
    grad_recv = lax.all_to_all(send_grad, EXPERT, split_axis=0, concat_axis=0, tiled=True)
    grad_act = jnp.einsum(
        "sxnd,xfd->sxnf", grad_recv, expert_output_weight, preferred_element_type=jnp.float32
    )
    grad_pre = jax.vjp(jax.nn.gelu, preact)[1](grad_act)[0].astype(jnp.bfloat16)
    grad_tok_expert = jnp.einsum(
        "sxnf,xdf->sxnd", grad_pre, expert_input_weight, preferred_element_type=jnp.float32
    ).astype(jnp.bfloat16)
    grad_adapt_expert = jnp.einsum(
        "sxnf,rf->sxnr", grad_pre, flattened_up_factors, preferred_element_type=jnp.float32
    ).astype(jnp.bfloat16)
    grad_up_ffn = jnp.einsum(
        "sxnr,sxnf->rf", adapt_part, grad_pre, preferred_element_type=jnp.float32
    ).reshape(adapter_total, adapter_rank_width, expert_hidden_width)
    grad_back_tok, grad_back_adapt = (
        lax.all_to_all(grad_tok_expert, EXPERT, split_axis=0, concat_axis=0, tiled=True),
        lax.all_to_all(grad_adapt_expert, EXPERT, split_axis=0, concat_axis=0, tiled=True),
    )
    grad_normed_two = jnp.sum(
        grad_back_tok.reshape(expert_count * capacity, width)[slot_index]
        .astype(jnp.float32)
        .reshape(row_count, 2, width),
        axis=1,
    )
    adapt_back = grad_back_adapt.reshape(
        expert_count * capacity, adapter_total, adapter_rank_width
    )[slot_index].astype(jnp.float32)
    grad_low_ffn = jnp.sum(
        jnp.sum(adapt_back * adapter_one[None, :, None], axis=1).reshape(
            row_count, 2, adapter_rank_width
        ),
        axis=1,
    )
    grad_low_router = jnp.einsum(
        "te,re->tr", grad_logits, routing_up_factor, preferred_element_type=jnp.float32
    )
    grad_up_router = jnp.einsum(
        "tr,te->re", low_router, grad_logits, preferred_element_type=jnp.float32
    )
    grad_down_router = jnp.einsum(
        "td,tr->dr", normed_two, grad_low_router, preferred_element_type=jnp.float32
    )
    grad_down_ffn = jnp.einsum(
        "td,tr->dr", normed_two, grad_low_ffn, preferred_element_type=jnp.float32
    )
    grad_normed_two = grad_normed_two + jnp.einsum(
        "tr,dr->td", grad_low_ffn, down_factor_list[5], preferred_element_type=jnp.float32
    )
    grad_normed_two = grad_normed_two + jnp.einsum(
        "te,de->td", grad_logits, router_weight, preferred_element_type=jnp.float32
    )
    grad_normed_two = grad_normed_two + jnp.einsum(
        "tr,dr->td", grad_low_router, down_factor_list[4], preferred_element_type=jnp.float32
    )
    grad_hidden = grad_out + norm_two_back(grad_normed_two)[0]
    grad_branch = grad_hidden.astype(jnp.bfloat16)
    weight_qkv_back, weight_out_back = (
        lax.all_gather(query_key_value_weight, FSDP, axis=1, tiled=True),
        lax.all_gather(attention_output_weight, FSDP, axis=0, tiled=True),
    )
    grad_up_out = jnp.einsum("tr,te->re", low_out, grad_branch, preferred_element_type=jnp.float32)
    grad_low_out = jnp.einsum(
        "te,re->tr", grad_branch, up_factor_list[3], preferred_element_type=jnp.float32
    )
    grad_down_out = jnp.einsum(
        "td,tr->dr", mixture, grad_low_out, preferred_element_type=jnp.float32
    )
    grad_mixture = (
        jnp.einsum("te,de->td", grad_branch, weight_out_back, preferred_element_type=jnp.float32)
        + jnp.einsum(
            "tr,dr->td", grad_low_out, down_factor_list[3], preferred_element_type=jnp.float32
        )
    ).astype(jnp.bfloat16)
    grad_query, grad_key, grad_value = attend_backward(
        qkv[0],
        key_rows,
        value_rows,
        grad_mixture,
        log_total,
        query_pos,
        query_doc,
        key_pos,
        key_doc,
    )
    sent_back = shifted(
        jnp.stack([grad_key[:row_count], grad_value[:row_count]]).astype(jnp.bfloat16), FSDP, -1
    ).astype(jnp.float32)
    grad_qkv = jnp.stack(
        [grad_query, grad_key[row_count:] + sent_back[0], grad_value[row_count:] + sent_back[1]]
    ).astype(jnp.bfloat16)
    grad_up_qkv = jnp.einsum("ptr,pte->pre", low_qkv, grad_qkv, preferred_element_type=jnp.float32)
    grad_low_qkv = jnp.einsum(
        "pte,pre->ptr", grad_qkv, up_factor_list[:3], preferred_element_type=jnp.float32
    )
    grad_down_qkv = jnp.einsum(
        "td,ptr->pdr", normed, grad_low_qkv, preferred_element_type=jnp.float32
    )
    grad_normed = jnp.einsum(
        "pte,pde->td", grad_qkv, weight_qkv_back, preferred_element_type=jnp.float32
    ) + jnp.einsum(
        "ptr,pdr->td", grad_low_qkv, down_factor_list[:3], preferred_element_type=jnp.float32
    )
    grad_tokens = (grad_hidden + norm_one_back(grad_normed)[0]).astype(jnp.bfloat16)
    grad_down = jnp.concatenate(
        [grad_down_qkv, grad_down_out[None], grad_down_router[None], grad_down_ffn[None]], axis=0
    )
    grad_down_all = adapter_one[None, :, None, None] * grad_down[:, None]
    grad_up_attn = jnp.concatenate([grad_up_qkv, grad_up_out[None]], axis=0)
    grad_up_attn_all = adapter_one[None, :, None, None] * grad_up_attn[:, None]
    grad_router_all = adapter_one[:, None, None] * grad_up_router[None]
    group_parts = (
        lax.psum_scatter(grad_down_all, (FSDP, EXPERT), scatter_dimension=2, tiled=True),
        lax.psum_scatter(grad_up_attn_all, (FSDP, EXPERT), scatter_dimension=3, tiled=True),
        lax.psum_scatter(grad_router_all, (FSDP, EXPERT), scatter_dimension=2, tiled=True),
        lax.psum_scatter(grad_up_ffn, (FSDP, EXPERT), scatter_dimension=2, tiled=True),
    )
    totals = lax.psum((group_parts[0], group_parts[1], group_parts[2], group_parts[3]), DP)
    return (output[None], grad_tokens[None], totals[0], totals[1], totals[2], totals[3])


def mxu(left, right, left_dim=1, right_dim=0):
    return lax.dot_general(
        left, right, (((left_dim,), (right_dim,)), ((), ())), preferred_element_type=jnp.float32
    )


def normed_rows(values, gain):
    return (
        values * lax.rsqrt(jnp.mean(values * values, axis=-1, keepdims=True) + EPSILON) * gain
    )


def norm_back(values, gain, grad):
    root = lax.rsqrt(jnp.mean(values * values, axis=-1, keepdims=True) + EPSILON)
    inner = grad * gain
    mean = jnp.mean(values * inner, axis=-1, keepdims=True)
    return root * inner - values * (root * root * root * mean)


def gate_rows(x, down, upr, router, routes):
    rank = upr.shape[1]
    low = mxu(down, x, 1, 1)
    low_router = low[:rank].astype(jnp.bfloat16)
    logits = mxu(router, x, 1, 1) + mxu(upr, low_router)
    ids = lax.broadcasted_iota(jnp.int32, logits.shape, 0)
    hot = (ids == routes[0:1]) | (ids == routes[1:2])
    top = jnp.max(jnp.where(hot, logits, -jnp.inf), axis=0, keepdims=True)
    ex = jnp.where(hot, jnp.exp(logits - top), 0.0)
    gates = ex / jnp.sum(ex, axis=0, keepdims=True)
    return low_router, low[rank:].astype(jnp.bfloat16), gates, hot, ids


def dense_call(kernel, scalars, grid, inputs, outputs, scratch, flops):
    return pl.pallas_call(
        kernel,
        grid_spec=pltpu.PrefetchScalarGridSpec(
            num_scalar_prefetch=1,
            grid=grid,
            in_specs=[pl.BlockSpec(block, index) for _, block, index in inputs],
            out_specs=[pl.BlockSpec(block, index) for _, _, block, index in outputs],
            scratch_shapes=[pltpu.VMEM(shape, kind) for shape, kind in scratch],
        ),
        out_shape=[jax.ShapeDtypeStruct(shape, kind) for shape, kind, _, _ in outputs],
        compiler_params=pltpu.CompilerParams(vmem_limit_bytes=56000 * 1024),
        cost_estimate=pl.CostEstimate(flops=flops, bytes_accessed=flops // 256, transcendentals=0),
    )(scalars, *(array for array, _, _ in inputs))


def fill_joined(half, mine, other, weight_s):
    tall = mine.shape[0]
    weight_s[pl.ds(pl.multiple_of(half * tall, tall), tall), :] = mine
    weight_s[pl.ds(pl.multiple_of((1 - half) * tall, tall), tall), :] = other


def first_kernel(sc, x_ref, left_ref, gain_ref, mine_ref, other_ref, down_ref, up_ref, *outs):
    normed_ref, low_ref, q_ref, kv_ref, xn_s, weight_s = outs
    step = pl.program_id(0)
    rows, width = x_ref.shape
    rank = up_ref.shape[2]
    bf16 = jnp.bfloat16

    @pl.when(step == 0)
    def _():
        gain = gain_ref[...].astype(jnp.float32)
        factors = down_ref[:, 0].reshape(down_ref.shape[0] * rank, width)
        for at, ref in ((0, left_ref), (rows, x_ref)):
            xn = normed_rows(ref[...].astype(jnp.float32), gain).astype(bf16)
            xn_s[at : at + rows, :width] = xn
            low = mxu(xn, factors, 1, 1).astype(bf16)
            blank = jnp.zeros((rows, xn_s.shape[1] - width - low.shape[1]), bf16)
            xn_s[at : at + rows, width:] = jnp.concatenate([low, blank], axis=1)
            if at > 0:
                normed_ref[...] = xn
                low = low.astype(jnp.float32).T.astype(bf16)
                for p in range(low_ref.shape[0]):
                    low_ref[p] = low[p * rank : (p + 1) * rank]
        weight_s[width:, :] = jnp.zeros((weight_s.shape[0] - width, width), bf16)

    fill_joined(sc[0], mine_ref[0], other_ref[0], weight_s)
    for p in range(low_ref.shape[0]):
        at = width + p * rank
        factor = up_ref[0, 0]
        weight_s[at : at + rank, :] = jnp.where(step == p, factor, jnp.zeros_like(factor))

    @pl.when(step == 0)
    def _():
        q_ref[...] = mxu(xn_s[rows:, :], weight_s[...]).astype(bf16)

    @pl.when(step > 0)
    def _():
        kv_ref[0] = mxu(xn_s[...], weight_s[...]).astype(bf16)


def project_in(scalars, x, left, gain, mine, other, downs, ups):
    rows, width = x.shape
    rank = downs.shape[2]
    bf16 = jnp.bfloat16
    whole = lambda i, s: (0, 0)
    lead = lambda i, s: (i, 0, 0)
    factor = lambda i, s: (i, s[1], 0, 0)
    return dense_call(
        first_kernel,
        scalars,
        (3,),
        [
            (x, (rows, width), whole),
            (left, (rows, width), whole),
            (gain.reshape(1, width), (1, width), whole),
            (mine, (1, width // 2, width), lead),
            (other, (1, width // 2, width), lead),
            (downs, (3, 1, rank, width), lambda i, s: (0, s[1], 0, 0)),
            (ups, (1, 1, rank, width), factor),
        ],
        [
            ((rows, width), bf16, (rows, width), whole),
            ((3, rank, rows), bf16, (3, rank, rows), lambda i, s: (0, 0, 0)),
            ((rows, width), bf16, (rows, width), whole),
            (
                (2, 2 * rows, width),
                bf16,
                (1, 2 * rows, width),
                lambda i, s: (jnp.maximum(i - 1, 0), 0, 0),
            ),
        ],
        [((2 * rows, width + 128), bf16), ((width + 128, width), bf16)],
        10 * rows * width * width,
    )


def middle_kernel(sc, x_ref, att_ref, mine_ref, other_ref, down_ref, up_ref, gain_ref, *outs):
    low_ref, hidden_ref, normed_ref, weight_s = outs

    @pl.when(pl.program_id(0) == 0)
    def _():
        fill_joined(sc[0], mine_ref[...], other_ref[...], weight_s)

    att = att_ref[...]
    low = mxu(att, down_ref[0, 0], 1, 1)
    low_ref[...] = low.T.astype(jnp.bfloat16)
    low = low.astype(jnp.bfloat16)
    hidden = x_ref[...].astype(jnp.float32) + (
        mxu(att, weight_s[...]) + mxu(low, up_ref[0, 0])
    )
    hidden_ref[...] = hidden
    normed_ref[...] = normed_rows(hidden, gain_ref[...].astype(jnp.float32)).astype(jnp.bfloat16)


def project_out(scalars, x, att, mine, other, downs, ups, gain):
    rows, width = x.shape
    rank = downs.shape[2]
    tall = rows // 2
    whole = lambda i, s: (0, 0)
    block = lambda i, s: (i, 0)
    return dense_call(
        middle_kernel,
        scalars,
        (2,),
        [
            (x, (tall, width), block),
            (att, (tall, width), block),
            (mine, (width // 2, width), whole),
            (other, (width // 2, width), whole),
            (downs, (1, 1, rank, width), lambda i, s: (3, s[1], 0, 0)),
            (ups, (1, 1, rank, width), lambda i, s: (3, s[1], 0, 0)),
            (gain.reshape(1, width), (1, width), whole),
        ],
        [
            ((rank, rows), jnp.bfloat16, (rank, tall), lambda i, s: (0, i)),
            ((rows, width), jnp.float32, (tall, width), block),
            ((rows, width), jnp.bfloat16, (tall, width), block),
        ],
        [((width, width), jnp.bfloat16)],
        2 * rows * width * width,
    )


def after_kernel(share, wide, sc, *refs):
    dx_refs, extra_refs = refs[:5], refs[5:10]
    (
        go_ref,
        hidden_ref,
        normed_ref,
        att_ref,
        low_ref,
        routes_ref,
        down45_ref,
        router_ref,
        upr_ref,
        down3_ref,
        up3_ref,
        mine_ref,
        other_ref,
        gain_ref,
        datt_ref,
        dh_ref,
        rows_ref,
        weight_s,
    ) = refs[10:]
    bf16, f32 = jnp.bfloat16, jnp.float32
    rank = down3_ref.shape[2]

    @pl.when(pl.program_id(0) == 0)
    def _():
        rows_ref[...] = jnp.zeros_like(rows_ref)
        fill_joined(sc[0], mine_ref[...], other_ref[...], weight_s)

    xn = normed_ref[...]
    low_router, _, gates, _, ids = gate_rows(
        xn, down45_ref[0], upr_ref[0], router_ref[...], routes_ref[0]
    )
    extra = sum(ref[...].astype(f32) for ref in extra_refs)
    dgate = 0.0
    for k in range(2):
        value = extra[rank + k : rank + k + 1] + extra[rank + 8 + k : rank + 9 + k]
        dgate = dgate + jnp.where(ids == routes_ref[0, k : k + 1], value, 0.0)
    dlogits = gates * (dgate - jnp.sum(gates * dgate, axis=0, keepdims=True))
    dlogits = dlogits.astype(bf16)
    dlr = mxu(upr_ref[0], dlogits, 0, 0).astype(bf16)
    dlf = extra[:rank].astype(bf16)
    dxn = sum(ref[...].astype(f32) for ref in dx_refs)
    dxn = dxn + mxu(dlr, down45_ref[0, :rank], 0, 0) + mxu(dlf, down45_ref[0, rank:], 0, 0)
    dxn = dxn + mxu(dlogits, router_ref[...], 0, 0)
    dh = go_ref[...].astype(f32) + norm_back(hidden_ref[...], gain_ref[...].astype(f32), dxn)
    dh_ref[...] = dh
    gb = dh.astype(bf16)
    att = att_ref[...]
    dlo = mxu(up3_ref[0, 0], gb, 1, 1).astype(bf16)
    datt_ref[...] = (mxu(gb, weight_s[...], 1, 1) + mxu(dlo, down3_ref[0, 0], 0, 0)).astype(bf16)
    router = mxu(low_router, dlogits, 1, 1).astype(bf16)
    choices, width = router_ref.shape
    column = lax.broadcasted_iota(jnp.int32, (choices, width), 0)
    lane = lax.broadcasted_iota(jnp.int32, (choices, width), 1)
    spot = lane == (column // wide) * share + column % wide
    rows_ref[0] += mxu(dlo, att)
    rows_ref[1] += mxu(dlr, xn)
    rows_ref[2] += mxu(dlf, xn)
    rows_ref[3] += mxu(low_ref[...], gb)
    rows_ref[4] += mxu(router, spot.astype(f32).astype(bf16))


def after_experts(
    scalars, dxs, go, hidden, normed, att, low, routes, down_t, router_t, upr_t, downs, ups, mine,
    other, gain, share, wide
):
    rows, width = hidden.shape
    rank = downs.shape[2]
    tall = rows // 2
    choices = router_t.shape[0]
    extra = dxs[0].shape[0] - rows
    whole = lambda i, s: (0, 0)
    block = lambda i, s: (i, 0)
    adapter = lambda i, s: (s[1], 0, 0)
    return dense_call(
        functools.partial(after_kernel, share, wide),
        scalars,
        (2,),
        [(dx, (tall, width), block) for dx in dxs]
        + [(dx, (extra, tall), lambda i, s: (rows // extra, i)) for dx in dxs]
        + [(array, (tall, width), block) for array in (go, hidden, normed, att)]
        + [
            (low, (rank, tall), lambda i, s: (0, i)),
            (routes, (1, 2, tall), lambda i, s: (0, 0, i)),
            (down_t, (1, 2 * rank, width), adapter),
            (router_t, (choices, width), whole),
            (upr_t, (1, choices, rank), adapter),
            (downs, (1, 1, rank, width), lambda i, s: (3, s[1], 0, 0)),
            (ups, (1, 1, rank, width), lambda i, s: (3, s[1], 0, 0)),
            (mine, (width // 2, width), whole),
            (other, (width // 2, width), whole),
            (gain.reshape(1, width), (1, width), whole),
        ],
        [
            ((rows, width), jnp.bfloat16, (tall, width), block),
            ((rows, width), jnp.float32, (tall, width), block),
            ((5, rank, width), jnp.float32, (5, rank, width), lambda i, s: (0, 0, 0)),
        ],
        [((width, width), jnp.bfloat16)],
        3 * rows * width * width,
    )


def factors_kernel(sc, dq_ref, own_ref, back_ref, low_ref, up_ref, normed_ref, early_ref, *outs):
    grad_ref, glow_ref, kept_ref, given_ref = outs
    p = pl.program_id(0)
    bf16 = jnp.bfloat16
    summed = (own_ref[0] + back_ref[0].astype(jnp.float32)).astype(bf16)
    grad = jnp.where(p == 0, dq_ref[...], summed)
    grad_ref[0] = grad
    glow = mxu(up_ref[0, 0], grad, 1, 1).astype(bf16)
    glow_ref[0] = glow
    rank, width = glow.shape[0], grad.shape[1]
    half = sc[0]

    def put(at, value):
        low, high = value[:, : width // 2], value[:, width // 2 :]
        at = pl.ds(pl.multiple_of(at * rank, rank), rank)
        kept_ref[at, :] = jnp.where(half == 0, low, high)
        given_ref[at, :] = jnp.where(half == 0, high, low).astype(bf16)

    put(p, mxu(glow, normed_ref[...]))
    put(6 + p, mxu(low_ref[0], grad))

    @pl.when(p == 0)
    def _():
        for i, at in enumerate((3, 4, 5, 9, 10)):
            put(at, early_ref[i])
        put(11, jnp.full((rank, width), 0.5, jnp.float32) * sc[1].astype(jnp.float32))


def factor_grads(scalars, dq, own, back, low, ups, normed, early):
    rows, width = dq.shape
    rank = ups.shape[2]
    total = 12 * rank
    whole = lambda i, s: (0, 0)
    prior = lambda i, s: (jnp.maximum(i - 1, 0), 0, 0)
    lead = lambda i, s: (i, 0, 0)
    return dense_call(
        factors_kernel,
        scalars,
        (3,),
        [
            (dq, (rows, width), whole),
            (own, (1, rows, width), prior),
            (back, (1, rows, width), prior),
            (low, (1, rank, rows), lead),
            (ups, (1, 1, rank, width), lambda i, s: (i, s[1], 0, 0)),
            (normed, (rows, width), whole),
            (early, (5, rank, width), lambda i, s: (0, 0, 0)),
        ],
        [
            ((3, rows, width), jnp.bfloat16, (1, rows, width), lead),
            ((3, rank, rows), jnp.bfloat16, (1, rank, rows), lead),
            ((total, width // 2), jnp.float32, (total, width // 2), whole),
            ((total, width // 2), jnp.bfloat16, (total, width // 2), whole),
        ],
        [],
        rows * width * width // 4,
    )


def last_kernel(sc, grad_ref, glow_ref, mine_ref, other_ref, down_ref, x_ref, gain_ref, *refs):
    dh_ref, grad_x_ref, acc, weight_s = refs
    p = pl.program_id(0)
    fill_joined(sc[0], mine_ref[0], other_ref[0], weight_s)
    term = mxu(grad_ref[0], weight_s[...], 1, 1) + mxu(glow_ref[0], down_ref[0, 0], 0, 0)
    acc[...] = jnp.where(p == 0, term, acc[...] + term)

    @pl.when(p == pl.num_programs(0) - 1)
    def _():
        back = norm_back(
            x_ref[...].astype(jnp.float32), gain_ref[...].astype(jnp.float32), acc[...]
        )
        grad_x_ref[...] = (dh_ref[...] + back).astype(grad_x_ref.dtype)


def last_rows(scalars, grads, glow, mine, other, downs, x, gain, dh):
    rows, width = x.shape
    rank = downs.shape[2]
    whole = lambda i, s: (0, 0)
    lead = lambda i, s: (i, 0, 0)
    return dense_call(
        last_kernel,
        scalars,
        (3,),
        [
            (grads, (1, rows, width), lead),
            (glow, (1, rank, rows), lead),
            (mine, (1, width // 2, width), lead),
            (other, (1, width // 2, width), lead),
            (downs, (1, 1, rank, width), lambda i, s: (i, s[1], 0, 0)),
            (x, (rows, width), whole),
            (gain.reshape(1, width), (1, width), whole),
            (dh, (rows, width), whole),
        ],
        [((rows, width), jnp.bfloat16, (rows, width), whole)],
        [((rows, width), jnp.float32), ((width, width), jnp.bfloat16)],
        6 * rows * width * width,
    )


def sums_kernel(count, share, sc, *refs):
    part_refs = refs[:count]
    down_ref, up_ref, router_ref, ffn_ref, acc = refs[count:]
    rank, wide = ffn_ref.shape[1], part_refs[0].shape[2]
    acc[...] = jnp.zeros_like(acc)
    for part_ref in part_refs:
        for s in range(part_ref.shape[0]):
            part = part_ref[s].astype(jnp.float32)
            label = jnp.max(part[11 * rank : 11 * rank + 8, :share]).astype(jnp.int32)
            acc[label] += part
    for a in range(acc.shape[0]):
        rows = acc[a]
        for i in range(6):
            down_ref[i, a] = rows[i * rank : (i + 1) * rank, :share]
        for i in range(4):
            up_ref[i, a] = rows[(6 + i) * rank : (7 + i) * rank, :share]
        router_ref[a] = rows[10 * rank : 11 * rank, :share]
        for i in range(ffn_ref.shape[2] // wide):
            ffn_ref[a, :, i * wide : (i + 1) * wide] = rows[(12 + i) * rank : (13 + i) * rank]


def adapter_sums(scalars, parts, choices, rank, share, wide):
    f32 = jnp.float32
    outs = [
        (6, choices, rank, share),
        (4, choices, rank, share),
        (choices, rank, share),
        (choices, rank, wide),
    ]
    fixed = lambda shape: (shape, lambda i, s: (0,) * len(shape))
    return dense_call(
        functools.partial(sums_kernel, len(parts), share),
        scalars,
        (1,),
        [(part, *fixed(part.shape)) for part in parts],
        [(shape, f32, *fixed(shape)) for shape in outs],
        [((choices, *parts[0].shape[1:]), f32)],
        10**6,
    )


def window_bias(bias, kdoc_ref, qdoc_ref, block):
    keys, cols = bias.shape[1:]
    kpos = lax.broadcasted_iota(jnp.int32, (keys, cols), 0) - (keys - cols)
    qpos = lax.broadcasted_iota(jnp.int32, (keys, cols), 1)
    key_doc = kdoc_ref[pl.ds(pl.multiple_of(block * cols, cols), keys), :]
    bias[block] = jnp.where((kpos <= qpos) & (key_doc == qdoc_ref[...]), 0.0, MASKED)


def head_probability(queries, key_parts, bias, block, first):
    tall = queries.shape[0]
    scores = [
        mxu(part, queries, 1, 1) + bias[block, (first + i) * tall : (first + i + 1) * tall, :]
        for i, part in enumerate(key_parts)
    ]
    top = functools.reduce(jnp.maximum, [jnp.max(s, axis=0, keepdims=True) for s in scores])
    parts = [jnp.exp(s - top) for s in scores]
    total = sum(jnp.sum(p, axis=0, keepdims=True) for p in parts)
    share = 1.0 / total
    return [p * share for p in parts]


def attend_kernel(reach, kdoc_ref, qdoc_ref, q_ref, *refs):
    key_refs, value_refs = refs[:3], refs[3:6]
    out_ref, bias = refs[6:]
    block = pl.program_id(1)

    @pl.when(pl.program_id(0) == 0)
    def _():
        window_bias(bias, kdoc_ref, qdoc_ref, block)

    def run(first):
        keys, values = ([ref[0] for ref in part[first:]] for part in (key_refs, value_refs))
        mixed = []
        for head in range(q_ref.shape[1] // HEAD_DIM):
            cols = slice(head * HEAD_DIM, (head + 1) * HEAD_DIM)
            queries = q_ref[:, cols] * (1.0 / math.sqrt(HEAD_DIM))
            probability = head_probability(
                queries, [key[:, cols] for key in keys], bias, block, first
            )
            mixed.append(
                sum(
                    mxu(value[:, cols], p.astype(jnp.bfloat16), 0, 0)
                    for value, p in zip(values, probability)
                )
            )
        out_ref[...] = jnp.concatenate(mixed, axis=0).T.astype(out_ref.dtype)

    for first in range(2):
        pl.when(reach[block] == first)(functools.partial(run, first))


def attend_back_kernel(reach, kdoc_ref, qdoc_ref, q_ref, *refs):
    key_refs, value_refs = refs[:3], refs[3:6]
    grad_ref, dq_ref, own_ref, left_ref, bias, acc = refs[6:]
    block = pl.program_id(1)
    scale = 1.0 / math.sqrt(HEAD_DIM)

    @pl.when(pl.program_id(0) == 0)
    def _():
        window_bias(bias, kdoc_ref, qdoc_ref, block)

    @pl.when(block == 0)
    def _():
        acc[...] = jnp.zeros_like(acc)

    def run(first):
        keys, values = ([ref[0] for ref in part[first:]] for part in (key_refs, value_refs))
        grad_queries = []
        for head in range(q_ref.shape[1] // HEAD_DIM):
            cols = slice(head * HEAD_DIM, (head + 1) * HEAD_DIM)
            queries = q_ref[:, cols] * scale
            grad = grad_ref[:, cols]
            probability = head_probability(
                queries, [key[:, cols] for key in keys], bias, block, first
            )
            grad_prob = [mxu(value[:, cols], grad, 1, 1) for value in values]
            inner = sum(
                jnp.sum(p * g, axis=0, keepdims=True) for p, g in zip(probability, grad_prob)
            )
            grad_score = [
                (p * (g - inner)).astype(jnp.bfloat16) for p, g in zip(probability, grad_prob)
            ]
            grad_queries.append(
                sum(mxu(key[:, cols], g, 0, 0) for key, g in zip(keys, grad_score)) * scale
            )
            for i, (p, g) in enumerate(zip(probability, grad_score)):
                acc[0, block + first + i, :, cols] += mxu(g, queries)
                acc[1, block + first + i, :, cols] += mxu(p.astype(jnp.bfloat16), grad)
        dq_ref[...] = jnp.concatenate(grad_queries, axis=0).T.astype(dq_ref.dtype)

    for first in range(2):
        pl.when(reach[block] == first)(functools.partial(run, first))

    @pl.when(block == pl.num_programs(1) - 1)
    def _():
        tall = q_ref.shape[0]
        for i in range(2):
            rows = slice(i * tall, (i + 1) * tall)
            for kind in range(2):
                left_ref[kind, rows, :] = acc[kind, i].astype(left_ref.dtype)
                own_ref[kind, rows, :] = acc[kind, 2 + i].astype(own_ref.dtype)


def attention_call(kernel, queries, keys_values, grads, key_doc, query_doc, outs, scratch, flops):
    rows, width = queries.shape
    lanes = 2 * HEAD_DIM
    tall = rows // 2
    starts = jnp.arange(2, dtype=jnp.int32) * tall
    reach = (key_doc[starts + tall - 1] != query_doc[starts]).astype(jnp.int32)

    sources = [
        pl.BlockSpec((1, tall, lanes), lambda g, b, s, p=p, i=i: (p, b + i, g))
        for p in range(2)
        for i in range(3)
    ]

    def stack(kind):
        return {
            "block": pl.BlockSpec((tall, lanes), lambda g, b, s: (b, g)),
            "pair": pl.BlockSpec((2, rows, lanes), lambda g, b, s: (0, 0, g)),
        }[kind]

    return pl.pallas_call(
        kernel,
        grid_spec=pltpu.PrefetchScalarGridSpec(
            num_scalar_prefetch=1,
            grid=(width // lanes, 2),
            in_specs=[
                pl.BlockSpec((2 * rows, 1), lambda g, b, s: (0, 0)),
                pl.BlockSpec((1, tall), lambda g, b, s: (0, b)),
                stack("block"),
                *sources,
            ]
            + [stack("block")] * len(grads),
            out_specs=[stack(kind) for kind, _ in outs],
            scratch_shapes=[pltpu.VMEM((2, 3 * tall, tall), jnp.float32)]
            + [pltpu.VMEM((2, 4, tall, lanes), jnp.float32)] * scratch,
        ),
        out_shape=[
            jax.ShapeDtypeStruct((rows, width) if kind == "block" else (2, rows, width), dtype)
            for kind, dtype in outs
        ],
        compiler_params=pltpu.CompilerParams(vmem_limit_bytes=56000 * 1024),
        cost_estimate=pl.CostEstimate(
            flops=flops * rows * rows * width,
            bytes_accessed=12 * rows * width,
            transcendentals=HEADS * rows * rows,
        ),
        name="ab2" if scratch else "at",
    )(
        reach,
        key_doc.reshape(-1, 1),
        query_doc.reshape(1, -1),
        queries,
        *([keys_values] * 6),
        *grads,
    )


def gelu_both(u):
    c = math.sqrt(2.0 / math.pi)
    sq = u * u
    t = jnp.tanh(u * (c + (c * 0.044715) * sq))
    half = 0.5 + 0.5 * t
    slope = half + (0.5 * u) * (1.0 - t * t) * (c + (3.0 * c * 0.044715) * sq)
    return u * half, slope


def expert_kernel(pieces, capacity, rank, *refs):
    scalars = refs[0]
    x_refs, g_refs = refs[1 : 1 + pieces], refs[1 + pieces : 1 + 2 * pieces]
    (
        route_ref,
        down_ref,
        upr_ref,
        uf_ref,
        router_ref,
        w1_ref,
        w2_ref,
        _,
        y_ref,
        dx_ref,
        gff_ref,
        x_s,
        g_s,
        xe,
        goe,
        dye,
        lfe,
        yacc,
        dxacc,
        dleacc,
        onehot_s,
        lft_s,
        gate_s,
        rank_s,
        ysum,
        dxsum,
        ext_s,
    ) = refs[1 + 2 * pieces :]
    e = pl.program_id(0)
    t = pl.program_id(1)
    last_t = pl.num_programs(1) - 1
    last_e = pl.num_programs(0) - 1
    rows, width = x_refs[0].shape
    tile = w1_ref.shape[2]
    ident = scalars[0] + e
    bf16, f32 = jnp.bfloat16, jnp.float32

    @pl.when((e == 0) & (t == 0))
    def _():
        ysum[...] = jnp.zeros_like(ysum)
        dxsum[...] = jnp.zeros_like(dxsum)
        ext_s[...] = jnp.zeros_like(ext_s)
        gff_ref[...] = jnp.zeros_like(gff_ref)
        x = sum(ref[...] for ref in x_refs)
        x_s[...] = x
        g_s[...] = sum(ref[...] for ref in g_refs)
        _, lft_s[...], gate_s[...], hot, _ = gate_rows(
            x, down_ref[0], upr_ref[0], router_ref[...], route_ref[0]
        )
        before = lax.broadcasted_iota(jnp.int32, (rows, rows), 0) < lax.broadcasted_iota(
            jnp.int32, (rows, rows), 1
        )
        ranks = mxu(hot.astype(f32).astype(bf16), before.astype(f32).astype(bf16))
        rank_s[...] = jnp.where(hot, ranks, -1.0)

    def slots():
        row = rank_s[pl.ds(ident, 1), :]
        picks = lax.broadcasted_iota(jnp.int32, (capacity, rows), 0).astype(f32) == row
        gate = gate_s[pl.ds(ident, 1), :]
        return picks, jnp.sum(jnp.where(picks, gate, 0.0), axis=1, keepdims=True)

    @pl.when(t == 0)
    def _():
        picks, gate_slot = slots()
        onehot = picks.astype(f32).astype(bf16)
        onehot_s[...] = onehot
        xe[...] = mxu(onehot, x_s[...]).astype(bf16)
        go = mxu(onehot, g_s[...])
        goe[...] = go.astype(bf16)
        dye[...] = (go * gate_slot).astype(bf16)
        lfe[...] = mxu(onehot, lft_s[...], 1, 1).astype(bf16)
        yacc[...] = jnp.zeros_like(yacc)
        dxacc[...] = jnp.zeros_like(dxacc)
        dleacc[...] = jnp.zeros_like(dleacc)

    off = pl.multiple_of(t * tile, tile)
    pre = mxu(xe[...], w1_ref[0]) + mxu(lfe[...], uf_ref[0])
    act, slope = gelu_both(pre)
    yacc[...] += mxu(act.astype(bf16), w2_ref[0])
    dpre = (mxu(dye[...], w2_ref[0], 1, 1) * slope).astype(bf16)
    dxacc[...] += mxu(dpre, w1_ref[0], 1, 1)
    dleacc[...] += mxu(uf_ref[0], dpre, 1, 1)
    gff_ref[0, :, pl.ds(off, tile)] += mxu(lfe[...], dpre, 0, 0)

    @pl.when(t == last_t)
    def _():
        picks, gate_slot = slots()
        onehot = onehot_s[...]
        y = yacc[...].astype(bf16).astype(f32)
        dgate = jnp.sum(goe[...].astype(f32) * y, axis=1, keepdims=True)
        dgate_row = jnp.sum(jnp.where(picks, dgate, 0.0), axis=0, keepdims=True)
        for k in range(2):
            mine = route_ref[0, k : k + 1] == ident
            ext_s[rank + k : rank + k + 1, :] += jnp.where(mine, dgate_row, 0.0)
        ext_s[0:rank, :] += mxu(dleacc[...].astype(bf16), onehot)
        ysum[...] += mxu(onehot, (y * gate_slot).astype(bf16), 0, 0)
        dxsum[...] += mxu(onehot, dxacc[...].astype(bf16), 0, 0)

    @pl.when((e == last_e) & (t == last_t))
    def _():
        y_ref[...] = ysum[...].astype(bf16)
        dx_ref[:rows, :] = dxsum[...].astype(bf16)
        extra = ext_s[...]
        gates = extra[rank:]
        low = gates - gates.astype(bf16).astype(f32)
        packed = jnp.concatenate([extra, low], axis=0).astype(bf16)
        if width > rows:
            blank = jnp.zeros((packed.shape[0], width - rows), bf16)
            packed = jnp.concatenate([packed, blank], axis=1)
        dx_ref[rows:, :] = packed


def run_experts(
    scalars, local, xs, gs, route_rows, down_t, router_t, upr_t, up_ffn, w1, w2, gff, capacity
):
    pieces = len(xs)
    rows, width = xs[0].shape
    hidden = w1.shape[2]
    expert_count = router_t.shape[0]
    rank = up_ffn.shape[1]
    tile = 1024 if hidden % 1024 == 0 else hidden
    fixed = lambda *shape, **kw: pl.BlockSpec(shape, lambda e, t, sc: (0,) * len(shape), **kw)
    adapter = lambda *shape: pl.BlockSpec((1, *shape), lambda e, t, sc: (sc[1], 0, 0))
    at_spot = lambda k, *shape: pl.BlockSpec(
        (1, *shape), lambda e, t, sc: (sc[1 + k], 0, 0)
    )
    in_specs = [fixed(rows, width, pipeline_mode=pl.Buffered(1))] * (2 * pieces) + [
        at_spot(1, 2, rows),
        adapter(2 * rank, width),
        adapter(expert_count, rank),
        pl.BlockSpec((1, rank, tile), lambda e, t, sc: (sc[1], 0, t)),
        fixed(expert_count, width),
        pl.BlockSpec((1, width, tile), lambda e, t, sc: (e + sc[4], 0, t)),
        pl.BlockSpec((1, tile, width), lambda e, t, sc: (e + sc[4], t, 0)),
        pl.BlockSpec(memory_space=pl.ANY),
    ]
    bf16, f32 = jnp.bfloat16, jnp.float32
    scratch = [
        ((rows, width), bf16),
        ((rows, width), bf16),
        ((capacity, width), bf16),
        ((capacity, width), bf16),
        ((capacity, width), bf16),
        ((capacity, rank), bf16),
        ((capacity, width), f32),
        ((capacity, width), f32),
        ((rank, capacity), f32),
        ((capacity, rows), bf16),
        ((rank, rows), bf16),
        ((expert_count, rows), f32),
        ((expert_count, rows), f32),
        ((rows, width), f32),
        ((rows, width), f32),
        ((rank + 8, rows), f32),
    ]
    return pl.pallas_call(
        functools.partial(expert_kernel, pieces, capacity, rank),
        grid_spec=pltpu.PrefetchScalarGridSpec(
            num_scalar_prefetch=1,
            grid=(local, hidden // tile),
            in_specs=in_specs,
            out_specs=[
                fixed(rows, width),
                fixed(rows + rank + 16, width),
                at_spot(2, rank, hidden),
            ],
            scratch_shapes=[pltpu.VMEM(shape, kind) for shape, kind in scratch],
        ),
        out_shape=[
            jax.ShapeDtypeStruct((rows, width), bf16),
            jax.ShapeDtypeStruct((rows + rank + 16, width), bf16),
            jax.ShapeDtypeStruct(gff.shape, f32),
        ],
        input_output_aliases={1 + 2 * pieces + 7: 2},
        compiler_params=pltpu.CompilerParams(vmem_limit_bytes=58 * 1024 * 1024),
        cost_estimate=pl.CostEstimate(
            flops=8 * local * capacity * width * hidden,
            bytes_accessed=4 * local * width * hidden + 8 * rows * width,
            transcendentals=0,
        ),
        name="ex",
    )(
        scalars, *xs, *gs, route_rows, down_t, upr_t, up_ffn, router_t, w1, w2, gff
    )


CROSS = [(0, 1), (1, 0), (2, 3), (3, 2)]
INNER = [(1, 2), (2, 1)]
OUTWARD = [(1, 0), (2, 3)]
INWARD = [(0, 1), (3, 2)]
SKIP = [(1, 3), (2, 0)]
TWICE = [(0, 2), (2, 0), (1, 3), (3, 1)]
MIRROR = [(0, 3), (3, 0), (1, 2), (2, 1)]


def on_line(block, route):
    return lax.ppermute(block, EXPERT, route)


def exchange_all(block, axis):
    count = lax.axis_size(axis)
    return [block] + [
        lax.ppermute(block, axis, [(i, (i + step) % count) for i in range(count)])
        for step in range(1, count)
    ]


def shards_by_tokens(
    tokens,
    attention_norm_gain,
    expert_norm_gain,
    query_key_value_weight,
    attention_output_weight,
    router_weight,
    expert_input_weight,
    expert_output_weight,
    adapter_down_factors,
    adapter_up_attention,
    adapter_up_routing,
    adapter_up_expert,
    sequence_adapter,
    position_document,
    routes,
    output_gradient,
):
    rows, width = tokens.shape[1:]
    local = expert_input_weight.shape[0]
    groups = lax.axis_size(EXPERT)
    choices = local * groups
    capacity = 4 * rows // choices
    adapter_total, rank, hidden = adapter_up_expert.shape
    adapter = sequence_adapter[0]
    half = lax.axis_index(FSDP)
    place = lax.axis_index(EXPERT)
    at_end = (place == 0) | (place == groups - 1)
    bf16, f32 = jnp.bfloat16, jnp.float32
    swap = [(0, 1), (1, 0)]
    x, go = tokens[0], output_gradient[0]
    downs = jnp.swapaxes(adapter_down_factors, 2, 3)
    ups = adapter_up_attention
    down_t = jnp.swapaxes(downs[4:6], 0, 1).reshape(adapter_total, 2 * rank, width)
    upr_t = jnp.swapaxes(adapter_up_routing, 1, 2)
    router_t = router_weight.T
    scalars = jnp.stack([half, adapter]).astype(jnp.int32)

    weight_other = lax.ppermute(query_key_value_weight, FSDP, swap)
    left = lax.ppermute(x, FSDP, [(0, 1)])
    about = jnp.concatenate([routes[0].T, jnp.full((1, rows), adapter, jnp.int32)])
    about = [about, *(on_line(about, route) for route in (CROSS, TWICE, MIRROR))]
    go_across, go_inner = on_line(go, CROSS), on_line(go, INNER)
    normed, low_qkv, queries, keys_values = project_in(
        scalars, x, left, attention_norm_gain, query_key_value_weight, weight_other, downs, ups
    )
    out_other = lax.ppermute(attention_output_weight, FSDP, swap)
    doc_row = position_document[0]
    own_doc = lax.dynamic_slice_in_dim(doc_row, half * rows, rows)
    key_doc = jnp.concatenate([jnp.where(half > 0, doc_row[:rows], -1), own_doc])
    go_far_ends, go_far_inner = on_line(go_inner, OUTWARD), on_line(go_across, INNER)
    (att,) = attention_call(
        attend_kernel, queries, keys_values, [], key_doc, own_doc, [("block", bf16)], 0, 4
    )
    low_out, hidden_rows, normed_two = project_out(
        scalars, x, att, attention_output_weight, out_other, downs, ups, expert_norm_gain
    )

    about = jnp.stack(about)
    route_rows, adapters = about[:, :2], about[:, 2, 0]
    third, fourth = jnp.where(at_end, adapters[2:], adapters[:1:-1])
    near, far = jnp.where(at_end, 2, 3), jnp.where(at_end, 3, 2)
    base, part = place * local, local // 2
    turns = [
        jnp.stack(turn).astype(jnp.int32)
        for turn in (
            [base, adapters[1], 1, place ^ 1, 0],
            [base, third, near, place ^ near, 0],
            [base, fourth, far, place ^ far, 0],
            [base, adapters[0], 0, place, 0],
            [base + part, adapters[0], 0, groups, part],
        )
    ]

    def call(turn, xs, gs, gff, count=local):
        return run_experts(
            turns[turn],
            count,
            xs,
            gs,
            route_rows,
            down_t,
            router_t,
            upr_t,
            adapter_up_expert,
            expert_input_weight,
            expert_output_weight,
            gff,
            capacity,
        )

    merge = lambda one, two: (one.astype(f32) + two.astype(f32)).astype(bf16)
    gff = jnp.zeros((groups + 1, rank, hidden), f32)
    across, inner = on_line(normed_two, CROSS), on_line(normed_two, INNER)
    y_e, dx_e, gff = call(3, [normed_two], [go], gff, part)
    go_last = on_line(go_far_inner, OUTWARD)
    far_ends, far_inner = on_line(inner, OUTWARD), on_line(across, INNER)
    y_b, dx_b, gff = call(0, [across], [go_across], gff)
    last = on_line(far_inner, OUTWARD)
    back_b = on_line(dx_b, CROSS)
    y_c, dx_c, gff = call(1, [inner, far_ends], [go_inner, go_far_ends], gff)
    part_c = on_line(dx_c, INWARD)
    y_part_c = on_line(y_c, INWARD)
    y_d, dx_d, gff = call(2, [far_inner, last], [go_far_inner, go_last], gff)
    part_d = on_line(dx_d, INWARD)
    back_c = on_line(merge(dx_c, part_c), INNER)
    y_part_d = on_line(y_d, INWARD)
    y_a, dx_a, gff = call(4, [normed_two], [go], gff, local - part)
    back_d = on_line(merge(dx_d, part_d), SKIP)
    halves = gff.reshape(groups + 1, rank, 2, -1)
    halves = [lax.dynamic_index_in_dim(halves, at, 2, keepdims=False) for at in (half, 1 - half)]
    ffn_part = halves[0] + lax.ppermute(halves[1].astype(bf16), FSDP, swap).astype(f32)
    ffn_part = ffn_part.astype(bf16).reshape(groups + 1, rank, groups, -1)
    ffn_part = lax.all_to_all(
        jnp.moveaxis(ffn_part, 2, 0), EXPERT, split_axis=0, concat_axis=0, tiled=True
    )
    ffn_part = ffn_part.astype(f32)
    ffn_part = jnp.sum(ffn_part[:, :groups], axis=0) + ffn_part[:, groups]
    share, wide = width // (2 * groups), choices // (2 * groups)
    datt, dh, early = after_experts(
        scalars,
        [dx_a, dx_e, back_b, back_c, back_d],
        go,
        hidden_rows,
        normed_two,
        att,
        low_out,
        route_rows,
        down_t,
        router_t,
        upr_t,
        downs,
        ups,
        attention_output_weight,
        out_other,
        expert_norm_gain,
        share,
        wide,
    )
    outs, datt = lax.optimization_barrier(((y_b, y_c, y_part_c, y_d, y_part_d), datt))
    outs = outs[0], merge(*outs[1:3]), merge(*outs[3:])
    outs = [on_line(part, route) for part, route in zip(outs, (CROSS, INNER, SKIP))]
    dq, own, left_grads = attention_call(
        attend_back_kernel,
        queries,
        keys_values,
        [datt],
        key_doc,
        own_doc,
        [("block", bf16), ("pair", f32), ("pair", bf16)],
        1,
        10,
    )
    back = lax.ppermute(left_grads, FSDP, [(1, 0)])
    grads, glow, kept, given = factor_grads(
        scalars, dq, own, back, low_qkv, ups, normed, early
    )
    kept = (kept + lax.ppermute(given, FSDP, swap).astype(f32)).astype(bf16)
    lanes = 128
    parts = jnp.swapaxes(kept.reshape(12 * rank, groups, share), 0, 1)
    parts = jnp.pad(parts, ((0, 0), (0, 0), (0, lanes - share)))
    parts = lax.all_to_all(parts, EXPERT, split_axis=0, concat_axis=0, tiled=True)
    ffn_part = ffn_part.astype(bf16).reshape(groups, rank, -1, lanes)
    ffn_part = jnp.swapaxes(ffn_part, 1, 2).reshape(groups, -1, lanes)
    (grad_tokens,) = last_rows(
        scalars,
        grads,
        glow,
        query_key_value_weight,
        weight_other,
        downs,
        x,
        attention_norm_gain,
        dh,
    )
    parts = exchange_all(jnp.concatenate([parts, ffn_part], axis=1), DP)
    output = (hidden_rows + sum(part.astype(f32) for part in [y_a, y_e, *outs])).astype(bf16)
    downs_sum, ups_sum, router_sum, ffn_sum = adapter_sums(
        scalars, parts, adapter_total, rank, share, hidden // (2 * groups)
    )
    return (
        output[None],
        grad_tokens[None],
        jnp.swapaxes(downs_sum, 2, 3),
        ups_sum,
        router_sum[:, :, :wide],
        ffn_sum,
    )


def solution(mesh):
    in_specs = (
        P((DP, EXPERT), FSDP, None),
        P(),
        P(),
        P(None, FSDP, None),
        P(FSDP, None),
        P(),
        P(EXPERT, None, None),
        P(EXPERT, None, None),
        P(),
        P(),
        P(),
        P(),
        P((DP, EXPERT)),
        P((DP, EXPERT), None),
        P((DP, EXPERT), FSDP, None),
        P((DP, EXPERT), FSDP, None),
    )
    out_specs = (
        P((DP, EXPERT), FSDP, None),
        P((DP, EXPERT), FSDP, None),
        P(None, None, (FSDP, EXPERT), None),
        P(None, None, None, (FSDP, EXPERT)),
        P(None, None, (FSDP, EXPERT)),
        P(None, None, (FSDP, EXPERT)),
    )
    specs = dict(mesh=mesh, in_specs=in_specs, out_specs=out_specs, check_vma=False)
    by_tokens = jax.shard_map(shards_by_tokens, **specs)
    by_slots = jax.shard_map(shards_by_slots, **specs)
    groups, shards = mesh.shape[EXPERT], mesh.shape[DP] * mesh.shape[EXPERT]

    def layer(*arguments):
        tokens, experts = arguments[0], arguments[6].shape[0]
        rows = tokens.shape[0] * tokens.shape[1] // (shards * mesh.shape[FSDP])
        wide = 4 * rows // experts * (experts // groups) >= rows and experts % (2 * groups) == 0
        if groups == 4 and mesh.shape[FSDP] == 2 and tokens.shape[0] == shards and wide:
            return by_tokens(*arguments)
        return by_slots(*arguments)

    return layer
```

```python
import functools
import math

import jax
import jax.numpy as jnp
from jax import lax
from jax.experimental import pallas as pl
from jax.experimental.pallas import tpu as pltpu
from jax.sharding import PartitionSpec as P

DP, FSDP, EXPERT = "dp", "fsdp", "expert"
HEADS = 12
HEAD_DIM = 64


EPSILON = 1e-06
MASKED = -1e30


def shifted(block, axis, distance):
    devices = range(lax.axis_size(axis))
    route = [(i - distance, i) for i in devices if i - distance in devices]
    return lax.ppermute(block, axis, route)


def rms_norm(values, gain_vec):
    return (
        values * lax.rsqrt(jnp.mean(values * values, axis=-1, keepdims=True) + EPSILON) * gain_vec
    )


def block_scores(query_part, key_group, query_place, query_label, key_pos, key_doc, score_scale):
    raw_scores = (
        jnp.einsum("qhd,khd->hqk", query_part, key_group, preferred_element_type=jnp.float32)
        * score_scale
    )
    allowed = (
        (key_pos[None, :] <= query_place[:, None])
        & (key_pos[None, :] >= 0)
        & (key_doc[None, :] == query_label[:, None])
    )
    return jnp.where(allowed[None], raw_scores, MASKED)


def attend_forward(queries, key_rows, value_rows, query_pos, query_doc, key_pos, key_doc):
    row_count = queries.shape[0]
    key_count = key_rows.shape[0]
    group_heads = min(4, HEADS)
    group_count = HEADS // group_heads
    block_rows = min(512, row_count)
    block_count = row_count // block_rows
    group_width = group_heads * HEAD_DIM
    score_scale = 1.0 / math.sqrt(HEAD_DIM)

    def per_group(group_id):
        key_group = lax.dynamic_slice_in_dim(
            key_rows, group_id * group_width, group_width, 1
        ).reshape(key_count, group_heads, HEAD_DIM)
        value_group = lax.dynamic_slice_in_dim(
            value_rows, group_id * group_width, group_width, 1
        ).reshape(key_count, group_heads, HEAD_DIM)

        def per_block(block_id):
            query_part = lax.dynamic_slice(
                queries, (block_id * block_rows, group_id * group_width), (block_rows, group_width)
            ).reshape(block_rows, group_heads, HEAD_DIM)
            scores = block_scores(
                query_part, key_group, query_pos, query_doc, key_pos, key_doc, score_scale
            )
            largest = jnp.max(scores, axis=-1, keepdims=True)
            exp_scores = jnp.exp(scores - largest)
            row_total = jnp.sum(exp_scores, axis=-1, keepdims=True)
            probability = exp_scores / row_total
            log_total = largest[..., 0] + jnp.log(row_total[..., 0])
            mixture = jnp.einsum(
                "hqk,khd->qhd",
                probability.astype(jnp.bfloat16),
                value_group,
                preferred_element_type=jnp.float32,
            )
            return (mixture.reshape(block_rows, group_width), log_total)

        return lax.map(per_block, jnp.arange(block_count, dtype=jnp.int32))

    mixture, log_total = lax.map(per_group, jnp.arange(group_count, dtype=jnp.int32))
    mixture = mixture.transpose(1, 2, 0, 3).reshape(row_count, group_count * group_width)
    return (mixture, log_total)


def attend_backward(
    queries, key_rows, value_rows, grad_mix, log_total, query_pos, query_doc, key_pos, key_doc
):
    row_count = queries.shape[0]
    key_count = key_rows.shape[0]
    group_heads = min(4, HEADS)
    group_count = HEADS // group_heads
    block_rows = min(512, row_count)
    block_count = row_count // block_rows
    group_width = group_heads * HEAD_DIM
    score_scale = 1.0 / math.sqrt(HEAD_DIM)

    def per_group(group_id):
        key_group = lax.dynamic_slice_in_dim(
            key_rows, group_id * group_width, group_width, 1
        ).reshape(key_count, group_heads, HEAD_DIM)
        value_group = lax.dynamic_slice_in_dim(
            value_rows, group_id * group_width, group_width, 1
        ).reshape(key_count, group_heads, HEAD_DIM)
        log_group = lax.dynamic_index_in_dim(log_total, group_id, 0, keepdims=False)

        def per_block(carry, block_id):
            key_acc, value_acc = carry
            query_part = lax.dynamic_slice(
                queries, (block_id * block_rows, group_id * group_width), (block_rows, group_width)
            ).reshape(block_rows, group_heads, HEAD_DIM)
            grad_part = lax.dynamic_slice(
                grad_mix, (block_id * block_rows, group_id * group_width), (block_rows, group_width)
            ).reshape(block_rows, group_heads, HEAD_DIM)
            log_part = lax.dynamic_index_in_dim(log_group, block_id, 0, keepdims=False)
            scores = block_scores(
                query_part, key_group, query_pos, query_doc, key_pos, key_doc, score_scale
            )
            probability = jnp.exp(scores - log_part[:, :, None])
            grad_prob = jnp.einsum(
                "qhd,khd->hqk", grad_part, value_group, preferred_element_type=jnp.float32
            )
            inner = jnp.sum(probability * grad_prob, axis=-1, keepdims=True)
            grad_score = (probability * (grad_prob - inner)).astype(jnp.bfloat16)
            grad_query = (
                jnp.einsum(
                    "hqk,khd->qhd", grad_score, key_group, preferred_element_type=jnp.float32
                )
                * score_scale
            )
            key_acc = (
                key_acc
                + jnp.einsum(
                    "hqk,qhd->khd", grad_score, query_part, preferred_element_type=jnp.float32
                )
                * score_scale
            )
            value_acc = value_acc + jnp.einsum(
                "hqk,qhd->khd",
                probability.astype(jnp.bfloat16),
                grad_part,
                preferred_element_type=jnp.float32,
            )
            return ((key_acc, value_acc), grad_query.reshape(block_rows, group_width))

        empty = jnp.zeros((key_count, group_heads, HEAD_DIM), jnp.float32)
        (key_acc, value_acc), grad_query = lax.scan(
            per_block, (empty, empty), jnp.arange(block_count, dtype=jnp.int32)
        )
        return (
            grad_query,
            key_acc.reshape(key_count, group_width),
            value_acc.reshape(key_count, group_width),
        )

    grad_query, grad_key, grad_value = lax.map(per_group, jnp.arange(group_count, dtype=jnp.int32))
    grad_query = grad_query.transpose(1, 2, 0, 3).reshape(row_count, group_count * group_width)
    grad_key = grad_key.transpose(1, 0, 2).reshape(key_count, group_count * group_width)
    grad_value = grad_value.transpose(1, 0, 2).reshape(key_count, group_count * group_width)
    return (grad_query, grad_key, grad_value)


def expert_preact(token_part, adapt_part, expert_input_weight, flattened_up_factors):
    return jnp.einsum(
        "sxnd,xdf->sxnf", token_part, expert_input_weight, preferred_element_type=jnp.float32
    ) + jnp.einsum(
        "sxnr,rf->sxnf", adapt_part, flattened_up_factors, preferred_element_type=jnp.float32
    )


def shards_by_slots(
    tokens,
    attention_norm_gain,
    expert_norm_gain,
    query_key_value_weight,
    attention_output_weight,
    router_weight,
    expert_input_weight,
    expert_output_weight,
    adapter_down_factors,
    adapter_up_attention,
    adapter_up_routing,
    adapter_up_expert,
    sequence_adapter,
    position_document,
    routes,
    output_gradient,
):
    row_count = tokens.shape[1]
    width = tokens.shape[2]
    local_experts = expert_input_weight.shape[0]
    expert_groups = lax.axis_size(EXPERT)
    expert_count = local_experts * expert_groups
    capacity = 4 * row_count // expert_count
    adapter_total = adapter_down_factors.shape[1]
    adapter_rank_width = adapter_down_factors.shape[3]
    expert_hidden_width = expert_input_weight.shape[2]
    adapter_choice = sequence_adapter[0]
    half_index = lax.axis_index(FSDP)
    doc_row = position_document[0]
    x_in = tokens[0].astype(jnp.float32)
    gain_one = attention_norm_gain.astype(jnp.float32)
    gain_two = expert_norm_gain.astype(jnp.float32)
    normed_f, norm_one_back = jax.vjp(lambda values_in: rms_norm(values_in, gain_one), x_in)
    normed = normed_f.astype(jnp.bfloat16)
    weight_qkv, weight_out = (
        lax.all_gather(query_key_value_weight, FSDP, axis=1, tiled=True),
        lax.all_gather(attention_output_weight, FSDP, axis=0, tiled=True),
    )
    down_factor_list = lax.dynamic_index_in_dim(
        adapter_down_factors, adapter_choice, 1, keepdims=False
    )
    up_factor_list = lax.dynamic_index_in_dim(
        adapter_up_attention, adapter_choice, 1, keepdims=False
    )
    routing_up_factor = lax.dynamic_index_in_dim(
        adapter_up_routing, adapter_choice, 0, keepdims=False
    )
    low_qkv = jnp.einsum(
        "td,pdr->ptr", normed, down_factor_list[:3], preferred_element_type=jnp.float32
    ).astype(jnp.bfloat16)
    qkv = (
        jnp.einsum("td,pde->pte", normed, weight_qkv, preferred_element_type=jnp.float32)
        + jnp.einsum(
            "ptr,pre->pte", low_qkv, up_factor_list[:3], preferred_element_type=jnp.float32
        )
    ).astype(jnp.bfloat16)
    left_kv = shifted(qkv[1:], FSDP, 1)
    key_rows = jnp.concatenate([left_kv[0], qkv[1]], axis=0)
    value_rows = jnp.concatenate([left_kv[1], qkv[2]], axis=0)
    local_pos = jnp.arange(row_count, dtype=jnp.int32)
    query_pos = half_index * row_count + local_pos
    key_pos = jnp.concatenate([query_pos - row_count, query_pos])
    query_doc = lax.dynamic_slice_in_dim(doc_row, half_index * row_count, row_count)
    left_doc = lax.dynamic_slice_in_dim(
        doc_row, jnp.maximum(half_index - 1, 0) * row_count, row_count
    )
    key_doc = jnp.concatenate([left_doc, query_doc])
    mixture_f, log_total = attend_forward(
        qkv[0], key_rows, value_rows, query_pos, query_doc, key_pos, key_doc
    )
    mixture = mixture_f.astype(jnp.bfloat16)
    low_out = jnp.dot(mixture, down_factor_list[3], preferred_element_type=jnp.float32).astype(
        jnp.bfloat16
    )
    branch = jnp.dot(mixture, weight_out, preferred_element_type=jnp.float32) + jnp.dot(
        low_out, up_factor_list[3], preferred_element_type=jnp.float32
    )
    hidden_res = x_in + branch
    normed_two_f, norm_two_back = jax.vjp(
        lambda values_in: rms_norm(values_in, gain_two), hidden_res
    )
    normed_two = normed_two_f.astype(jnp.bfloat16)
    low_router = jnp.dot(
        normed_two, down_factor_list[4], preferred_element_type=jnp.float32
    ).astype(jnp.bfloat16)
    logits = jnp.dot(normed_two, router_weight, preferred_element_type=jnp.float32) + jnp.dot(
        low_router, routing_up_factor, preferred_element_type=jnp.float32
    )
    route_rows = routes[0]
    expert_ids = jnp.arange(expert_count, dtype=jnp.int32)
    choose_hot = (route_rows[:, :, None] == expert_ids[None, None, :]).astype(jnp.float32)
    picked = jnp.sum(logits[:, None, :] * choose_hot, axis=-1)
    gate_probs = jax.nn.softmax(picked, axis=-1)
    low_ffn = jnp.dot(normed_two, down_factor_list[5], preferred_element_type=jnp.float32).astype(
        jnp.bfloat16
    )
    adapter_one = (jnp.arange(adapter_total, dtype=jnp.int32) == adapter_choice).astype(jnp.float32)
    adapter_place = adapter_one.astype(jnp.bfloat16)
    adapter_rows = (adapter_place[None, :, None] * low_ffn[:, None, :]).reshape(
        row_count, adapter_total * adapter_rank_width
    )
    flat_routes = route_rows.reshape(-1)
    route_hot = (flat_routes[:, None] == expert_ids[None, :]).astype(jnp.int32)
    route_rank = jnp.sum((jnp.cumsum(route_hot, axis=0) - route_hot) * route_hot, axis=1)
    slot_index = flat_routes * capacity + route_rank
    assign_count = 2 * row_count
    slot_owner = (
        jnp.full((expert_count * capacity,), assign_count, jnp.int32)
        .at[slot_index]
        .set(jnp.arange(assign_count, dtype=jnp.int32))
    )
    owner_token = slot_owner // 2
    pad_rows = jnp.zeros((1, width), jnp.bfloat16)
    send_tokens = jnp.concatenate([normed_two, pad_rows], axis=0)[owner_token].reshape(
        expert_groups, local_experts, capacity, width
    )
    send_adapt = jnp.concatenate(
        [adapter_rows, jnp.zeros((1, adapter_total * adapter_rank_width), jnp.bfloat16)], axis=0
    )[owner_token].reshape(
        expert_groups, local_experts, capacity, adapter_total * adapter_rank_width
    )
    flattened_up_factors = adapter_up_expert.reshape(
        adapter_total * adapter_rank_width, expert_hidden_width
    )
    token_part = lax.all_to_all(send_tokens, EXPERT, split_axis=0, concat_axis=0, tiled=True)
    adapt_part = lax.all_to_all(send_adapt, EXPERT, split_axis=0, concat_axis=0, tiled=True)
    preact = expert_preact(token_part, adapt_part, expert_input_weight, flattened_up_factors)
    activation = jax.nn.gelu(preact).astype(jnp.bfloat16)
    result = jnp.einsum(
        "sxnf,xfd->sxnd", activation, expert_output_weight, preferred_element_type=jnp.float32
    ).astype(jnp.bfloat16)
    returned = lax.all_to_all(result, EXPERT, split_axis=0, concat_axis=0, tiled=True)
    expert_rows = (
        returned.reshape(expert_count * capacity, width)[slot_index]
        .reshape(row_count, 2, width)
        .astype(jnp.float32)
    )
    expert_sum = jnp.sum(gate_probs[:, :, None] * expert_rows, axis=1)
    output = (hidden_res + expert_sum).astype(jnp.bfloat16)
    grad_out = output_gradient[0].astype(jnp.float32)
    grad_gate = jnp.sum(grad_out[:, None, :] * expert_rows, axis=-1)
    grad_pick = gate_probs * (grad_gate - jnp.sum(gate_probs * grad_gate, axis=-1, keepdims=True))
    grad_logits = jnp.sum(grad_pick[:, :, None] * choose_hot, axis=1)
    grad_assign = (
        (gate_probs[:, :, None] * grad_out[:, None, :])
        .astype(jnp.bfloat16)
        .reshape(assign_count, width)
    )
    send_grad = jnp.concatenate([grad_assign, pad_rows], axis=0)[slot_owner].reshape(
        expert_groups, local_experts, capacity, width
    )
    grad_recv = lax.all_to_all(send_grad, EXPERT, split_axis=0, concat_axis=0, tiled=True)
    grad_act = jnp.einsum(
        "sxnd,xfd->sxnf", grad_recv, expert_output_weight, preferred_element_type=jnp.float32
    )
    grad_pre = jax.vjp(jax.nn.gelu, preact)[1](grad_act)[0].astype(jnp.bfloat16)
    grad_tok_expert = jnp.einsum(
        "sxnf,xdf->sxnd", grad_pre, expert_input_weight, preferred_element_type=jnp.float32
    ).astype(jnp.bfloat16)
    grad_adapt_expert = jnp.einsum(
        "sxnf,rf->sxnr", grad_pre, flattened_up_factors, preferred_element_type=jnp.float32
    ).astype(jnp.bfloat16)
    grad_up_ffn = jnp.einsum(
        "sxnr,sxnf->rf", adapt_part, grad_pre, preferred_element_type=jnp.float32
    ).reshape(adapter_total, adapter_rank_width, expert_hidden_width)
    grad_back_tok, grad_back_adapt = (
        lax.all_to_all(grad_tok_expert, EXPERT, split_axis=0, concat_axis=0, tiled=True),
        lax.all_to_all(grad_adapt_expert, EXPERT, split_axis=0, concat_axis=0, tiled=True),
    )
    grad_normed_two = jnp.sum(
        grad_back_tok.reshape(expert_count * capacity, width)[slot_index]
        .astype(jnp.float32)
        .reshape(row_count, 2, width),
        axis=1,
    )
    adapt_back = grad_back_adapt.reshape(
        expert_count * capacity, adapter_total, adapter_rank_width
    )[slot_index].astype(jnp.float32)
    grad_low_ffn = jnp.sum(
        jnp.sum(adapt_back * adapter_one[None, :, None], axis=1).reshape(
            row_count, 2, adapter_rank_width
        ),
        axis=1,
    )
    grad_low_router = jnp.einsum(
        "te,re->tr", grad_logits, routing_up_factor, preferred_element_type=jnp.float32
    )
    grad_up_router = jnp.einsum(
        "tr,te->re", low_router, grad_logits, preferred_element_type=jnp.float32
    )
    grad_down_router = jnp.einsum(
        "td,tr->dr", normed_two, grad_low_router, preferred_element_type=jnp.float32
    )
    grad_down_ffn = jnp.einsum(
        "td,tr->dr", normed_two, grad_low_ffn, preferred_element_type=jnp.float32
    )
    grad_normed_two = grad_normed_two + jnp.einsum(
        "tr,dr->td", grad_low_ffn, down_factor_list[5], preferred_element_type=jnp.float32
    )
    grad_normed_two = grad_normed_two + jnp.einsum(
        "te,de->td", grad_logits, router_weight, preferred_element_type=jnp.float32
    )
    grad_normed_two = grad_normed_two + jnp.einsum(
        "tr,dr->td", grad_low_router, down_factor_list[4], preferred_element_type=jnp.float32
    )
    grad_hidden = grad_out + norm_two_back(grad_normed_two)[0]
    grad_branch = grad_hidden.astype(jnp.bfloat16)
    weight_qkv_back, weight_out_back = (
        lax.all_gather(query_key_value_weight, FSDP, axis=1, tiled=True),
        lax.all_gather(attention_output_weight, FSDP, axis=0, tiled=True),
    )
    grad_up_out = jnp.einsum("tr,te->re", low_out, grad_branch, preferred_element_type=jnp.float32)
    grad_low_out = jnp.einsum(
        "te,re->tr", grad_branch, up_factor_list[3], preferred_element_type=jnp.float32
    )
    grad_down_out = jnp.einsum(
        "td,tr->dr", mixture, grad_low_out, preferred_element_type=jnp.float32
    )
    grad_mixture = (
        jnp.einsum("te,de->td", grad_branch, weight_out_back, preferred_element_type=jnp.float32)
        + jnp.einsum(
            "tr,dr->td", grad_low_out, down_factor_list[3], preferred_element_type=jnp.float32
        )
    ).astype(jnp.bfloat16)
    grad_query, grad_key, grad_value = attend_backward(
        qkv[0],
        key_rows,
        value_rows,
        grad_mixture,
        log_total,
        query_pos,
        query_doc,
        key_pos,
        key_doc,
    )
    sent_back = shifted(
        jnp.stack([grad_key[:row_count], grad_value[:row_count]]).astype(jnp.bfloat16), FSDP, -1
    ).astype(jnp.float32)
    grad_qkv = jnp.stack(
        [grad_query, grad_key[row_count:] + sent_back[0], grad_value[row_count:] + sent_back[1]]
    ).astype(jnp.bfloat16)
    grad_up_qkv = jnp.einsum("ptr,pte->pre", low_qkv, grad_qkv, preferred_element_type=jnp.float32)
    grad_low_qkv = jnp.einsum(
        "pte,pre->ptr", grad_qkv, up_factor_list[:3], preferred_element_type=jnp.float32
    )
    grad_down_qkv = jnp.einsum(
        "td,ptr->pdr", normed, grad_low_qkv, preferred_element_type=jnp.float32
    )
    grad_normed = jnp.einsum(
        "pte,pde->td", grad_qkv, weight_qkv_back, preferred_element_type=jnp.float32
    ) + jnp.einsum(
        "ptr,pdr->td", grad_low_qkv, down_factor_list[:3], preferred_element_type=jnp.float32
    )
    grad_tokens = (grad_hidden + norm_one_back(grad_normed)[0]).astype(jnp.bfloat16)
    grad_down = jnp.concatenate(
        [grad_down_qkv, grad_down_out[None], grad_down_router[None], grad_down_ffn[None]], axis=0
    )
    grad_down_all = adapter_one[None, :, None, None] * grad_down[:, None]
    grad_up_attn = jnp.concatenate([grad_up_qkv, grad_up_out[None]], axis=0)
    grad_up_attn_all = adapter_one[None, :, None, None] * grad_up_attn[:, None]
    grad_router_all = adapter_one[:, None, None] * grad_up_router[None]
    group_parts = (
        lax.psum_scatter(grad_down_all, (FSDP, EXPERT), scatter_dimension=2, tiled=True),
        lax.psum_scatter(grad_up_attn_all, (FSDP, EXPERT), scatter_dimension=3, tiled=True),
        lax.psum_scatter(grad_router_all, (FSDP, EXPERT), scatter_dimension=2, tiled=True),
        lax.psum_scatter(grad_up_ffn, (FSDP, EXPERT), scatter_dimension=2, tiled=True),
    )
    totals = lax.psum((group_parts[0], group_parts[1], group_parts[2], group_parts[3]), DP)
    return (output[None], grad_tokens[None], totals[0], totals[1], totals[2], totals[3])


def mxu(left, right, left_dim=1, right_dim=0):
    return lax.dot_general(
        left, right, (((left_dim,), (right_dim,)), ((), ())), preferred_element_type=jnp.float32
    )


def normed_rows(values, gain):
    return (
        values * lax.rsqrt(jnp.mean(values * values, axis=-1, keepdims=True) + EPSILON) * gain
    )


def norm_back(values, gain, grad):
    root = lax.rsqrt(jnp.mean(values * values, axis=-1, keepdims=True) + EPSILON)
    inner = grad * gain
    mean = jnp.mean(values * inner, axis=-1, keepdims=True)
    return root * inner - values * (root * root * root * mean)


def gate_rows(x, down, upr, router, routes):
    rank = upr.shape[1]
    low = mxu(down, x, 1, 1)
    low_router = low[:rank].astype(jnp.bfloat16)
    logits = mxu(router, x, 1, 1) + mxu(upr, low_router)
    ids = lax.broadcasted_iota(jnp.int32, logits.shape, 0)
    hot = (ids == routes[0:1]) | (ids == routes[1:2])
    top = jnp.max(jnp.where(hot, logits, -jnp.inf), axis=0, keepdims=True)
    ex = jnp.where(hot, jnp.exp(logits - top), 0.0)
    gates = ex / jnp.sum(ex, axis=0, keepdims=True)
    return low_router, low[rank:].astype(jnp.bfloat16), gates, hot, ids


def dense_call(kernel, scalars, grid, inputs, outputs, scratch, flops):
    return pl.pallas_call(
        kernel,
        grid_spec=pltpu.PrefetchScalarGridSpec(
            num_scalar_prefetch=1,
            grid=grid,
            in_specs=[pl.BlockSpec(block, index) for _, block, index in inputs],
            out_specs=[pl.BlockSpec(block, index) for _, _, block, index in outputs],
            scratch_shapes=[pltpu.VMEM(shape, kind) for shape, kind in scratch],
        ),
        out_shape=[jax.ShapeDtypeStruct(shape, kind) for shape, kind, _, _ in outputs],
        compiler_params=pltpu.CompilerParams(vmem_limit_bytes=56000 * 1024),
        cost_estimate=pl.CostEstimate(flops=flops, bytes_accessed=flops // 256, transcendentals=0),
    )(scalars, *(array for array, _, _ in inputs))


def fill_joined(half, mine, other, weight_s):
    tall = mine.shape[0]
    weight_s[pl.ds(pl.multiple_of(half * tall, tall), tall), :] = mine
    weight_s[pl.ds(pl.multiple_of((1 - half) * tall, tall), tall), :] = other


def first_kernel(sc, x_ref, left_ref, gain_ref, mine_ref, other_ref, down_ref, up_ref, *outs):
    normed_ref, low_ref, q_ref, kv_ref, xn_s, weight_s = outs
    step = pl.program_id(0)
    rows, width = x_ref.shape
    rank = up_ref.shape[2]
    bf16 = jnp.bfloat16

    @pl.when(step == 0)
    def _():
        gain = gain_ref[...].astype(jnp.float32)
        factors = down_ref[:, 0].reshape(down_ref.shape[0] * rank, width)
        for at, ref in ((0, left_ref), (rows, x_ref)):
            xn = normed_rows(ref[...].astype(jnp.float32), gain).astype(bf16)
            xn_s[at : at + rows, :width] = xn
            low = mxu(xn, factors, 1, 1).astype(bf16)
            blank = jnp.zeros((rows, xn_s.shape[1] - width - low.shape[1]), bf16)
            xn_s[at : at + rows, width:] = jnp.concatenate([low, blank], axis=1)
            if at > 0:
                normed_ref[...] = xn
                low = low.astype(jnp.float32).T.astype(bf16)
                for p in range(low_ref.shape[0]):
                    low_ref[p] = low[p * rank : (p + 1) * rank]
        weight_s[width:, :] = jnp.zeros((weight_s.shape[0] - width, width), bf16)

    fill_joined(sc[0], mine_ref[0], other_ref[0], weight_s)
    for p in range(low_ref.shape[0]):
        at = width + p * rank
        factor = up_ref[0, 0]
        weight_s[at : at + rank, :] = jnp.where(step == p, factor, jnp.zeros_like(factor))

    @pl.when(step == 0)
    def _():
        q_ref[...] = mxu(xn_s[rows:, :], weight_s[...]).astype(bf16)

    @pl.when(step > 0)
    def _():
        kv_ref[0] = mxu(xn_s[...], weight_s[...]).astype(bf16)


def project_in(scalars, x, left, gain, mine, other, downs, ups):
    rows, width = x.shape
    rank = downs.shape[2]
    bf16 = jnp.bfloat16
    whole = lambda i, s: (0, 0)
    lead = lambda i, s: (i, 0, 0)
    factor = lambda i, s: (i, s[1], 0, 0)
    return dense_call(
        first_kernel,
        scalars,
        (3,),
        [
            (x, (rows, width), whole),
            (left, (rows, width), whole),
            (gain.reshape(1, width), (1, width), whole),
            (mine, (1, width // 2, width), lead),
            (other, (1, width // 2, width), lead),
            (downs, (3, 1, rank, width), lambda i, s: (0, s[1], 0, 0)),
            (ups, (1, 1, rank, width), factor),
        ],
        [
            ((rows, width), bf16, (rows, width), whole),
            ((3, rank, rows), bf16, (3, rank, rows), lambda i, s: (0, 0, 0)),
            ((rows, width), bf16, (rows, width), whole),
            (
                (2, 2 * rows, width),
                bf16,
                (1, 2 * rows, width),
                lambda i, s: (jnp.maximum(i - 1, 0), 0, 0),
            ),
        ],
        [((2 * rows, width + 128), bf16), ((width + 128, width), bf16)],
        10 * rows * width * width,
    )


def middle_kernel(sc, x_ref, att_ref, mine_ref, other_ref, down_ref, up_ref, gain_ref, *outs):
    low_ref, hidden_ref, normed_ref, weight_s = outs

    @pl.when(pl.program_id(0) == 0)
    def _():
        fill_joined(sc[0], mine_ref[...], other_ref[...], weight_s)

    att = att_ref[...]
    low = mxu(att, down_ref[0, 0], 1, 1)
    low_ref[...] = low.T.astype(jnp.bfloat16)
    low = low.astype(jnp.bfloat16)
    hidden = x_ref[...].astype(jnp.float32) + (
        mxu(att, weight_s[...]) + mxu(low, up_ref[0, 0])
    )
    hidden_ref[...] = hidden
    normed_ref[...] = normed_rows(hidden, gain_ref[...].astype(jnp.float32)).astype(jnp.bfloat16)


def project_out(scalars, x, att, mine, other, downs, ups, gain):
    rows, width = x.shape
    rank = downs.shape[2]
    tall = rows // 2
    whole = lambda i, s: (0, 0)
    block = lambda i, s: (i, 0)
    return dense_call(
        middle_kernel,
        scalars,
        (2,),
        [
            (x, (tall, width), block),
            (att, (tall, width), block),
            (mine, (width // 2, width), whole),
            (other, (width // 2, width), whole),
            (downs, (1, 1, rank, width), lambda i, s: (3, s[1], 0, 0)),
            (ups, (1, 1, rank, width), lambda i, s: (3, s[1], 0, 0)),
            (gain.reshape(1, width), (1, width), whole),
        ],
        [
            ((rank, rows), jnp.bfloat16, (rank, tall), lambda i, s: (0, i)),
            ((rows, width), jnp.float32, (tall, width), block),
            ((rows, width), jnp.bfloat16, (tall, width), block),
        ],
        [((width, width), jnp.bfloat16)],
        2 * rows * width * width,
    )


def after_kernel(share, wide, sc, *refs):
    dx_refs, extra_refs = refs[:5], refs[5:10]
    (
        go_ref,
        hidden_ref,
        normed_ref,
        att_ref,
        low_ref,
        routes_ref,
        down45_ref,
        router_ref,
        upr_ref,
        down3_ref,
        up3_ref,
        mine_ref,
        other_ref,
        gain_ref,
        datt_ref,
        dh_ref,
        rows_ref,
        weight_s,
    ) = refs[10:]
    bf16, f32 = jnp.bfloat16, jnp.float32
    rank = down3_ref.shape[2]

    @pl.when(pl.program_id(0) == 0)
    def _():
        rows_ref[...] = jnp.zeros_like(rows_ref)
        fill_joined(sc[0], mine_ref[...], other_ref[...], weight_s)

    xn = normed_ref[...]
    low_router, _, gates, _, ids = gate_rows(
        xn, down45_ref[0], upr_ref[0], router_ref[...], routes_ref[0]
    )
    extra = sum(ref[...].astype(f32) for ref in extra_refs)
    dgate = 0.0
    for k in range(2):
        value = extra[rank + k : rank + k + 1] + extra[rank + 8 + k : rank + 9 + k]
        dgate = dgate + jnp.where(ids == routes_ref[0, k : k + 1], value, 0.0)
    dlogits = gates * (dgate - jnp.sum(gates * dgate, axis=0, keepdims=True))
    dlogits = dlogits.astype(bf16)
    dlr = mxu(upr_ref[0], dlogits, 0, 0).astype(bf16)
    dlf = extra[:rank].astype(bf16)
    dxn = sum(ref[...].astype(f32) for ref in dx_refs)
    dxn = dxn + mxu(dlr, down45_ref[0, :rank], 0, 0) + mxu(dlf, down45_ref[0, rank:], 0, 0)
    dxn = dxn + mxu(dlogits, router_ref[...], 0, 0)
    dh = go_ref[...].astype(f32) + norm_back(hidden_ref[...], gain_ref[...].astype(f32), dxn)
    dh_ref[...] = dh
    gb = dh.astype(bf16)
    att = att_ref[...]
    dlo = mxu(up3_ref[0, 0], gb, 1, 1).astype(bf16)
    datt_ref[...] = (mxu(gb, weight_s[...], 1, 1) + mxu(dlo, down3_ref[0, 0], 0, 0)).astype(bf16)
    router = mxu(low_router, dlogits, 1, 1).astype(bf16)
    choices, width = router_ref.shape
    column = lax.broadcasted_iota(jnp.int32, (choices, width), 0)
    lane = lax.broadcasted_iota(jnp.int32, (choices, width), 1)
    spot = lane == (column // wide) * share + column % wide
    rows_ref[0] += mxu(dlo, att)
    rows_ref[1] += mxu(dlr, xn)
    rows_ref[2] += mxu(dlf, xn)
    rows_ref[3] += mxu(low_ref[...], gb)
    rows_ref[4] += mxu(router, spot.astype(f32).astype(bf16))


def after_experts(
    scalars, dxs, go, hidden, normed, att, low, routes, down_t, router_t, upr_t, downs, ups, mine,
    other, gain, share, wide
):
    rows, width = hidden.shape
    rank = downs.shape[2]
    tall = rows // 2
    choices = router_t.shape[0]
    extra = dxs[0].shape[0] - rows
    whole = lambda i, s: (0, 0)
    block = lambda i, s: (i, 0)
    adapter = lambda i, s: (s[1], 0, 0)
    return dense_call(
        functools.partial(after_kernel, share, wide),
        scalars,
        (2,),
        [(dx, (tall, width), block) for dx in dxs]
        + [(dx, (extra, tall), lambda i, s: (rows // extra, i)) for dx in dxs]
        + [(array, (tall, width), block) for array in (go, hidden, normed, att)]
        + [
            (low, (rank, tall), lambda i, s: (0, i)),
            (routes, (1, 2, tall), lambda i, s: (0, 0, i)),
            (down_t, (1, 2 * rank, width), adapter),
            (router_t, (choices, width), whole),
            (upr_t, (1, choices, rank), adapter),
            (downs, (1, 1, rank, width), lambda i, s: (3, s[1], 0, 0)),
            (ups, (1, 1, rank, width), lambda i, s: (3, s[1], 0, 0)),
            (mine, (width // 2, width), whole),
            (other, (width // 2, width), whole),
            (gain.reshape(1, width), (1, width), whole),
        ],
        [
            ((rows, width), jnp.bfloat16, (tall, width), block),
            ((rows, width), jnp.float32, (tall, width), block),
            ((5, rank, width), jnp.float32, (5, rank, width), lambda i, s: (0, 0, 0)),
        ],
        [((width, width), jnp.bfloat16)],
        3 * rows * width * width,
    )


def factors_kernel(sc, dq_ref, own_ref, back_ref, low_ref, up_ref, normed_ref, early_ref, *outs):
    grad_ref, glow_ref, kept_ref, given_ref = outs
    p = pl.program_id(0)
    bf16 = jnp.bfloat16
    summed = (own_ref[0] + back_ref[0].astype(jnp.float32)).astype(bf16)
    grad = jnp.where(p == 0, dq_ref[...], summed)
    grad_ref[0] = grad
    glow = mxu(up_ref[0, 0], grad, 1, 1).astype(bf16)
    glow_ref[0] = glow
    rank, width = glow.shape[0], grad.shape[1]
    half = sc[0]

    def put(at, value):
        low, high = value[:, : width // 2], value[:, width // 2 :]
        at = pl.ds(pl.multiple_of(at * rank, rank), rank)
        kept_ref[at, :] = jnp.where(half == 0, low, high)
        given_ref[at, :] = jnp.where(half == 0, high, low).astype(bf16)

    put(p, mxu(glow, normed_ref[...]))
    put(6 + p, mxu(low_ref[0], grad))

    @pl.when(p == 0)
    def _():
        for i, at in enumerate((3, 4, 5, 9, 10)):
            put(at, early_ref[i])
        put(11, jnp.full((rank, width), 0.5, jnp.float32) * sc[1].astype(jnp.float32))


def factor_grads(scalars, dq, own, back, low, ups, normed, early):
    rows, width = dq.shape
    rank = ups.shape[2]
    total = 12 * rank
    whole = lambda i, s: (0, 0)
    prior = lambda i, s: (jnp.maximum(i - 1, 0), 0, 0)
    lead = lambda i, s: (i, 0, 0)
    return dense_call(
        factors_kernel,
        scalars,
        (3,),
        [
            (dq, (rows, width), whole),
            (own, (1, rows, width), prior),
            (back, (1, rows, width), prior),
            (low, (1, rank, rows), lead),
            (ups, (1, 1, rank, width), lambda i, s: (i, s[1], 0, 0)),
            (normed, (rows, width), whole),
            (early, (5, rank, width), lambda i, s: (0, 0, 0)),
        ],
        [
            ((3, rows, width), jnp.bfloat16, (1, rows, width), lead),
            ((3, rank, rows), jnp.bfloat16, (1, rank, rows), lead),
            ((total, width // 2), jnp.float32, (total, width // 2), whole),
            ((total, width // 2), jnp.bfloat16, (total, width // 2), whole),
        ],
        [],
        rows * width * width // 4,
    )


def last_kernel(sc, grad_ref, glow_ref, mine_ref, other_ref, down_ref, x_ref, gain_ref, *refs):
    dh_ref, grad_x_ref, acc, weight_s = refs
    p = pl.program_id(0)
    fill_joined(sc[0], mine_ref[0], other_ref[0], weight_s)
    term = mxu(grad_ref[0], weight_s[...], 1, 1) + mxu(glow_ref[0], down_ref[0, 0], 0, 0)
    acc[...] = jnp.where(p == 0, term, acc[...] + term)

    @pl.when(p == pl.num_programs(0) - 1)
    def _():
        back = norm_back(
            x_ref[...].astype(jnp.float32), gain_ref[...].astype(jnp.float32), acc[...]
        )
        grad_x_ref[...] = (dh_ref[...] + back).astype(grad_x_ref.dtype)


def last_rows(scalars, grads, glow, mine, other, downs, x, gain, dh):
    rows, width = x.shape
    rank = downs.shape[2]
    whole = lambda i, s: (0, 0)
    lead = lambda i, s: (i, 0, 0)
    return dense_call(
        last_kernel,
        scalars,
        (3,),
        [
            (grads, (1, rows, width), lead),
            (glow, (1, rank, rows), lead),
            (mine, (1, width // 2, width), lead),
            (other, (1, width // 2, width), lead),
            (downs, (1, 1, rank, width), lambda i, s: (i, s[1], 0, 0)),
            (x, (rows, width), whole),
            (gain.reshape(1, width), (1, width), whole),
            (dh, (rows, width), whole),
        ],
        [((rows, width), jnp.bfloat16, (rows, width), whole)],
        [((rows, width), jnp.float32), ((width, width), jnp.bfloat16)],
        6 * rows * width * width,
    )


def sums_kernel(count, share, sc, *refs):
    part_refs = refs[:count]
    down_ref, up_ref, router_ref, ffn_ref, acc = refs[count:]
    rank, wide = ffn_ref.shape[1], part_refs[0].shape[2]
    acc[...] = jnp.zeros_like(acc)
    for part_ref in part_refs:
        for s in range(part_ref.shape[0]):
            part = part_ref[s].astype(jnp.float32)
            label = jnp.max(part[11 * rank : 11 * rank + 8, :share]).astype(jnp.int32)
            acc[label] += part
    for a in range(acc.shape[0]):
        rows = acc[a]
        for i in range(6):
            down_ref[i, a] = rows[i * rank : (i + 1) * rank, :share]
        for i in range(4):
            up_ref[i, a] = rows[(6 + i) * rank : (7 + i) * rank, :share]
        router_ref[a] = rows[10 * rank : 11 * rank].T[: router_ref.shape[1]]
        for i in range(ffn_ref.shape[2] // wide):
            ffn_ref[a, :, i * wide : (i + 1) * wide] = rows[(12 + i) * rank : (13 + i) * rank]


def adapter_sums(scalars, parts, choices, rank, share, narrow, wide):
    f32 = jnp.float32
    outs = [
        (6, choices, rank, share),
        (4, choices, rank, share),
        (choices, narrow, rank),
        (choices, rank, wide),
    ]
    fixed = lambda shape: (shape, lambda i, s: (0,) * len(shape))
    return dense_call(
        functools.partial(sums_kernel, len(parts), share),
        scalars,
        (1,),
        [(part, *fixed(part.shape)) for part in parts],
        [(shape, f32, *fixed(shape)) for shape in outs],
        [((choices, *parts[0].shape[1:]), f32)],
        10**6,
    )


def window_bias(bias, kdoc_ref, qdoc_ref, block):
    keys, cols = bias.shape[1:]
    kpos = lax.broadcasted_iota(jnp.int32, (keys, cols), 0) - (keys - cols)
    qpos = lax.broadcasted_iota(jnp.int32, (keys, cols), 1)
    key_doc = kdoc_ref[pl.ds(pl.multiple_of(block * cols, cols), keys), :]
    bias[block] = jnp.where((kpos <= qpos) & (key_doc == qdoc_ref[...]), 0.0, MASKED)


def head_probability(queries, key_parts, bias, block, first):
    tall = queries.shape[0]
    scores = [
        mxu(part, queries, 1, 1) + bias[block, (first + i) * tall : (first + i + 1) * tall, :]
        for i, part in enumerate(key_parts)
    ]
    top = functools.reduce(jnp.maximum, [jnp.max(s, axis=0, keepdims=True) for s in scores])
    parts = [jnp.exp(s - top) for s in scores]
    total = sum(jnp.sum(p, axis=0, keepdims=True) for p in parts)
    share = 1.0 / total
    return [p * share for p in parts]


def attend_kernel(reach, kdoc_ref, qdoc_ref, q_ref, *refs):
    key_refs, value_refs = refs[:3], refs[3:6]
    out_ref, bias = refs[6:]
    block = pl.program_id(1)

    @pl.when(pl.program_id(0) == 0)
    def _():
        window_bias(bias, kdoc_ref, qdoc_ref, block)

    def run(first):
        keys, values = ([ref[0] for ref in part[first:]] for part in (key_refs, value_refs))
        mixed = []
        for head in range(q_ref.shape[1] // HEAD_DIM):
            cols = slice(head * HEAD_DIM, (head + 1) * HEAD_DIM)
            queries = q_ref[:, cols] * (1.0 / math.sqrt(HEAD_DIM))
            probability = head_probability(
                queries, [key[:, cols] for key in keys], bias, block, first
            )
            mixed.append(
                sum(
                    mxu(value[:, cols], p.astype(jnp.bfloat16), 0, 0)
                    for value, p in zip(values, probability)
                )
            )
        out_ref[...] = jnp.concatenate(mixed, axis=0).T.astype(out_ref.dtype)

    for first in range(3):
        pl.when(reach[block] == first)(functools.partial(run, first))


def attend_back_kernel(reach, kdoc_ref, qdoc_ref, q_ref, *refs):
    key_refs, value_refs = refs[:3], refs[3:6]
    grad_ref, dq_ref, own_ref, left_ref, bias, acc = refs[6:]
    block = pl.program_id(1)
    scale = 1.0 / math.sqrt(HEAD_DIM)

    @pl.when(pl.program_id(0) == 0)
    def _():
        window_bias(bias, kdoc_ref, qdoc_ref, block)

    @pl.when(block == 0)
    def _():
        acc[...] = jnp.zeros_like(acc)

    def run(first):
        keys, values = ([ref[0] for ref in part[first:]] for part in (key_refs, value_refs))
        grad_queries = []
        for head in range(q_ref.shape[1] // HEAD_DIM):
            cols = slice(head * HEAD_DIM, (head + 1) * HEAD_DIM)
            queries = q_ref[:, cols] * scale
            grad = grad_ref[:, cols]
            probability = head_probability(
                queries, [key[:, cols] for key in keys], bias, block, first
            )
            grad_prob = [mxu(value[:, cols], grad, 1, 1) for value in values]
            inner = sum(
                jnp.sum(p * g, axis=0, keepdims=True) for p, g in zip(probability, grad_prob)
            )
            grad_score = [
                (p * (g - inner)).astype(jnp.bfloat16) for p, g in zip(probability, grad_prob)
            ]
            grad_queries.append(
                sum(mxu(key[:, cols], g, 0, 0) for key, g in zip(keys, grad_score)) * scale
            )
            for i, (p, g) in enumerate(zip(probability, grad_score)):
                acc[0, block + first + i, :, cols] += mxu(g, queries)
                acc[1, block + first + i, :, cols] += mxu(p.astype(jnp.bfloat16), grad)
        dq_ref[...] = jnp.concatenate(grad_queries, axis=0).T.astype(dq_ref.dtype)

    for first in range(3):
        pl.when(reach[block] == first)(functools.partial(run, first))

    @pl.when(block == pl.num_programs(1) - 1)
    def _():
        tall = q_ref.shape[0]
        for i in range(2):
            rows = slice(i * tall, (i + 1) * tall)
            for kind in range(2):
                left_ref[kind, rows, :] = acc[kind, i].astype(left_ref.dtype)
                own_ref[kind, rows, :] = acc[kind, 2 + i].astype(own_ref.dtype)


def attention_call(kernel, queries, keys_values, grads, key_doc, query_doc, outs, scratch, flops):
    rows, width = queries.shape
    lanes = 2 * HEAD_DIM
    tall = rows // 2
    starts = jnp.arange(2, dtype=jnp.int32) * tall
    reach = sum(
        (key_doc[starts + (i + 1) * tall - 1] != query_doc[starts]).astype(jnp.int32)
        for i in range(2)
    )

    sources = [
        pl.BlockSpec((1, tall, lanes), lambda g, b, s, p=p, i=i: (p, b + i, g))
        for p in range(2)
        for i in range(3)
    ]

    def stack(kind):
        return {
            "block": pl.BlockSpec((tall, lanes), lambda g, b, s: (b, g)),
            "pair": pl.BlockSpec((2, rows, lanes), lambda g, b, s: (0, 0, g)),
        }[kind]

    return pl.pallas_call(
        kernel,
        grid_spec=pltpu.PrefetchScalarGridSpec(
            num_scalar_prefetch=1,
            grid=(width // lanes, 2),
            in_specs=[
                pl.BlockSpec((2 * rows, 1), lambda g, b, s: (0, 0)),
                pl.BlockSpec((1, tall), lambda g, b, s: (0, b)),
                stack("block"),
                *sources,
            ]
            + [stack("block")] * len(grads),
            out_specs=[stack(kind) for kind, _ in outs],
            scratch_shapes=[pltpu.VMEM((2, 3 * tall, tall), jnp.float32)]
            + [pltpu.VMEM((2, 4, tall, lanes), jnp.float32)] * scratch,
        ),
        out_shape=[
            jax.ShapeDtypeStruct((rows, width) if kind == "block" else (2, rows, width), dtype)
            for kind, dtype in outs
        ],
        compiler_params=pltpu.CompilerParams(vmem_limit_bytes=56000 * 1024),
        cost_estimate=pl.CostEstimate(
            flops=flops * rows * rows * width,
            bytes_accessed=12 * rows * width,
            transcendentals=HEADS * rows * rows,
        ),
        name="ab2" if scratch else "at",
    )(
        reach,
        key_doc.reshape(-1, 1),
        query_doc.reshape(1, -1),
        queries,
        *([keys_values] * 6),
        *grads,
    )


def gelu_both(u):
    c = math.sqrt(2.0 / math.pi)
    sq = u * u
    t = jnp.tanh(u * (c + (c * 0.044715) * sq))
    half = 0.5 + 0.5 * t
    slope = half + (0.5 * u) * (1.0 - t * t) * (c + (3.0 * c * 0.044715) * sq)
    return u * half, slope


def expert_kernel(turn, pieces, capacity, rank, *refs):
    scalars = refs[0]
    x_refs, g_refs = refs[1 : 1 + pieces], refs[1 + pieces : 1 + 2 * pieces]
    (
        route_ref,
        down_ref,
        upr_ref,
        uf_ref,
        router_ref,
        w1_ref,
        w2_ref,
        _,
        y_ref,
        dx_ref,
        gff_ref,
        x_s,
        g_s,
        xe,
        goe,
        dye,
        lfe,
        yacc,
        dxacc,
        dleacc,
        onehot_s,
        lft_s,
        gate_s,
        rank_s,
        ysum,
        dxsum,
        ext_s,
    ) = refs[1 + 2 * pieces :]
    e = pl.program_id(0)
    t = pl.program_id(1)
    last_t = pl.num_programs(1) - 1
    last_e = pl.num_programs(0) - 1
    rows, width = x_refs[0].shape
    tile = w1_ref.shape[2]
    ident = scalars[5 * turn] + e
    bf16, f32 = jnp.bfloat16, jnp.float32

    @pl.when((e == 0) & (t == 0))
    def _():
        ysum[...] = jnp.zeros_like(ysum)
        dxsum[...] = jnp.zeros_like(dxsum)
        ext_s[...] = jnp.zeros_like(ext_s)
        gff_ref[...] = jnp.zeros_like(gff_ref)
        x = sum(ref[...] for ref in x_refs)
        x_s[...] = x
        g_s[...] = sum(ref[...] for ref in g_refs)
        _, lft_s[...], gate_s[...], hot, _ = gate_rows(
            x, down_ref[0], upr_ref[0], router_ref[...], route_ref[0]
        )
        before = lax.broadcasted_iota(jnp.int32, (rows, rows), 0) < lax.broadcasted_iota(
            jnp.int32, (rows, rows), 1
        )
        ranks = mxu(hot.astype(f32).astype(bf16), before.astype(f32).astype(bf16))
        rank_s[...] = jnp.where(hot, ranks, -1.0)

    def slots():
        row = rank_s[pl.ds(ident, 1), :]
        picks = lax.broadcasted_iota(jnp.int32, (capacity, rows), 0).astype(f32) == row
        gate = gate_s[pl.ds(ident, 1), :]
        return picks, jnp.sum(jnp.where(picks, gate, 0.0), axis=1, keepdims=True)

    @pl.when(t == 0)
    def _():
        picks, gate_slot = slots()
        onehot = picks.astype(f32).astype(bf16)
        onehot_s[...] = onehot
        xe[...] = mxu(onehot, x_s[...]).astype(bf16)
        go = mxu(onehot, g_s[...])
        goe[...] = go.astype(bf16)
        dye[...] = (go * gate_slot).astype(bf16)
        lfe[...] = mxu(onehot, lft_s[...], 1, 1).astype(bf16)
        yacc[...] = jnp.zeros_like(yacc)
        dxacc[...] = jnp.zeros_like(dxacc)
        dleacc[...] = jnp.zeros_like(dleacc)

    off = pl.multiple_of(t * tile, tile)
    pre = mxu(xe[...], w1_ref[0]) + mxu(lfe[...], uf_ref[0])
    act, slope = gelu_both(pre)
    yacc[...] += mxu(act.astype(bf16), w2_ref[0])
    dpre = (mxu(dye[...], w2_ref[0], 1, 1) * slope).astype(bf16)
    dxacc[...] += mxu(dpre, w1_ref[0], 1, 1)
    dleacc[...] += mxu(uf_ref[0], dpre, 1, 1)
    gff_ref[0, :, pl.ds(off, tile)] += mxu(lfe[...], dpre, 0, 0)

    @pl.when(t == last_t)
    def _():
        picks, gate_slot = slots()
        onehot = onehot_s[...]
        y = yacc[...].astype(bf16).astype(f32)
        dgate = jnp.sum(goe[...].astype(f32) * y, axis=1, keepdims=True)
        dgate_row = jnp.sum(jnp.where(picks, dgate, 0.0), axis=0, keepdims=True)
        for k in range(2):
            mine = route_ref[0, k : k + 1] == ident
            ext_s[rank + k : rank + k + 1, :] += jnp.where(mine, dgate_row, 0.0)
        ext_s[0:rank, :] += mxu(dleacc[...].astype(bf16), onehot)
        ysum[...] += mxu(onehot, (y * gate_slot).astype(bf16), 0, 0)
        dxsum[...] += mxu(onehot, dxacc[...].astype(bf16), 0, 0)

    @pl.when((e == last_e) & (t == last_t))
    def _():
        y_ref[...] = ysum[...].astype(bf16)
        dx_ref[:rows, :] = dxsum[...].astype(bf16)
        extra = ext_s[...]
        gates = extra[rank:]
        low = gates - gates.astype(bf16).astype(f32)
        packed = jnp.concatenate([extra, low], axis=0).astype(bf16)
        if width > rows:
            blank = jnp.zeros((packed.shape[0], width - rows), bf16)
            packed = jnp.concatenate([packed, blank], axis=1)
        dx_ref[rows:, :] = packed


def run_experts(
    turn, scalars, local, xs, gs, route_rows, down_t, router_t, upr_t, up_ffn, w1, w2, gff, capacity
):
    pieces = len(xs)
    rows, width = xs[0].shape
    hidden = w1.shape[2]
    expert_count = router_t.shape[0]
    rank = up_ffn.shape[1]
    tile = 1024 if hidden % 1024 == 0 else hidden
    fixed = lambda *shape, **kw: pl.BlockSpec(shape, lambda e, t, sc: (0,) * len(shape), **kw)
    adapter = lambda *shape: pl.BlockSpec((1, *shape), lambda e, t, sc: (sc[5 * turn + 1], 0, 0))
    at_spot = lambda k, *shape: pl.BlockSpec(
        (1, *shape), lambda e, t, sc: (sc[5 * turn + 1 + k], 0, 0)
    )
    in_specs = [fixed(rows, width, pipeline_mode=pl.Buffered(1))] * (2 * pieces) + [
        at_spot(1, 2, rows),
        adapter(2 * rank, width),
        adapter(expert_count, rank),
        pl.BlockSpec((1, rank, tile), lambda e, t, sc: (sc[5 * turn + 1], 0, t)),
        fixed(expert_count, width),
        pl.BlockSpec((1, width, tile), lambda e, t, sc: (e + sc[5 * turn + 4], 0, t)),
        pl.BlockSpec((1, tile, width), lambda e, t, sc: (e + sc[5 * turn + 4], t, 0)),
        pl.BlockSpec(memory_space=pl.ANY),
    ]
    bf16, f32 = jnp.bfloat16, jnp.float32
    scratch = [
        ((rows, width), bf16),
        ((rows, width), bf16),
        ((capacity, width), bf16),
        ((capacity, width), bf16),
        ((capacity, width), bf16),
        ((capacity, rank), bf16),
        ((capacity, width), f32),
        ((capacity, width), f32),
        ((rank, capacity), f32),
        ((capacity, rows), bf16),
        ((rank, rows), bf16),
        ((expert_count, rows), f32),
        ((expert_count, rows), f32),
        ((rows, width), f32),
        ((rows, width), f32),
        ((rank + 8, rows), f32),
    ]
    return pl.pallas_call(
        functools.partial(expert_kernel, turn, pieces, capacity, rank),
        grid_spec=pltpu.PrefetchScalarGridSpec(
            num_scalar_prefetch=1,
            grid=(local, hidden // tile),
            in_specs=in_specs,
            out_specs=[
                fixed(rows, width),
                fixed(rows + rank + 16, width),
                at_spot(2, rank, hidden),
            ],
            scratch_shapes=[pltpu.VMEM(shape, kind) for shape, kind in scratch],
        ),
        out_shape=[
            jax.ShapeDtypeStruct((rows, width), bf16),
            jax.ShapeDtypeStruct((rows + rank + 16, width), bf16),
            jax.ShapeDtypeStruct(gff.shape, f32),
        ],
        input_output_aliases={1 + 2 * pieces + 7: 2},
        compiler_params=pltpu.CompilerParams(vmem_limit_bytes=58 * 1024 * 1024),
        cost_estimate=pl.CostEstimate(
            flops=8 * local * capacity * width * hidden,
            bytes_accessed=4 * local * width * hidden + 8 * rows * width,
            transcendentals=0,
        ),
        name="ex",
    )(
        scalars, *xs, *gs, route_rows, down_t, upr_t, up_ffn, router_t, w1, w2, gff
    )


CROSS = [(0, 1), (1, 0), (2, 3), (3, 2)]
INNER = [(1, 2), (2, 1)]
OUTWARD = [(1, 0), (2, 3)]
INWARD = [(0, 1), (3, 2)]
SKIP = [(1, 3), (2, 0)]
TWICE = [(0, 2), (2, 0), (1, 3), (3, 1)]
MIRROR = [(0, 3), (3, 0), (1, 2), (2, 1)]


def on_line(block, route):
    return lax.ppermute(block, EXPERT, route)


def exchange_all(block, axis):
    count = lax.axis_size(axis)
    return [block] + [
        lax.ppermute(block, axis, [(i, (i + step) % count) for i in range(count)])
        for step in range(1, count)
    ]


def shards_by_tokens(
    tokens,
    attention_norm_gain,
    expert_norm_gain,
    query_key_value_weight,
    attention_output_weight,
    router_weight,
    expert_input_weight,
    expert_output_weight,
    adapter_down_factors,
    adapter_up_attention,
    adapter_up_routing,
    adapter_up_expert,
    sequence_adapter,
    position_document,
    routes,
    output_gradient,
):
    rows, width = tokens.shape[1:]
    local = expert_input_weight.shape[0]
    groups = lax.axis_size(EXPERT)
    choices = local * groups
    capacity = 4 * rows // choices
    adapter_total, rank, hidden = adapter_up_expert.shape
    adapter = sequence_adapter[0]
    half = lax.axis_index(FSDP)
    place = lax.axis_index(EXPERT)
    at_end = (place == 0) | (place == groups - 1)
    bf16, f32 = jnp.bfloat16, jnp.float32
    swap = [(0, 1), (1, 0)]
    x, go = tokens[0], output_gradient[0]
    downs = jnp.swapaxes(adapter_down_factors, 2, 3)
    ups = adapter_up_attention
    down_t = jnp.swapaxes(downs[4:6], 0, 1).reshape(adapter_total, 2 * rank, width)
    upr_t = jnp.swapaxes(adapter_up_routing, 1, 2)
    router_t = router_weight.T
    scalars = jnp.stack([half, adapter]).astype(jnp.int32)

    weight_other = lax.ppermute(query_key_value_weight, FSDP, swap)
    left = lax.ppermute(x, FSDP, [(0, 1)])
    about = jnp.concatenate([routes[0].T, jnp.full((1, rows), adapter, jnp.int32)])
    about = [about, *(on_line(about, route) for route in (CROSS, TWICE, MIRROR))]
    go_across, go_inner = on_line(go, CROSS), on_line(go, INNER)
    normed, low_qkv, queries, keys_values = project_in(
        scalars, x, left, attention_norm_gain, query_key_value_weight, weight_other, downs, ups
    )
    out_other = lax.ppermute(attention_output_weight, FSDP, swap)
    doc_row = position_document[0]
    own_doc = lax.dynamic_slice_in_dim(doc_row, half * rows, rows)
    key_doc = jnp.concatenate([jnp.where(half > 0, doc_row[:rows], -1), own_doc])
    go_far_ends, go_far_inner = on_line(go_inner, OUTWARD), on_line(go_across, INNER)
    (att,) = attention_call(
        attend_kernel, queries, keys_values, [], key_doc, own_doc, [("block", bf16)], 0, 4
    )
    low_out, hidden_rows, normed_two = project_out(
        scalars, x, att, attention_output_weight, out_other, downs, ups, expert_norm_gain
    )

    about = jnp.stack(about)
    route_rows, adapters = about[:, :2], about[:, 2, 0]
    part = local // 2
    steps = jnp.arange(5, dtype=jnp.int32)
    distance = jnp.where(steps < 3, steps + 1, 0)
    distance = jnp.where((distance > 1) & ~at_end, 5 - distance, distance)
    hot = distance[:, None] == jnp.arange(groups, dtype=jnp.int32)[None]
    chosen = jnp.sum(jnp.where(hot, adapters[None], 0), axis=1)
    later = jnp.where(steps == 4, part, 0)
    block = jnp.where(steps == 4, groups, place ^ distance)
    turns = jnp.stack([place * local + later, chosen, distance, block, later], axis=1)
    turns = turns.reshape(-1).astype(jnp.int32)

    def call(turn, xs, gs, gff, count=local):
        return run_experts(
            turn,
            turns,
            count,
            xs,
            gs,
            route_rows,
            down_t,
            router_t,
            upr_t,
            adapter_up_expert,
            expert_input_weight,
            expert_output_weight,
            gff,
            capacity,
        )

    merge = lambda one, two: (one.astype(f32) + two.astype(f32)).astype(bf16)
    gff = jnp.zeros((groups + 1, rank, hidden), f32)
    across, inner = on_line(normed_two, CROSS), on_line(normed_two, INNER)
    y_e, dx_e, gff = call(3, [normed_two], [go], gff, part)
    go_last = on_line(go_far_inner, OUTWARD)
    far_ends, far_inner = on_line(inner, OUTWARD), on_line(across, INNER)
    y_b, dx_b, gff = call(0, [across], [go_across], gff)
    last = on_line(far_inner, OUTWARD)
    back_b = on_line(dx_b, CROSS)
    y_c, dx_c, gff = call(1, [inner, far_ends], [go_inner, go_far_ends], gff)
    part_c = on_line(dx_c, INWARD)
    y_part_c = on_line(y_c, INWARD)
    y_d, dx_d, gff = call(2, [far_inner, last], [go_far_inner, go_last], gff)
    part_d = on_line(dx_d, INWARD)
    back_c = on_line(merge(dx_c, part_c), INNER)
    y_part_d = on_line(y_d, INWARD)
    y_a, dx_a, gff = call(4, [normed_two], [go], gff, local - part)
    merged = merge(dx_d, part_d)
    back_d = on_line(merged, SKIP)
    gff, _ = lax.optimization_barrier((gff, merged))
    halves = gff.reshape(groups + 1, rank, 2, -1)
    halves = [lax.dynamic_index_in_dim(halves, at, 2, keepdims=False) for at in (half, 1 - half)]
    ffn_part = halves[0] + lax.ppermute(halves[1].astype(bf16), FSDP, swap).astype(f32)
    ffn_part = ffn_part.astype(bf16).reshape(groups + 1, rank, groups, -1)
    ffn_part = lax.all_to_all(
        jnp.moveaxis(ffn_part, 2, 0), EXPERT, split_axis=0, concat_axis=0, tiled=True
    )
    ffn_part = ffn_part.astype(f32)
    ffn_part = jnp.sum(ffn_part[:, :groups], axis=0) + ffn_part[:, groups]
    share, wide = width // (2 * groups), choices // (2 * groups)
    datt, dh, early = after_experts(
        scalars,
        [dx_a, dx_e, back_b, back_c, back_d],
        go,
        hidden_rows,
        normed_two,
        att,
        low_out,
        route_rows,
        down_t,
        router_t,
        upr_t,
        downs,
        ups,
        attention_output_weight,
        out_other,
        expert_norm_gain,
        share,
        wide,
    )
    outs, datt = lax.optimization_barrier(((y_b, y_c, y_part_c, y_d, y_part_d), datt))
    outs = outs[0], merge(*outs[1:3]), merge(*outs[3:])
    outs = [on_line(part, route) for part, route in zip(outs, (CROSS, INNER, SKIP))]
    dq, own, left_grads = attention_call(
        attend_back_kernel,
        queries,
        keys_values,
        [datt],
        key_doc,
        own_doc,
        [("block", bf16), ("pair", f32), ("pair", bf16)],
        1,
        10,
    )
    back = lax.ppermute(left_grads, FSDP, [(1, 0)])
    grads, glow, kept, given = factor_grads(
        scalars, dq, own, back, low_qkv, ups, normed, early
    )
    kept = (kept + lax.ppermute(given, FSDP, swap).astype(f32)).astype(bf16)
    lanes = 128
    parts = jnp.swapaxes(kept.reshape(12 * rank, groups, share), 0, 1)
    parts = jnp.pad(parts, ((0, 0), (0, 0), (0, lanes - share)))
    parts = lax.all_to_all(parts, EXPERT, split_axis=0, concat_axis=0, tiled=True)
    ffn_part = ffn_part.astype(bf16).reshape(groups, rank, -1, lanes)
    ffn_part = jnp.swapaxes(ffn_part, 1, 2).reshape(groups, -1, lanes)
    (grad_tokens,) = last_rows(
        scalars,
        grads,
        glow,
        query_key_value_weight,
        weight_other,
        downs,
        x,
        attention_norm_gain,
        dh,
    )
    parts = exchange_all(jnp.concatenate([parts, ffn_part], axis=1), DP)
    output = (hidden_rows + sum(part.astype(f32) for part in [y_a, y_e, *outs])).astype(bf16)
    downs_sum, ups_sum, router_sum, ffn_sum = adapter_sums(
        scalars, parts, adapter_total, rank, share, wide, hidden // (2 * groups)
    )
    return (
        output[None],
        grad_tokens[None],
        jnp.swapaxes(downs_sum, 2, 3),
        ups_sum,
        jnp.swapaxes(router_sum, 1, 2),
        ffn_sum,
    )


def solution(mesh):
    in_specs = (
        P((DP, EXPERT), FSDP, None),
        P(),
        P(),
        P(None, FSDP, None),
        P(FSDP, None),
        P(),
        P(EXPERT, None, None),
        P(EXPERT, None, None),
        P(),
        P(),
        P(),
        P(),
        P((DP, EXPERT)),
        P((DP, EXPERT), None),
        P((DP, EXPERT), FSDP, None),
        P((DP, EXPERT), FSDP, None),
    )
    out_specs = (
        P((DP, EXPERT), FSDP, None),
        P((DP, EXPERT), FSDP, None),
        P(None, None, (FSDP, EXPERT), None),
        P(None, None, None, (FSDP, EXPERT)),
        P(None, None, (FSDP, EXPERT)),
        P(None, None, (FSDP, EXPERT)),
    )
    specs = dict(mesh=mesh, in_specs=in_specs, out_specs=out_specs, check_vma=False)
    by_tokens = jax.shard_map(shards_by_tokens, **specs)
    by_slots = jax.shard_map(shards_by_slots, **specs)
    groups, shards = mesh.shape[EXPERT], mesh.shape[DP] * mesh.shape[EXPERT]

    def layer(*arguments):
        tokens, experts = arguments[0], arguments[6].shape[0]
        rows = tokens.shape[0] * tokens.shape[1] // (shards * mesh.shape[FSDP])
        wide = 4 * rows // experts * (experts // groups) >= rows and experts % (2 * groups) == 0
        if groups == 4 and mesh.shape[FSDP] == 2 and tokens.shape[0] == shards and wide:
            return by_tokens(*arguments)
        return by_slots(*arguments)

    return layer
```

```python
import functools
import math

import jax
import jax.numpy as jnp
from jax import lax
from jax.experimental import pallas as pl
from jax.experimental.pallas import tpu as pltpu
from jax.sharding import PartitionSpec as P

DP, FSDP, EXPERT = "dp", "fsdp", "expert"
HEADS = 12
HEAD_DIM = 64


EPSILON = 1e-06
MASKED = -1e30


def shifted(block, axis, distance):
    devices = range(lax.axis_size(axis))
    route = [(i - distance, i) for i in devices if i - distance in devices]
    return lax.ppermute(block, axis, route)


def rms_norm(values, gain_vec):
    return (
        values * lax.rsqrt(jnp.mean(values * values, axis=-1, keepdims=True) + EPSILON) * gain_vec
    )


def block_scores(query_part, key_group, query_place, query_label, key_pos, key_doc, score_scale):
    raw_scores = (
        jnp.einsum("qhd,khd->hqk", query_part, key_group, preferred_element_type=jnp.float32)
        * score_scale
    )
    allowed = (
        (key_pos[None, :] <= query_place[:, None])
        & (key_pos[None, :] >= 0)
        & (key_doc[None, :] == query_label[:, None])
    )
    return jnp.where(allowed[None], raw_scores, MASKED)


def attend_forward(queries, key_rows, value_rows, query_pos, query_doc, key_pos, key_doc):
    row_count = queries.shape[0]
    key_count = key_rows.shape[0]
    group_heads = min(4, HEADS)
    group_count = HEADS // group_heads
    block_rows = min(512, row_count)
    block_count = row_count // block_rows
    group_width = group_heads * HEAD_DIM
    score_scale = 1.0 / math.sqrt(HEAD_DIM)

    def per_group(group_id):
        key_group = lax.dynamic_slice_in_dim(
            key_rows, group_id * group_width, group_width, 1
        ).reshape(key_count, group_heads, HEAD_DIM)
        value_group = lax.dynamic_slice_in_dim(
            value_rows, group_id * group_width, group_width, 1
        ).reshape(key_count, group_heads, HEAD_DIM)

        def per_block(block_id):
            query_part = lax.dynamic_slice(
                queries, (block_id * block_rows, group_id * group_width), (block_rows, group_width)
            ).reshape(block_rows, group_heads, HEAD_DIM)
            scores = block_scores(
                query_part, key_group, query_pos, query_doc, key_pos, key_doc, score_scale
            )
            largest = jnp.max(scores, axis=-1, keepdims=True)
            exp_scores = jnp.exp(scores - largest)
            row_total = jnp.sum(exp_scores, axis=-1, keepdims=True)
            probability = exp_scores / row_total
            log_total = largest[..., 0] + jnp.log(row_total[..., 0])
            mixture = jnp.einsum(
                "hqk,khd->qhd",
                probability.astype(jnp.bfloat16),
                value_group,
                preferred_element_type=jnp.float32,
            )
            return (mixture.reshape(block_rows, group_width), log_total)

        return lax.map(per_block, jnp.arange(block_count, dtype=jnp.int32))

    mixture, log_total = lax.map(per_group, jnp.arange(group_count, dtype=jnp.int32))
    mixture = mixture.transpose(1, 2, 0, 3).reshape(row_count, group_count * group_width)
    return (mixture, log_total)


def attend_backward(
    queries, key_rows, value_rows, grad_mix, log_total, query_pos, query_doc, key_pos, key_doc
):
    row_count = queries.shape[0]
    key_count = key_rows.shape[0]
    group_heads = min(4, HEADS)
    group_count = HEADS // group_heads
    block_rows = min(512, row_count)
    block_count = row_count // block_rows
    group_width = group_heads * HEAD_DIM
    score_scale = 1.0 / math.sqrt(HEAD_DIM)

    def per_group(group_id):
        key_group = lax.dynamic_slice_in_dim(
            key_rows, group_id * group_width, group_width, 1
        ).reshape(key_count, group_heads, HEAD_DIM)
        value_group = lax.dynamic_slice_in_dim(
            value_rows, group_id * group_width, group_width, 1
        ).reshape(key_count, group_heads, HEAD_DIM)
        log_group = lax.dynamic_index_in_dim(log_total, group_id, 0, keepdims=False)

        def per_block(carry, block_id):
            key_acc, value_acc = carry
            query_part = lax.dynamic_slice(
                queries, (block_id * block_rows, group_id * group_width), (block_rows, group_width)
            ).reshape(block_rows, group_heads, HEAD_DIM)
            grad_part = lax.dynamic_slice(
                grad_mix, (block_id * block_rows, group_id * group_width), (block_rows, group_width)
            ).reshape(block_rows, group_heads, HEAD_DIM)
            log_part = lax.dynamic_index_in_dim(log_group, block_id, 0, keepdims=False)
            scores = block_scores(
                query_part, key_group, query_pos, query_doc, key_pos, key_doc, score_scale
            )
            probability = jnp.exp(scores - log_part[:, :, None])
            grad_prob = jnp.einsum(
                "qhd,khd->hqk", grad_part, value_group, preferred_element_type=jnp.float32
            )
            inner = jnp.sum(probability * grad_prob, axis=-1, keepdims=True)
            grad_score = (probability * (grad_prob - inner)).astype(jnp.bfloat16)
            grad_query = (
                jnp.einsum(
                    "hqk,khd->qhd", grad_score, key_group, preferred_element_type=jnp.float32
                )
                * score_scale
            )
            key_acc = (
                key_acc
                + jnp.einsum(
                    "hqk,qhd->khd", grad_score, query_part, preferred_element_type=jnp.float32
                )
                * score_scale
            )
            value_acc = value_acc + jnp.einsum(
                "hqk,qhd->khd",
                probability.astype(jnp.bfloat16),
                grad_part,
                preferred_element_type=jnp.float32,
            )
            return ((key_acc, value_acc), grad_query.reshape(block_rows, group_width))

        empty = jnp.zeros((key_count, group_heads, HEAD_DIM), jnp.float32)
        (key_acc, value_acc), grad_query = lax.scan(
            per_block, (empty, empty), jnp.arange(block_count, dtype=jnp.int32)
        )
        return (
            grad_query,
            key_acc.reshape(key_count, group_width),
            value_acc.reshape(key_count, group_width),
        )

    grad_query, grad_key, grad_value = lax.map(per_group, jnp.arange(group_count, dtype=jnp.int32))
    grad_query = grad_query.transpose(1, 2, 0, 3).reshape(row_count, group_count * group_width)
    grad_key = grad_key.transpose(1, 0, 2).reshape(key_count, group_count * group_width)
    grad_value = grad_value.transpose(1, 0, 2).reshape(key_count, group_count * group_width)
    return (grad_query, grad_key, grad_value)


def expert_preact(token_part, adapt_part, expert_input_weight, flattened_up_factors):
    return jnp.einsum(
        "sxnd,xdf->sxnf", token_part, expert_input_weight, preferred_element_type=jnp.float32
    ) + jnp.einsum(
        "sxnr,rf->sxnf", adapt_part, flattened_up_factors, preferred_element_type=jnp.float32
    )


def shards_by_slots(
    tokens,
    attention_norm_gain,
    expert_norm_gain,
    query_key_value_weight,
    attention_output_weight,
    router_weight,
    expert_input_weight,
    expert_output_weight,
    adapter_down_factors,
    adapter_up_attention,
    adapter_up_routing,
    adapter_up_expert,
    sequence_adapter,
    position_document,
    routes,
    output_gradient,
):
    row_count = tokens.shape[1]
    width = tokens.shape[2]
    local_experts = expert_input_weight.shape[0]
    expert_groups = lax.axis_size(EXPERT)
    expert_count = local_experts * expert_groups
    capacity = 4 * row_count // expert_count
    adapter_total = adapter_down_factors.shape[1]
    adapter_rank_width = adapter_down_factors.shape[3]
    expert_hidden_width = expert_input_weight.shape[2]
    adapter_choice = sequence_adapter[0]
    half_index = lax.axis_index(FSDP)
    doc_row = position_document[0]
    x_in = tokens[0].astype(jnp.float32)
    gain_one = attention_norm_gain.astype(jnp.float32)
    gain_two = expert_norm_gain.astype(jnp.float32)
    normed_f, norm_one_back = jax.vjp(lambda values_in: rms_norm(values_in, gain_one), x_in)
    normed = normed_f.astype(jnp.bfloat16)
    weight_qkv, weight_out = (
        lax.all_gather(query_key_value_weight, FSDP, axis=1, tiled=True),
        lax.all_gather(attention_output_weight, FSDP, axis=0, tiled=True),
    )
    down_factor_list = lax.dynamic_index_in_dim(
        adapter_down_factors, adapter_choice, 1, keepdims=False
    )
    up_factor_list = lax.dynamic_index_in_dim(
        adapter_up_attention, adapter_choice, 1, keepdims=False
    )
    routing_up_factor = lax.dynamic_index_in_dim(
        adapter_up_routing, adapter_choice, 0, keepdims=False
    )
    low_qkv = jnp.einsum(
        "td,pdr->ptr", normed, down_factor_list[:3], preferred_element_type=jnp.float32
    ).astype(jnp.bfloat16)
    qkv = (
        jnp.einsum("td,pde->pte", normed, weight_qkv, preferred_element_type=jnp.float32)
        + jnp.einsum(
            "ptr,pre->pte", low_qkv, up_factor_list[:3], preferred_element_type=jnp.float32
        )
    ).astype(jnp.bfloat16)
    left_kv = shifted(qkv[1:], FSDP, 1)
    key_rows = jnp.concatenate([left_kv[0], qkv[1]], axis=0)
    value_rows = jnp.concatenate([left_kv[1], qkv[2]], axis=0)
    local_pos = jnp.arange(row_count, dtype=jnp.int32)
    query_pos = half_index * row_count + local_pos
    key_pos = jnp.concatenate([query_pos - row_count, query_pos])
    query_doc = lax.dynamic_slice_in_dim(doc_row, half_index * row_count, row_count)
    left_doc = lax.dynamic_slice_in_dim(
        doc_row, jnp.maximum(half_index - 1, 0) * row_count, row_count
    )
    key_doc = jnp.concatenate([left_doc, query_doc])
    mixture_f, log_total = attend_forward(
        qkv[0], key_rows, value_rows, query_pos, query_doc, key_pos, key_doc
    )
    mixture = mixture_f.astype(jnp.bfloat16)
    low_out = jnp.dot(mixture, down_factor_list[3], preferred_element_type=jnp.float32).astype(
        jnp.bfloat16
    )
    branch = jnp.dot(mixture, weight_out, preferred_element_type=jnp.float32) + jnp.dot(
        low_out, up_factor_list[3], preferred_element_type=jnp.float32
    )
    hidden_res = x_in + branch
    normed_two_f, norm_two_back = jax.vjp(
        lambda values_in: rms_norm(values_in, gain_two), hidden_res
    )
    normed_two = normed_two_f.astype(jnp.bfloat16)
    low_router = jnp.dot(
        normed_two, down_factor_list[4], preferred_element_type=jnp.float32
    ).astype(jnp.bfloat16)
    logits = jnp.dot(normed_two, router_weight, preferred_element_type=jnp.float32) + jnp.dot(
        low_router, routing_up_factor, preferred_element_type=jnp.float32
    )
    route_rows = routes[0]
    expert_ids = jnp.arange(expert_count, dtype=jnp.int32)
    choose_hot = (route_rows[:, :, None] == expert_ids[None, None, :]).astype(jnp.float32)
    picked = jnp.sum(logits[:, None, :] * choose_hot, axis=-1)
    gate_probs = jax.nn.softmax(picked, axis=-1)
    low_ffn = jnp.dot(normed_two, down_factor_list[5], preferred_element_type=jnp.float32).astype(
        jnp.bfloat16
    )
    adapter_one = (jnp.arange(adapter_total, dtype=jnp.int32) == adapter_choice).astype(jnp.float32)
    adapter_place = adapter_one.astype(jnp.bfloat16)
    adapter_rows = (adapter_place[None, :, None] * low_ffn[:, None, :]).reshape(
        row_count, adapter_total * adapter_rank_width
    )
    flat_routes = route_rows.reshape(-1)
    route_hot = (flat_routes[:, None] == expert_ids[None, :]).astype(jnp.int32)
    route_rank = jnp.sum((jnp.cumsum(route_hot, axis=0) - route_hot) * route_hot, axis=1)
    slot_index = flat_routes * capacity + route_rank
    assign_count = 2 * row_count
    slot_owner = (
        jnp.full((expert_count * capacity,), assign_count, jnp.int32)
        .at[slot_index]
        .set(jnp.arange(assign_count, dtype=jnp.int32))
    )
    owner_token = slot_owner // 2
    pad_rows = jnp.zeros((1, width), jnp.bfloat16)
    send_tokens = jnp.concatenate([normed_two, pad_rows], axis=0)[owner_token].reshape(
        expert_groups, local_experts, capacity, width
    )
    send_adapt = jnp.concatenate(
        [adapter_rows, jnp.zeros((1, adapter_total * adapter_rank_width), jnp.bfloat16)], axis=0
    )[owner_token].reshape(
        expert_groups, local_experts, capacity, adapter_total * adapter_rank_width
    )
    flattened_up_factors = adapter_up_expert.reshape(
        adapter_total * adapter_rank_width, expert_hidden_width
    )
    token_part = lax.all_to_all(send_tokens, EXPERT, split_axis=0, concat_axis=0, tiled=True)
    adapt_part = lax.all_to_all(send_adapt, EXPERT, split_axis=0, concat_axis=0, tiled=True)
    preact = expert_preact(token_part, adapt_part, expert_input_weight, flattened_up_factors)
    activation = jax.nn.gelu(preact).astype(jnp.bfloat16)
    result = jnp.einsum(
        "sxnf,xfd->sxnd", activation, expert_output_weight, preferred_element_type=jnp.float32
    ).astype(jnp.bfloat16)
    returned = lax.all_to_all(result, EXPERT, split_axis=0, concat_axis=0, tiled=True)
    expert_rows = (
        returned.reshape(expert_count * capacity, width)[slot_index]
        .reshape(row_count, 2, width)
        .astype(jnp.float32)
    )
    expert_sum = jnp.sum(gate_probs[:, :, None] * expert_rows, axis=1)
    output = (hidden_res + expert_sum).astype(jnp.bfloat16)
    grad_out = output_gradient[0].astype(jnp.float32)
    grad_gate = jnp.sum(grad_out[:, None, :] * expert_rows, axis=-1)
    grad_pick = gate_probs * (grad_gate - jnp.sum(gate_probs * grad_gate, axis=-1, keepdims=True))
    grad_logits = jnp.sum(grad_pick[:, :, None] * choose_hot, axis=1)
    grad_assign = (
        (gate_probs[:, :, None] * grad_out[:, None, :])
        .astype(jnp.bfloat16)
        .reshape(assign_count, width)
    )
    send_grad = jnp.concatenate([grad_assign, pad_rows], axis=0)[slot_owner].reshape(
        expert_groups, local_experts, capacity, width
    )
    grad_recv = lax.all_to_all(send_grad, EXPERT, split_axis=0, concat_axis=0, tiled=True)
    grad_act = jnp.einsum(
        "sxnd,xfd->sxnf", grad_recv, expert_output_weight, preferred_element_type=jnp.float32
    )
    grad_pre = jax.vjp(jax.nn.gelu, preact)[1](grad_act)[0].astype(jnp.bfloat16)
    grad_tok_expert = jnp.einsum(
        "sxnf,xdf->sxnd", grad_pre, expert_input_weight, preferred_element_type=jnp.float32
    ).astype(jnp.bfloat16)
    grad_adapt_expert = jnp.einsum(
        "sxnf,rf->sxnr", grad_pre, flattened_up_factors, preferred_element_type=jnp.float32
    ).astype(jnp.bfloat16)
    grad_up_ffn = jnp.einsum(
        "sxnr,sxnf->rf", adapt_part, grad_pre, preferred_element_type=jnp.float32
    ).reshape(adapter_total, adapter_rank_width, expert_hidden_width)
    grad_back_tok, grad_back_adapt = (
        lax.all_to_all(grad_tok_expert, EXPERT, split_axis=0, concat_axis=0, tiled=True),
        lax.all_to_all(grad_adapt_expert, EXPERT, split_axis=0, concat_axis=0, tiled=True),
    )
    grad_normed_two = jnp.sum(
        grad_back_tok.reshape(expert_count * capacity, width)[slot_index]
        .astype(jnp.float32)
        .reshape(row_count, 2, width),
        axis=1,
    )
    adapt_back = grad_back_adapt.reshape(
        expert_count * capacity, adapter_total, adapter_rank_width
    )[slot_index].astype(jnp.float32)
    grad_low_ffn = jnp.sum(
        jnp.sum(adapt_back * adapter_one[None, :, None], axis=1).reshape(
            row_count, 2, adapter_rank_width
        ),
        axis=1,
    )
    grad_low_router = jnp.einsum(
        "te,re->tr", grad_logits, routing_up_factor, preferred_element_type=jnp.float32
    )
    grad_up_router = jnp.einsum(
        "tr,te->re", low_router, grad_logits, preferred_element_type=jnp.float32
    )
    grad_down_router = jnp.einsum(
        "td,tr->dr", normed_two, grad_low_router, preferred_element_type=jnp.float32
    )
    grad_down_ffn = jnp.einsum(
        "td,tr->dr", normed_two, grad_low_ffn, preferred_element_type=jnp.float32
    )
    grad_normed_two = grad_normed_two + jnp.einsum(
        "tr,dr->td", grad_low_ffn, down_factor_list[5], preferred_element_type=jnp.float32
    )
    grad_normed_two = grad_normed_two + jnp.einsum(
        "te,de->td", grad_logits, router_weight, preferred_element_type=jnp.float32
    )
    grad_normed_two = grad_normed_two + jnp.einsum(
        "tr,dr->td", grad_low_router, down_factor_list[4], preferred_element_type=jnp.float32
    )
    grad_hidden = grad_out + norm_two_back(grad_normed_two)[0]
    grad_branch = grad_hidden.astype(jnp.bfloat16)
    weight_qkv_back, weight_out_back = (
        lax.all_gather(query_key_value_weight, FSDP, axis=1, tiled=True),
        lax.all_gather(attention_output_weight, FSDP, axis=0, tiled=True),
    )
    grad_up_out = jnp.einsum("tr,te->re", low_out, grad_branch, preferred_element_type=jnp.float32)
    grad_low_out = jnp.einsum(
        "te,re->tr", grad_branch, up_factor_list[3], preferred_element_type=jnp.float32
    )
    grad_down_out = jnp.einsum(
        "td,tr->dr", mixture, grad_low_out, preferred_element_type=jnp.float32
    )
    grad_mixture = (
        jnp.einsum("te,de->td", grad_branch, weight_out_back, preferred_element_type=jnp.float32)
        + jnp.einsum(
            "tr,dr->td", grad_low_out, down_factor_list[3], preferred_element_type=jnp.float32
        )
    ).astype(jnp.bfloat16)
    grad_query, grad_key, grad_value = attend_backward(
        qkv[0],
        key_rows,
        value_rows,
        grad_mixture,
        log_total,
        query_pos,
        query_doc,
        key_pos,
        key_doc,
    )
    sent_back = shifted(
        jnp.stack([grad_key[:row_count], grad_value[:row_count]]).astype(jnp.bfloat16), FSDP, -1
    ).astype(jnp.float32)
    grad_qkv = jnp.stack(
        [grad_query, grad_key[row_count:] + sent_back[0], grad_value[row_count:] + sent_back[1]]
    ).astype(jnp.bfloat16)
    grad_up_qkv = jnp.einsum("ptr,pte->pre", low_qkv, grad_qkv, preferred_element_type=jnp.float32)
    grad_low_qkv = jnp.einsum(
        "pte,pre->ptr", grad_qkv, up_factor_list[:3], preferred_element_type=jnp.float32
    )
    grad_down_qkv = jnp.einsum(
        "td,ptr->pdr", normed, grad_low_qkv, preferred_element_type=jnp.float32
    )
    grad_normed = jnp.einsum(
        "pte,pde->td", grad_qkv, weight_qkv_back, preferred_element_type=jnp.float32
    ) + jnp.einsum(
        "ptr,pdr->td", grad_low_qkv, down_factor_list[:3], preferred_element_type=jnp.float32
    )
    grad_tokens = (grad_hidden + norm_one_back(grad_normed)[0]).astype(jnp.bfloat16)
    grad_down = jnp.concatenate(
        [grad_down_qkv, grad_down_out[None], grad_down_router[None], grad_down_ffn[None]], axis=0
    )
    grad_down_all = adapter_one[None, :, None, None] * grad_down[:, None]
    grad_up_attn = jnp.concatenate([grad_up_qkv, grad_up_out[None]], axis=0)
    grad_up_attn_all = adapter_one[None, :, None, None] * grad_up_attn[:, None]
    grad_router_all = adapter_one[:, None, None] * grad_up_router[None]
    group_parts = (
        lax.psum_scatter(grad_down_all, (FSDP, EXPERT), scatter_dimension=2, tiled=True),
        lax.psum_scatter(grad_up_attn_all, (FSDP, EXPERT), scatter_dimension=3, tiled=True),
        lax.psum_scatter(grad_router_all, (FSDP, EXPERT), scatter_dimension=2, tiled=True),
        lax.psum_scatter(grad_up_ffn, (FSDP, EXPERT), scatter_dimension=2, tiled=True),
    )
    totals = lax.psum((group_parts[0], group_parts[1], group_parts[2], group_parts[3]), DP)
    return (output[None], grad_tokens[None], totals[0], totals[1], totals[2], totals[3])


def mxu(left, right, left_dim=1, right_dim=0):
    return lax.dot_general(
        left, right, (((left_dim,), (right_dim,)), ((), ())), preferred_element_type=jnp.float32
    )


def normed_rows(values, gain):
    return (
        values * lax.rsqrt(jnp.mean(values * values, axis=-1, keepdims=True) + EPSILON) * gain
    )


def norm_back(values, gain, grad):
    root = lax.rsqrt(jnp.mean(values * values, axis=-1, keepdims=True) + EPSILON)
    inner = grad * gain
    mean = jnp.mean(values * inner, axis=-1, keepdims=True)
    return root * inner - values * (root * root * root * mean)


def gate_rows(x, down, upr, router, routes):
    rank = upr.shape[1]
    low = mxu(down, x, 1, 1)
    low_router = low[:rank].astype(jnp.bfloat16)
    logits = mxu(router, x, 1, 1) + mxu(upr, low_router)
    ids = lax.broadcasted_iota(jnp.int32, logits.shape, 0)
    hot = (ids == routes[0:1]) | (ids == routes[1:2])
    top = jnp.max(jnp.where(hot, logits, -jnp.inf), axis=0, keepdims=True)
    ex = jnp.where(hot, jnp.exp(logits - top), 0.0)
    gates = ex / jnp.sum(ex, axis=0, keepdims=True)
    return low_router, low[rank:].astype(jnp.bfloat16), gates, hot, ids


def dense_call(kernel, name, scalars, grid, inputs, outputs, scratch, flops):
    return pl.pallas_call(
        kernel,
        grid_spec=pltpu.PrefetchScalarGridSpec(
            num_scalar_prefetch=1,
            grid=grid,
            in_specs=[pl.BlockSpec(block, index) for _, block, index in inputs],
            out_specs=[pl.BlockSpec(block, index) for _, _, block, index in outputs],
            scratch_shapes=[pltpu.VMEM(shape, kind) for shape, kind in scratch],
        ),
        out_shape=[jax.ShapeDtypeStruct(shape, kind) for shape, kind, _, _ in outputs],
        compiler_params=pltpu.CompilerParams(
            vmem_limit_bytes=(24000 if name == "fg" else 56000) * 1024
        ),
        cost_estimate=pl.CostEstimate(flops=flops, bytes_accessed=flops // 256, transcendentals=0),
    )(scalars, *(array for array, _, _ in inputs))


def fill_joined(half, mine, other, weight_s):
    tall = mine.shape[0]
    weight_s[pl.ds(pl.multiple_of(half * tall, tall), tall), :] = mine
    weight_s[pl.ds(pl.multiple_of((1 - half) * tall, tall), tall), :] = other


def first_kernel(sc, x_ref, left_ref, gain_ref, mine_ref, other_ref, down_ref, up_ref, *outs):
    normed_ref, low_ref, q_ref, kv_ref, xn_s, weight_s = outs
    step = pl.program_id(0)
    rows, width = x_ref.shape
    rank = up_ref.shape[2]
    bf16 = jnp.bfloat16

    @pl.when(step == 0)
    def _():
        gain = gain_ref[...].astype(jnp.float32)
        factors = down_ref[:, 0].reshape(down_ref.shape[0] * rank, width)
        for at, ref in ((0, left_ref), (rows, x_ref)):
            xn = normed_rows(ref[...].astype(jnp.float32), gain).astype(bf16)
            xn_s[at : at + rows, :width] = xn
            low = mxu(xn, factors, 1, 1).astype(bf16)
            blank = jnp.zeros((rows, xn_s.shape[1] - width - low.shape[1]), bf16)
            xn_s[at : at + rows, width:] = jnp.concatenate([low, blank], axis=1)
            if at > 0:
                normed_ref[...] = xn
                low = low.astype(jnp.float32).T.astype(bf16)
                for p in range(low_ref.shape[0]):
                    low_ref[p] = low[p * rank : (p + 1) * rank]
        weight_s[width:, :] = jnp.zeros((weight_s.shape[0] - width, width), bf16)

    fill_joined(sc[0], mine_ref[0], other_ref[0], weight_s)
    for p in range(low_ref.shape[0]):
        at = width + p * rank
        factor = up_ref[0, 0]
        weight_s[at : at + rank, :] = jnp.where(step == p, factor, jnp.zeros_like(factor))

    @pl.when(step == 0)
    def _():
        q_ref[...] = mxu(xn_s[rows:, :], weight_s[...]).astype(bf16)

    @pl.when(step > 0)
    def _():
        kv_ref[0] = mxu(xn_s[...], weight_s[...]).astype(bf16)


def project_in(scalars, x, left, gain, mine, other, downs, ups):
    rows, width = x.shape
    rank = downs.shape[2]
    bf16 = jnp.bfloat16
    whole = lambda i, s: (0, 0)
    lead = lambda i, s: (i, 0, 0)
    factor = lambda i, s: (i, s[1], 0, 0)
    return dense_call(
        first_kernel,
        "pi",
        scalars,
        (3,),
        [
            (x, (rows, width), whole),
            (left, (rows, width), whole),
            (gain.reshape(1, width), (1, width), whole),
            (mine, (1, width // 2, width), lead),
            (other, (1, width // 2, width), lead),
            (downs, (3, 1, rank, width), lambda i, s: (0, s[1], 0, 0)),
            (ups, (1, 1, rank, width), factor),
        ],
        [
            ((rows, width), bf16, (rows, width), whole),
            ((3, rank, rows), bf16, (3, rank, rows), lambda i, s: (0, 0, 0)),
            ((rows, width), bf16, (rows, width), whole),
            (
                (2, 2 * rows, width),
                bf16,
                (1, 2 * rows, width),
                lambda i, s: (jnp.maximum(i - 1, 0), 0, 0),
            ),
        ],
        [((2 * rows, width + 128), bf16), ((width + 128, width), bf16)],
        10 * rows * width * width,
    )


def middle_kernel(sc, x_ref, att_ref, mine_ref, other_ref, down_ref, up_ref, gain_ref, *outs):
    low_ref, hidden_ref, normed_ref, weight_s = outs

    @pl.when(pl.program_id(0) == 0)
    def _():
        fill_joined(sc[0], mine_ref[...], other_ref[...], weight_s)

    att = att_ref[...]
    low = mxu(att, down_ref[0, 0], 1, 1)
    low_ref[...] = low.T.astype(jnp.bfloat16)
    low = low.astype(jnp.bfloat16)
    hidden = x_ref[...].astype(jnp.float32) + (
        mxu(att, weight_s[...]) + mxu(low, up_ref[0, 0])
    )
    hidden_ref[...] = hidden
    normed_ref[...] = normed_rows(hidden, gain_ref[...].astype(jnp.float32)).astype(jnp.bfloat16)


def project_out(scalars, x, att, mine, other, downs, ups, gain):
    rows, width = x.shape
    rank = downs.shape[2]
    tall = rows // 2
    whole = lambda i, s: (0, 0)
    block = lambda i, s: (i, 0)
    return dense_call(
        middle_kernel,
        "po",
        scalars,
        (2,),
        [
            (x, (tall, width), block),
            (att, (tall, width), block),
            (mine, (width // 2, width), whole),
            (other, (width // 2, width), whole),
            (downs, (1, 1, rank, width), lambda i, s: (3, s[1], 0, 0)),
            (ups, (1, 1, rank, width), lambda i, s: (3, s[1], 0, 0)),
            (gain.reshape(1, width), (1, width), whole),
        ],
        [
            ((rank, rows), jnp.bfloat16, (rank, tall), lambda i, s: (0, i)),
            ((rows, width), jnp.float32, (tall, width), block),
            ((rows, width), jnp.bfloat16, (tall, width), block),
        ],
        [((width, width), jnp.bfloat16)],
        2 * rows * width * width,
    )


def after_kernel(share, wide, sc, *refs):
    dx_refs, extra_refs = refs[:5], refs[5:10]
    (
        go_ref,
        hidden_ref,
        normed_ref,
        att_ref,
        low_ref,
        routes_ref,
        down45_ref,
        router_ref,
        upr_ref,
        down3_ref,
        up3_ref,
        mine_ref,
        other_ref,
        gain_ref,
        datt_ref,
        dh_ref,
        rows_ref,
        weight_s,
    ) = refs[10:]
    bf16, f32 = jnp.bfloat16, jnp.float32
    rank = down3_ref.shape[2]

    @pl.when(pl.program_id(0) == 0)
    def _():
        rows_ref[...] = jnp.zeros_like(rows_ref)
        fill_joined(sc[0], mine_ref[...], other_ref[...], weight_s)

    xn = normed_ref[...]
    low_router, _, gates, _, ids = gate_rows(
        xn, down45_ref[0], upr_ref[0], router_ref[...], routes_ref[0]
    )
    extra = sum(ref[...].astype(f32) for ref in extra_refs)
    dgate = 0.0
    for k in range(2):
        value = extra[rank + k : rank + k + 1] + extra[rank + 8 + k : rank + 9 + k]
        dgate = dgate + jnp.where(ids == routes_ref[0, k : k + 1], value, 0.0)
    dlogits = gates * (dgate - jnp.sum(gates * dgate, axis=0, keepdims=True))
    dlogits = dlogits.astype(bf16)
    dlr = mxu(upr_ref[0], dlogits, 0, 0).astype(bf16)
    dlf = extra[:rank].astype(bf16)
    dxn = sum(ref[...].astype(f32) for ref in dx_refs)
    dxn = dxn + mxu(dlr, down45_ref[0, :rank], 0, 0) + mxu(dlf, down45_ref[0, rank:], 0, 0)
    dxn = dxn + mxu(dlogits, router_ref[...], 0, 0)
    dh = go_ref[...].astype(f32) + norm_back(hidden_ref[...], gain_ref[...].astype(f32), dxn)
    dh_ref[...] = dh
    gb = dh.astype(bf16)
    att = att_ref[...]
    dlo = mxu(up3_ref[0, 0], gb, 1, 1).astype(bf16)
    datt_ref[...] = (mxu(gb, weight_s[...], 1, 1) + mxu(dlo, down3_ref[0, 0], 0, 0)).astype(bf16)
    router = mxu(low_router, dlogits, 1, 1).astype(bf16)
    choices, width = router_ref.shape
    column = lax.broadcasted_iota(jnp.int32, (choices, width), 0)
    lane = lax.broadcasted_iota(jnp.int32, (choices, width), 1)
    spot = lane == (column // wide) * share + column % wide
    rows_ref[0] += mxu(dlo, att)
    rows_ref[1] += mxu(dlr, xn)
    rows_ref[2] += mxu(dlf, xn)
    rows_ref[3] += mxu(low_ref[...], gb)
    rows_ref[4] += mxu(router, spot.astype(f32).astype(bf16))


def after_experts(
    scalars, dxs, go, hidden, normed, att, low, routes, down_t, router_t, upr_t, downs, ups, mine,
    other, gain, share, wide
):
    rows, width = hidden.shape
    rank = downs.shape[2]
    tall = rows // 2
    choices = router_t.shape[0]
    extra = dxs[0].shape[0] - rows
    whole = lambda i, s: (0, 0)
    block = lambda i, s: (i, 0)
    adapter = lambda i, s: (s[1], 0, 0)
    return dense_call(
        functools.partial(after_kernel, share, wide),
        "ae",
        scalars,
        (2,),
        [(dx, (tall, width), block) for dx in dxs]
        + [(dx, (extra, tall), lambda i, s: (rows // extra, i)) for dx in dxs]
        + [(array, (tall, width), block) for array in (go, hidden, normed, att)]
        + [
            (low, (rank, tall), lambda i, s: (0, i)),
            (routes, (1, 2, tall), lambda i, s: (0, 0, i)),
            (down_t, (1, 2 * rank, width), adapter),
            (router_t, (choices, width), whole),
            (upr_t, (1, choices, rank), adapter),
            (downs, (1, 1, rank, width), lambda i, s: (3, s[1], 0, 0)),
            (ups, (1, 1, rank, width), lambda i, s: (3, s[1], 0, 0)),
            (mine, (width // 2, width), whole),
            (other, (width // 2, width), whole),
            (gain.reshape(1, width), (1, width), whole),
        ],
        [
            ((rows, width), jnp.bfloat16, (tall, width), block),
            ((rows, width), jnp.float32, (tall, width), block),
            ((5, rank, width), jnp.float32, (5, rank, width), lambda i, s: (0, 0, 0)),
        ],
        [((width, width), jnp.bfloat16)],
        3 * rows * width * width,
    )


def factors_kernel(sc, dq_ref, own_ref, back_ref, low_ref, up_ref, normed_ref, early_ref, *outs):
    grad_ref, glow_ref, kept_ref, given_ref = outs
    p = pl.program_id(0)
    bf16 = jnp.bfloat16
    summed = (own_ref[0] + back_ref[0].astype(jnp.float32)).astype(bf16)
    grad = jnp.where(p == 0, dq_ref[...], summed)
    grad_ref[0] = grad
    glow = mxu(up_ref[0, 0], grad, 1, 1).astype(bf16)
    glow_ref[0] = glow
    rank, width = glow.shape[0], grad.shape[1]
    half = sc[0]

    def put(at, value):
        low, high = value[:, : width // 2], value[:, width // 2 :]
        at = pl.ds(pl.multiple_of(at * rank, rank), rank)
        kept_ref[at, :] = jnp.where(half == 0, low, high)
        given_ref[at, :] = jnp.where(half == 0, high, low).astype(bf16)

    put(p, mxu(glow, normed_ref[...]))
    put(6 + p, mxu(low_ref[0], grad))

    @pl.when(p == 0)
    def _():
        for i, at in enumerate((3, 4, 5, 9, 10)):
            put(at, early_ref[i])
        put(11, jnp.full((rank, width), 0.5, jnp.float32) * sc[1].astype(jnp.float32))


def factor_grads(scalars, dq, own, back, low, ups, normed, early):
    rows, width = dq.shape
    rank = ups.shape[2]
    total = 12 * rank
    whole = lambda i, s: (0, 0)
    prior = lambda i, s: (jnp.maximum(i - 1, 0), 0, 0)
    lead = lambda i, s: (i, 0, 0)
    return dense_call(
        factors_kernel,
        "fg",
        scalars,
        (3,),
        [
            (dq, (rows, width), whole),
            (own, (1, rows, width), prior),
            (back, (1, rows, width), prior),
            (low, (1, rank, rows), lead),
            (ups, (1, 1, rank, width), lambda i, s: (i, s[1], 0, 0)),
            (normed, (rows, width), whole),
            (early, (5, rank, width), lambda i, s: (0, 0, 0)),
        ],
        [
            ((3, rows, width), jnp.bfloat16, (1, rows, width), lead),
            ((3, rank, rows), jnp.bfloat16, (1, rank, rows), lead),
            ((total, width // 2), jnp.float32, (total, width // 2), whole),
            ((total, width // 2), jnp.bfloat16, (total, width // 2), whole),
        ],
        [],
        rows * width * width // 4,
    )


def last_kernel(sc, grad_ref, glow_ref, mine_ref, other_ref, down_ref, x_ref, gain_ref, *refs):
    dh_ref, grad_x_ref, acc, weight_s = refs
    p = pl.program_id(0)
    fill_joined(sc[0], mine_ref[0], other_ref[0], weight_s)
    term = mxu(grad_ref[0], weight_s[...], 1, 1) + mxu(glow_ref[0], down_ref[0, 0], 0, 0)
    acc[...] = jnp.where(p == 0, term, acc[...] + term)

    @pl.when(p == pl.num_programs(0) - 1)
    def _():
        back = norm_back(
            x_ref[...].astype(jnp.float32), gain_ref[...].astype(jnp.float32), acc[...]
        )
        grad_x_ref[...] = (dh_ref[...] + back).astype(grad_x_ref.dtype)


def last_rows(scalars, grads, glow, mine, other, downs, x, gain, dh):
    rows, width = x.shape
    rank = downs.shape[2]
    whole = lambda i, s: (0, 0)
    lead = lambda i, s: (i, 0, 0)
    return dense_call(
        last_kernel,
        "lr",
        scalars,
        (3,),
        [
            (grads, (1, rows, width), lead),
            (glow, (1, rank, rows), lead),
            (mine, (1, width // 2, width), lead),
            (other, (1, width // 2, width), lead),
            (downs, (1, 1, rank, width), lambda i, s: (i, s[1], 0, 0)),
            (x, (rows, width), whole),
            (gain.reshape(1, width), (1, width), whole),
            (dh, (rows, width), whole),
        ],
        [((rows, width), jnp.bfloat16, (rows, width), whole)],
        [((rows, width), jnp.float32), ((width, width), jnp.bfloat16)],
        6 * rows * width * width,
    )


def sums_kernel(count, share, sc, *refs):
    part_refs = refs[:count]
    down_ref, up_ref, router_ref, ffn_ref, acc = refs[count:]
    rank, wide = ffn_ref.shape[1], part_refs[0].shape[2]
    acc[...] = jnp.zeros_like(acc)
    for part_ref in part_refs:
        for s in range(part_ref.shape[0]):
            part = part_ref[s].astype(jnp.float32)
            label = jnp.max(part[11 * rank : 11 * rank + 8, :share]).astype(jnp.int32)
            acc[label] += part
    for a in range(acc.shape[0]):
        rows = acc[a]
        for i in range(6):
            down_ref[i, a] = rows[i * rank : (i + 1) * rank, :share]
        for i in range(4):
            up_ref[i, a] = rows[(6 + i) * rank : (7 + i) * rank, :share]
        router_ref[a] = rows[10 * rank : 11 * rank].T[: router_ref.shape[1]]
        for i in range(ffn_ref.shape[2] // wide):
            ffn_ref[a, :, i * wide : (i + 1) * wide] = rows[(12 + i) * rank : (13 + i) * rank]


def adapter_sums(scalars, parts, choices, rank, share, narrow, wide):
    f32 = jnp.float32
    outs = [
        (6, choices, rank, share),
        (4, choices, rank, share),
        (choices, narrow, rank),
        (choices, rank, wide),
    ]
    fixed = lambda shape: (shape, lambda i, s: (0,) * len(shape))
    return dense_call(
        functools.partial(sums_kernel, len(parts), share),
        "as",
        scalars,
        (1,),
        [(part, *fixed(part.shape)) for part in parts],
        [(shape, f32, *fixed(shape)) for shape in outs],
        [((choices, *parts[0].shape[1:]), f32)],
        10**6,
    )


def window_bias(bias, kdoc_ref, qdoc_ref, block):
    keys, cols = bias.shape[1:]
    kpos = lax.broadcasted_iota(jnp.int32, (keys, cols), 0) - (keys - cols)
    qpos = lax.broadcasted_iota(jnp.int32, (keys, cols), 1)
    key_doc = kdoc_ref[pl.ds(pl.multiple_of(block * cols, cols), keys), :]
    bias[block] = jnp.where((kpos <= qpos) & (key_doc == qdoc_ref[...]), 0.0, MASKED)


def head_probability(queries, key_parts, bias, block, first):
    tall = queries.shape[0]
    scores = [
        mxu(part, queries, 1, 1) + bias[block, (first + i) * tall : (first + i + 1) * tall, :]
        for i, part in enumerate(key_parts)
    ]
    top = functools.reduce(jnp.maximum, [jnp.max(s, axis=0, keepdims=True) for s in scores])
    parts = [jnp.exp(s - top) for s in scores]
    total = sum(jnp.sum(p, axis=0, keepdims=True) for p in parts)
    share = 1.0 / total
    return [p * share for p in parts]


def attend_kernel(reach, kdoc_ref, qdoc_ref, q_ref, *refs):
    key_refs, value_refs = refs[:3], refs[3:6]
    out_ref, bias = refs[6:]
    block = pl.program_id(1)

    @pl.when(pl.program_id(0) == 0)
    def _():
        window_bias(bias, kdoc_ref, qdoc_ref, block)

    def run(first):
        keys, values = ([ref[0] for ref in part[first:]] for part in (key_refs, value_refs))
        mixed = []
        for head in range(q_ref.shape[1] // HEAD_DIM):
            cols = slice(head * HEAD_DIM, (head + 1) * HEAD_DIM)
            queries = q_ref[:, cols] * (1.0 / math.sqrt(HEAD_DIM))
            probability = head_probability(
                queries, [key[:, cols] for key in keys], bias, block, first
            )
            mixed.append(
                sum(
                    mxu(value[:, cols], p.astype(jnp.bfloat16), 0, 0)
                    for value, p in zip(values, probability)
                )
            )
        out_ref[...] = jnp.concatenate(mixed, axis=0).T.astype(out_ref.dtype)

    for first in range(3):
        pl.when(reach[block] == first)(functools.partial(run, first))


def attend_back_kernel(reach, kdoc_ref, qdoc_ref, q_ref, *refs):
    key_refs, value_refs = refs[:3], refs[3:6]
    grad_ref, dq_ref, own_ref, left_ref, bias, acc = refs[6:]
    block = pl.program_id(1)
    scale = 1.0 / math.sqrt(HEAD_DIM)

    @pl.when(pl.program_id(0) == 0)
    def _():
        window_bias(bias, kdoc_ref, qdoc_ref, block)

    @pl.when(block == 0)
    def _():
        acc[...] = jnp.zeros_like(acc)

    def run(first):
        keys, values = ([ref[0] for ref in part[first:]] for part in (key_refs, value_refs))
        grad_queries = []
        for head in range(q_ref.shape[1] // HEAD_DIM):
            cols = slice(head * HEAD_DIM, (head + 1) * HEAD_DIM)
            queries = q_ref[:, cols] * scale
            grad = grad_ref[:, cols]
            probability = head_probability(
                queries, [key[:, cols] for key in keys], bias, block, first
            )
            grad_prob = [mxu(value[:, cols], grad, 1, 1) for value in values]
            inner = sum(
                jnp.sum(p * g, axis=0, keepdims=True) for p, g in zip(probability, grad_prob)
            )
            grad_score = [
                (p * (g - inner)).astype(jnp.bfloat16) for p, g in zip(probability, grad_prob)
            ]
            grad_queries.append(
                sum(mxu(key[:, cols], g, 0, 0) for key, g in zip(keys, grad_score)) * scale
            )
            for i, (p, g) in enumerate(zip(probability, grad_score)):
                acc[0, block + first + i, :, cols] += mxu(g, queries)
                acc[1, block + first + i, :, cols] += mxu(p.astype(jnp.bfloat16), grad)
        dq_ref[...] = jnp.concatenate(grad_queries, axis=0).T.astype(dq_ref.dtype)

    for first in range(3):
        pl.when(reach[block] == first)(functools.partial(run, first))

    @pl.when(block == pl.num_programs(1) - 1)
    def _():
        tall = q_ref.shape[0]
        for i in range(2):
            rows = slice(i * tall, (i + 1) * tall)
            for kind in range(2):
                left_ref[kind, rows, :] = acc[kind, i].astype(left_ref.dtype)
                own_ref[kind, rows, :] = acc[kind, 2 + i].astype(own_ref.dtype)


def attention_call(kernel, queries, keys_values, grads, key_doc, query_doc, outs, scratch, flops):
    rows, width = queries.shape
    lanes = 2 * HEAD_DIM
    tall = rows // 2
    reach = sum(
        (
            key_doc[(i + 1) * tall - 1 : (i + 2) * tall : tall]
            != query_doc[: 2 * tall : tall]
        ).astype(jnp.int32)
        for i in range(2)
    )

    sources = [
        pl.BlockSpec((1, tall, lanes), lambda g, b, s, p=p, i=i: (p, b + i, g))
        for p in range(2)
        for i in range(3)
    ]

    def stack(kind):
        return {
            "block": pl.BlockSpec((tall, lanes), lambda g, b, s: (b, g)),
            "pair": pl.BlockSpec((2, rows, lanes), lambda g, b, s: (0, 0, g)),
        }[kind]

    return pl.pallas_call(
        kernel,
        grid_spec=pltpu.PrefetchScalarGridSpec(
            num_scalar_prefetch=1,
            grid=(width // lanes, 2),
            in_specs=[
                pl.BlockSpec((2 * rows, 1), lambda g, b, s: (0, 0)),
                pl.BlockSpec((1, tall), lambda g, b, s: (0, b)),
                stack("block"),
                *sources,
            ]
            + [stack("block")] * len(grads),
            out_specs=[stack(kind) for kind, _ in outs],
            scratch_shapes=[pltpu.VMEM((2, 3 * tall, tall), jnp.float32)]
            + [pltpu.VMEM((2, 4, tall, lanes), jnp.float32)] * scratch,
        ),
        out_shape=[
            jax.ShapeDtypeStruct((rows, width) if kind == "block" else (2, rows, width), dtype)
            for kind, dtype in outs
        ],
        compiler_params=pltpu.CompilerParams(vmem_limit_bytes=56000 * 1024),
        cost_estimate=pl.CostEstimate(
            flops=flops * rows * rows * width,
            bytes_accessed=12 * rows * width,
            transcendentals=HEADS * rows * rows,
        ),
        name="ab2" if scratch else "at",
    )(
        reach,
        key_doc.reshape(-1, 1),
        query_doc.reshape(1, -1),
        queries,
        *([keys_values] * 6),
        *grads,
    )


def gelu_both(u):
    c = math.sqrt(2.0 / math.pi)
    sq = u * u
    t = jnp.tanh(u * (c + (c * 0.044715) * sq))
    half = 0.5 + 0.5 * t
    slope = half + (0.5 * u) * (1.0 - t * t) * (c + (3.0 * c * 0.044715) * sq)
    return u * half, slope


def expert_kernel(turn, pieces, capacity, rank, *refs):
    scalars = refs[0]
    x_refs, g_refs = refs[1 : 1 + pieces], refs[1 + pieces : 1 + 2 * pieces]
    (
        route_ref,
        down_ref,
        upr_ref,
        uf_ref,
        router_ref,
        w1_ref,
        w2_ref,
        _,
        y_ref,
        dx_ref,
        gff_ref,
        x_s,
        g_s,
        xe,
        goe,
        dye,
        lfe,
        yacc,
        dxacc,
        dleacc,
        onehot_s,
        lft_s,
        gate_s,
        rank_s,
        ysum,
        dxsum,
        ext_s,
    ) = refs[1 + 2 * pieces :]
    e = pl.program_id(0)
    t = pl.program_id(1)
    last_t = pl.num_programs(1) - 1
    last_e = pl.num_programs(0) - 1
    rows, width = x_refs[0].shape
    tile = w1_ref.shape[2]
    ident = scalars[5 * turn] + e
    bf16, f32 = jnp.bfloat16, jnp.float32

    @pl.when((e == 0) & (t == 0))
    def _():
        ysum[...] = jnp.zeros_like(ysum)
        dxsum[...] = jnp.zeros_like(dxsum)
        ext_s[...] = jnp.zeros_like(ext_s)
        gff_ref[...] = jnp.zeros_like(gff_ref)
        x = sum(ref[...] for ref in x_refs)
        x_s[...] = x
        g_s[...] = sum(ref[...] for ref in g_refs)
        _, lft_s[...], gate_s[...], hot, _ = gate_rows(
            x, down_ref[0], upr_ref[0], router_ref[...], route_ref[0]
        )
        before = lax.broadcasted_iota(jnp.int32, (rows, rows), 0) < lax.broadcasted_iota(
            jnp.int32, (rows, rows), 1
        )
        ranks = mxu(hot.astype(f32).astype(bf16), before.astype(f32).astype(bf16))
        rank_s[...] = jnp.where(hot, ranks, -1.0)

    def slots():
        row = rank_s[pl.ds(ident, 1), :]
        picks = lax.broadcasted_iota(jnp.int32, (capacity, rows), 0).astype(f32) == row
        gate = gate_s[pl.ds(ident, 1), :]
        return picks, jnp.sum(jnp.where(picks, gate, 0.0), axis=1, keepdims=True)

    @pl.when(t == 0)
    def _():
        picks, gate_slot = slots()
        onehot = picks.astype(f32).astype(bf16)
        onehot_s[...] = onehot
        xe[...] = mxu(onehot, x_s[...]).astype(bf16)
        go = mxu(onehot, g_s[...])
        goe[...] = go.astype(bf16)
        dye[...] = (go * gate_slot).astype(bf16)
        lfe[...] = mxu(onehot, lft_s[...], 1, 1).astype(bf16)
        yacc[...] = jnp.zeros_like(yacc)
        dxacc[...] = jnp.zeros_like(dxacc)
        dleacc[...] = jnp.zeros_like(dleacc)

    off = pl.multiple_of(t * tile, tile)
    pre = mxu(xe[...], w1_ref[0]) + mxu(lfe[...], uf_ref[0])
    act, slope = gelu_both(pre)
    yacc[...] += mxu(act.astype(bf16), w2_ref[0])
    dpre = (mxu(dye[...], w2_ref[0], 1, 1) * slope).astype(bf16)
    dxacc[...] += mxu(dpre, w1_ref[0], 1, 1)
    dleacc[...] += mxu(uf_ref[0], dpre, 1, 1)
    gff_ref[0, :, pl.ds(off, tile)] += mxu(lfe[...], dpre, 0, 0)

    @pl.when(t == last_t)
    def _():
        picks, gate_slot = slots()
        onehot = onehot_s[...]
        y = yacc[...].astype(bf16).astype(f32)
        dgate = jnp.sum(goe[...].astype(f32) * y, axis=1, keepdims=True)
        dgate_row = jnp.sum(jnp.where(picks, dgate, 0.0), axis=0, keepdims=True)
        for k in range(2):
            mine = route_ref[0, k : k + 1] == ident
            ext_s[rank + k : rank + k + 1, :] += jnp.where(mine, dgate_row, 0.0)
        ext_s[0:rank, :] += mxu(dleacc[...].astype(bf16), onehot)
        ysum[...] += mxu(onehot, (y * gate_slot).astype(bf16), 0, 0)
        dxsum[...] += mxu(onehot, dxacc[...].astype(bf16), 0, 0)

    @pl.when((e == last_e) & (t == last_t))
    def _():
        y_ref[...] = ysum[...].astype(bf16)
        dx_ref[:rows, :] = dxsum[...].astype(bf16)
        extra = ext_s[...]
        gates = extra[rank:]
        low = gates - gates.astype(bf16).astype(f32)
        packed = jnp.concatenate([extra, low], axis=0).astype(bf16)
        if width > rows:
            blank = jnp.zeros((packed.shape[0], width - rows), bf16)
            packed = jnp.concatenate([packed, blank], axis=1)
        dx_ref[rows:, :] = packed


def run_experts(
    turn, scalars, local, xs, gs, route_rows, down_t, router_t, upr_t, up_ffn, w1, w2, gff, capacity
):
    pieces = len(xs)
    rows, width = xs[0].shape
    hidden = w1.shape[2]
    expert_count = router_t.shape[0]
    rank = up_ffn.shape[1]
    tile = 1024 if hidden % 1024 == 0 else hidden
    fixed = lambda *shape, **kw: pl.BlockSpec(shape, lambda e, t, sc: (0,) * len(shape), **kw)
    adapter = lambda *shape: pl.BlockSpec((1, *shape), lambda e, t, sc: (sc[5 * turn + 1], 0, 0))
    at_spot = lambda k, *shape: pl.BlockSpec(
        (1, *shape), lambda e, t, sc: (sc[5 * turn + 1 + k], 0, 0)
    )
    in_specs = [fixed(rows, width, pipeline_mode=pl.Buffered(1))] * (2 * pieces) + [
        at_spot(1, 2, rows),
        adapter(2 * rank, width),
        adapter(expert_count, rank),
        pl.BlockSpec((1, rank, tile), lambda e, t, sc: (sc[5 * turn + 1], 0, t)),
        fixed(expert_count, width),
        pl.BlockSpec((1, width, tile), lambda e, t, sc: (e + sc[5 * turn + 4], 0, t)),
        pl.BlockSpec((1, tile, width), lambda e, t, sc: (e + sc[5 * turn + 4], t, 0)),
        pl.BlockSpec(memory_space=pl.ANY),
    ]
    bf16, f32 = jnp.bfloat16, jnp.float32
    scratch = [
        ((rows, width), bf16),
        ((rows, width), bf16),
        ((capacity, width), bf16),
        ((capacity, width), bf16),
        ((capacity, width), bf16),
        ((capacity, rank), bf16),
        ((capacity, width), f32),
        ((capacity, width), f32),
        ((rank, capacity), f32),
        ((capacity, rows), bf16),
        ((rank, rows), bf16),
        ((expert_count, rows), f32),
        ((expert_count, rows), f32),
        ((rows, width), f32),
        ((rows, width), f32),
        ((rank + 8, rows), f32),
    ]
    return pl.pallas_call(
        functools.partial(expert_kernel, turn, pieces, capacity, rank),
        grid_spec=pltpu.PrefetchScalarGridSpec(
            num_scalar_prefetch=1,
            grid=(local, hidden // tile),
            in_specs=in_specs,
            out_specs=[
                fixed(rows, width),
                fixed(rows + rank + 16, width),
                at_spot(2, rank, hidden),
            ],
            scratch_shapes=[pltpu.VMEM(shape, kind) for shape, kind in scratch],
        ),
        out_shape=[
            jax.ShapeDtypeStruct((rows, width), bf16),
            jax.ShapeDtypeStruct((rows + rank + 16, width), bf16),
            jax.ShapeDtypeStruct(gff.shape, f32),
        ],
        input_output_aliases={1 + 2 * pieces + 7: 2},
        compiler_params=pltpu.CompilerParams(vmem_limit_bytes=58 * 1024 * 1024),
        cost_estimate=pl.CostEstimate(
            flops=8 * local * capacity * width * hidden,
            bytes_accessed=4 * local * width * hidden + 8 * rows * width,
            transcendentals=0,
        ),
        name="ex",
    )(
        scalars, *xs, *gs, route_rows, down_t, upr_t, up_ffn, router_t, w1, w2, gff
    )


CROSS = [(0, 1), (1, 0), (2, 3), (3, 2)]
INNER = [(1, 2), (2, 1)]
OUTWARD = [(1, 0), (2, 3)]
INWARD = [(0, 1), (3, 2)]
SKIP = [(1, 3), (2, 0)]
TWICE = [(0, 2), (2, 0), (1, 3), (3, 1)]
MIRROR = [(0, 3), (3, 0), (1, 2), (2, 1)]


def on_line(block, route):
    return lax.ppermute(block, EXPERT, route)


def exchange_all(block, axis):
    count = lax.axis_size(axis)
    return [block] + [
        lax.ppermute(block, axis, [(i, (i + step) % count) for i in range(count)])
        for step in range(1, count)
    ]


def shards_by_tokens(
    tokens,
    attention_norm_gain,
    expert_norm_gain,
    query_key_value_weight,
    attention_output_weight,
    router_weight,
    expert_input_weight,
    expert_output_weight,
    adapter_down_factors,
    adapter_up_attention,
    adapter_up_routing,
    adapter_up_expert,
    sequence_adapter,
    position_document,
    routes,
    output_gradient,
):
    rows, width = tokens.shape[1:]
    local = expert_input_weight.shape[0]
    groups = lax.axis_size(EXPERT)
    choices = local * groups
    capacity = 4 * rows // choices
    adapter_total, rank, hidden = adapter_up_expert.shape
    adapter = sequence_adapter[0]
    half = lax.axis_index(FSDP)
    place = lax.axis_index(EXPERT)
    at_end = (place == 0) | (place == groups - 1)
    bf16, f32 = jnp.bfloat16, jnp.float32
    swap = [(0, 1), (1, 0)]
    x, go = tokens[0], output_gradient[0]
    downs = jnp.swapaxes(adapter_down_factors, 2, 3)
    ups = adapter_up_attention
    down_t = jnp.swapaxes(downs[4:6], 0, 1).reshape(adapter_total, 2 * rank, width)
    upr_t = jnp.swapaxes(adapter_up_routing, 1, 2)
    router_t = router_weight.T
    scalars = jnp.stack([half, adapter]).astype(jnp.int32)

    weight_other = lax.ppermute(query_key_value_weight, FSDP, swap)
    left = lax.ppermute(x, FSDP, [(0, 1)])
    about = jnp.concatenate([routes[0].T, jnp.full((1, rows), adapter, jnp.int32)])
    about = [about, *(on_line(about, route) for route in (CROSS, TWICE, MIRROR))]
    go_across, go_inner = on_line(go, CROSS), on_line(go, INNER)
    normed, low_qkv, queries, keys_values = project_in(
        scalars, x, left, attention_norm_gain, query_key_value_weight, weight_other, downs, ups
    )
    out_other = lax.ppermute(attention_output_weight, FSDP, swap)
    doc_row = position_document[0]
    own_doc = lax.dynamic_slice_in_dim(doc_row, half * rows, rows)
    key_doc = jnp.concatenate([jnp.where(half > 0, doc_row[:rows], -1), own_doc])
    go_far_ends, go_far_inner = on_line(go_inner, OUTWARD), on_line(go_across, INNER)
    (att,) = attention_call(
        attend_kernel, queries, keys_values, [], key_doc, own_doc, [("block", bf16)], 0, 4
    )
    low_out, hidden_rows, normed_two = project_out(
        scalars, x, att, attention_output_weight, out_other, downs, ups, expert_norm_gain
    )

    about = jnp.stack(about)
    route_rows, adapters = about[:, :2], about[:, 2, 0]
    part = local // 2
    steps = jnp.arange(5, dtype=jnp.int32)
    distance = jnp.where(steps < 3, steps + 1, 0)
    distance = jnp.where((distance > 1) & ~at_end, 5 - distance, distance)
    hot = distance[:, None] == jnp.arange(groups, dtype=jnp.int32)[None]
    chosen = jnp.sum(jnp.where(hot, adapters[None], 0), axis=1)
    later = jnp.where(steps == 4, part, 0)
    block = jnp.where(steps == 4, groups, place ^ distance)
    turns = jnp.stack([place * local + later, chosen, distance, block, later], axis=1)
    turns = turns.reshape(-1).astype(jnp.int32)

    def call(turn, xs, gs, gff, count=local):
        return run_experts(
            turn,
            turns,
            count,
            xs,
            gs,
            route_rows,
            down_t,
            router_t,
            upr_t,
            adapter_up_expert,
            expert_input_weight,
            expert_output_weight,
            gff,
            capacity,
        )

    merge = lambda one, two: (one.astype(f32) + two.astype(f32)).astype(bf16)
    gff = jnp.zeros((groups + 1, rank, hidden), f32)
    across, inner = on_line(normed_two, CROSS), on_line(normed_two, INNER)
    y_e, dx_e, gff = call(3, [normed_two], [go], gff, part)
    go_last = on_line(go_far_inner, OUTWARD)
    far_ends, far_inner = on_line(inner, OUTWARD), on_line(across, INNER)
    y_b, dx_b, gff = call(0, [across], [go_across], gff)
    last = on_line(far_inner, OUTWARD)
    back_b = on_line(dx_b, CROSS)
    y_c, dx_c, gff = call(1, [inner, far_ends], [go_inner, go_far_ends], gff)
    part_c = on_line(dx_c, INWARD)
    y_part_c = on_line(y_c, INWARD)
    y_d, dx_d, gff = call(2, [far_inner, last], [go_far_inner, go_last], gff)
    part_d = on_line(dx_d, INWARD)
    back_c = on_line(merge(dx_c, part_c), INNER)
    y_part_d = on_line(y_d, INWARD)
    y_a, dx_a, gff = call(4, [normed_two], [go], gff, local - part)
    merged = merge(dx_d, part_d)
    back_d = on_line(merged, SKIP)
    gff, _ = lax.optimization_barrier((gff, merged))
    outs, _ = lax.optimization_barrier(((y_b, y_c, y_part_c), merged))
    y_b, y_c = on_line(outs[0], CROSS), on_line(merge(*outs[1:]), INNER)
    halves = gff.reshape(groups + 1, rank, 2, -1)
    halves = [lax.dynamic_index_in_dim(halves, at, 2, keepdims=False) for at in (half, 1 - half)]
    ffn_part = halves[0] + lax.ppermute(halves[1].astype(bf16), FSDP, swap).astype(f32)
    ffn_part = ffn_part.astype(bf16).reshape(groups + 1, rank, groups, -1)
    ffn_part = lax.all_to_all(
        jnp.moveaxis(ffn_part, 2, 0), EXPERT, split_axis=0, concat_axis=0, tiled=True
    )
    ffn_part = ffn_part.astype(f32)
    ffn_part = jnp.sum(ffn_part[:, :groups], axis=0) + ffn_part[:, groups]
    share, wide = width // (2 * groups), choices // (2 * groups)
    datt, dh, early = after_experts(
        scalars,
        [dx_a, dx_e, back_b, back_c, back_d],
        go,
        hidden_rows,
        normed_two,
        att,
        low_out,
        route_rows,
        down_t,
        router_t,
        upr_t,
        downs,
        ups,
        attention_output_weight,
        out_other,
        expert_norm_gain,
        share,
        wide,
    )
    outs, datt = lax.optimization_barrier(((y_d, y_part_d), datt))
    outs = [y_b, y_c, on_line(merge(*outs), SKIP)]
    dq, own, left_grads = attention_call(
        attend_back_kernel,
        queries,
        keys_values,
        [datt],
        key_doc,
        own_doc,
        [("block", bf16), ("pair", f32), ("pair", bf16)],
        1,
        10,
    )
    back = lax.ppermute(left_grads, FSDP, [(1, 0)])
    grads, glow, kept, given = factor_grads(
        scalars, dq, own, back, low_qkv, ups, normed, early
    )
    kept = (kept + lax.ppermute(given, FSDP, swap).astype(f32)).astype(bf16)
    lanes = 128
    parts = jnp.swapaxes(kept.reshape(12 * rank, groups, share), 0, 1)
    parts = jnp.pad(parts, ((0, 0), (0, 0), (0, lanes - share)))
    parts = lax.all_to_all(parts, EXPERT, split_axis=0, concat_axis=0, tiled=True)
    ffn_part = ffn_part.astype(bf16).reshape(groups, rank, -1, lanes)
    ffn_part = jnp.swapaxes(ffn_part, 1, 2).reshape(groups, -1, lanes)
    (grad_tokens,) = last_rows(
        scalars,
        grads,
        glow,
        query_key_value_weight,
        weight_other,
        downs,
        x,
        attention_norm_gain,
        dh,
    )
    parts = exchange_all(jnp.concatenate([parts, ffn_part], axis=1), DP)
    output = (hidden_rows + sum(part.astype(f32) for part in [y_a, y_e, *outs])).astype(bf16)
    downs_sum, ups_sum, router_sum, ffn_sum = adapter_sums(
        scalars, parts, adapter_total, rank, share, wide, hidden // (2 * groups)
    )
    return (
        output[None],
        grad_tokens[None],
        jnp.swapaxes(downs_sum, 2, 3),
        ups_sum,
        jnp.swapaxes(router_sum, 1, 2),
        ffn_sum,
    )


def solution(mesh):
    in_specs = (
        P((DP, EXPERT), FSDP, None),
        P(),
        P(),
        P(None, FSDP, None),
        P(FSDP, None),
        P(),
        P(EXPERT, None, None),
        P(EXPERT, None, None),
        P(),
        P(),
        P(),
        P(),
        P((DP, EXPERT)),
        P((DP, EXPERT), None),
        P((DP, EXPERT), FSDP, None),
        P((DP, EXPERT), FSDP, None),
    )
    out_specs = (
        P((DP, EXPERT), FSDP, None),
        P((DP, EXPERT), FSDP, None),
        P(None, None, (FSDP, EXPERT), None),
        P(None, None, None, (FSDP, EXPERT)),
        P(None, None, (FSDP, EXPERT)),
        P(None, None, (FSDP, EXPERT)),
    )
    specs = dict(mesh=mesh, in_specs=in_specs, out_specs=out_specs, check_vma=False)
    by_tokens = jax.shard_map(shards_by_tokens, **specs)
    by_slots = jax.shard_map(shards_by_slots, **specs)
    groups, shards = mesh.shape[EXPERT], mesh.shape[DP] * mesh.shape[EXPERT]

    def layer(*arguments):
        tokens, experts = arguments[0], arguments[6].shape[0]
        rows = tokens.shape[0] * tokens.shape[1] // (shards * mesh.shape[FSDP])
        wide = 4 * rows // experts * (experts // groups) >= rows and experts % (2 * groups) == 0
        if groups == 4 and mesh.shape[FSDP] == 2 and tokens.shape[0] == shards and wide:
            return by_tokens(*arguments)
        return by_slots(*arguments)

    return layer
```
